128 devices in a mesh: ctx: 16 (over y, x), exp: 8 (over z, core).
Axes of the slice: x: 4, y: 4, z: 4, core: 2. Of those that a mesh axis runs over, the one named last changes fastest.
Arguments:
- queries: bfloat16 [4, 1024, 8192], P(None, 'ctx', 'exp'), may hold values from -2 to 2
- keys: bfloat16 [4, 1024, 8192], P(None, 'ctx', 'exp'), may hold values from -2 to 2
- values: bfloat16 [4, 1024, 8192], P(None, 'ctx', 'exp'), may hold values from -6 to 6
- decay_log: float32 [1024, 64], P('ctx', 'exp'), may hold values from -0.9 to 0
- out_gate: bfloat16 [4, 1024, 8192], P(None, 'ctx', 'exp'), may hold values from -6 to 6
- head_gain: float32 [8192], P('exp'), may hold values from 0.1 to 1.9
- out_weight: bfloat16 [8192, 6144], P('exp', 'ctx'), may hold values from -0.0625 to 0.0625
- stream: bfloat16 [4, 1024, 6144], P(None, ('ctx', 'exp')), may hold values from -6 to 6
- norm_gain: float32 [6144], replicated, may hold values from 0.1 to 1.9
- expert_ids: int32 [128, 32, 2], P(('ctx', 'exp')), may hold values from 0 to 7, all different within a row; in each aligned block of 32 rows (0 to 31, 32 to 63, ..., all dimensions but the last counted through in order) at most 9 rows name the same one
- expert_share: float32 [128, 32, 2], P(('ctx', 'exp')), may hold values from 0.2 to 1
- w_gate: bfloat16 [8, 6144, 9216], P('exp', None, 'ctx'), may hold values from -0.078125 to 0.078125
- w_up: bfloat16 [8, 6144, 9216], P('exp', None, 'ctx'), may hold values from -0.078125 to 0.078125
- w_down: bfloat16 [8, 9216, 6144], P('exp', 'ctx'), may hold values from -0.0625 to 0.0625
Outputs:
- layer_out: bfloat16 [4, 1024, 6144], P(None, ('ctx', 'exp'))
The draws below stay inside these ranges and needn't reach their ends.
Inputs may be any that keep to these rules, and one draw needn't show every extreme that they name: `expert_ids`: within a routing group no expert takes more than 9 copies, some group gives one expert exactly 9, and the two picks of a token differ.
All inputs are finite; a program needn't handle non-finite values.
Results may differ from the reference program's by a relative error of at most 0.02.
Values may be sent and summed in bfloat16 or wider, within the bound.
A program may use at most 192 MiB of HBM per device.

```python
import math
import jax
import jax.numpy as jnp
import numpy as np
from jax import lax

D = 6144
HEAD_TOTAL = 64
HD = 128
HID = 9216
SEQS = 4
BLOCK = 64
SEQUENCE_LENGTH = 1024
SUB = 8
TOK_DEV = 32
GROUPS = 128
HID_DEV = 576
EXPERTS = 8
MOST = 9
N_CTX = 16


def draw_decay_log(key, part):
    every_key_row = jax.random.split(key, 6)
    fast_share = 0.5
    chooser = jax.random.uniform(every_key_row[0], (HEAD_TOTAL,))
    fast_rate = jnp.exp(jax.random.uniform(every_key_row[1], (HEAD_TOTAL,), minval=math.log(1.0 / 50.0), maxval=math.log(1.0 / 30.0)))
    slow_rate = jnp.exp(jax.random.uniform(every_key_row[2], (HEAD_TOTAL,), minval=math.log(0.05 / SEQUENCE_LENGTH), maxval=math.log(0.5 / SEQUENCE_LENGTH)))
    baseline_decay_rate = jnp.where(chooser < fast_share, fast_rate, slow_rate)
    jitter_amplitude = jnp.exp(jax.random.uniform(every_key_row[3], (SEQUENCE_LENGTH, HEAD_TOTAL), minval=math.log(0.5), maxval=math.log(2.0)))
    spike_positions = jax.random.randint(every_key_row[4], (3,), 0, SEQUENCE_LENGTH)
    spike_flags = jnp.any(jnp.arange(SEQUENCE_LENGTH)[:, None] == spike_positions[None, :], axis=1)
    spike_magnitude = jax.random.uniform(every_key_row[5], (SEQUENCE_LENGTH, HEAD_TOTAL), minval=math.log(0.5), maxval=math.log(0.8))
    decay_result = -baseline_decay_rate[None, :] * jitter_amplitude + jnp.where(spike_flags[:, None], spike_magnitude, 0.0)
    return decay_result.astype(jnp.float32)


def shard_levels(stream_key, dims, shards, least, top_value):
    def one(dim, blocks):
        draws = jax.random.uniform(jax.random.fold_in(jax.random.fold_in(stream_key, 6), dim), (blocks,), jnp.float32, least / len(shards), top_value / len(shards))
        return jnp.repeat(jnp.exp(draws), dims[dim] // blocks).reshape((-1,) + (1,) * (len(dims) - dim - 1))

    level = one(*shards[0])
    for cut in shards[1:]:
        level = level * one(*cut)
    return level


def routed_block(own_key, own, number, rows, amount, top, most, slope):
    order = jax.random.permutation(own_key, amount)
    crowded, usual = portions_of(amount, rows * top, most, slope, True), portions_of(amount, rows * top, most, slope, False)
    places = jnp.arange(amount)

    def named(tallies, offset_by):
        used = int((tallies > 0).sum())
        fixed = max(1, used // 4)
        passed = fixed + (places - fixed + offset_by * (used - fixed)) % max(1, amount - fixed)
        return jnp.zeros((amount,), jnp.int32).at[order[jnp.where(places < fixed, places, passed)]].set(jnp.asarray(tallies, jnp.int32))

    tallies = jnp.where(number % 4 == 0, named(crowded, number // 4), named(usual, number - number // 4 - 1))
    mixed = jax.random.permutation(jax.random.fold_in(own, 3), amount)
    donor, sink = mixed[0:amount // 2 * 2:2], mixed[1:amount // 2 * 2:2]
    slack = jnp.minimum(tallies[donor] - 1, most - tallies[sink]) // 2
    slack = jnp.where((donor == order[0]) | (sink == order[0]) | (tallies[sink] == 0), 0, jnp.maximum(slack, 0))
    passed = jax.random.randint(jax.random.fold_in(own, 4), (amount // 2,), 0, 1 << 20) % (slack + 1)
    tallies = tallies.at[donor].add(-passed).at[sink].add(passed)
    members = jnp.searchsorted(jnp.cumsum(tallies), jnp.arange(rows * top), side="right").astype(jnp.int32)
    listing = members.reshape(top, rows).T
    listing = listing[jax.random.permutation(jax.random.fold_in(own, 1), rows)]
    offset_by = jax.random.randint(jax.random.fold_in(own, 2), (rows, 1), 0, top)
    return jnp.take_along_axis(listing, (jnp.arange(top)[None, :] + offset_by) % top, axis=1)


def portions_of(amount, total, bound, slope, full):
    loads = [(1 << 20) // math.isqrt(grade ** slope) + 1 for grade in range(1, amount + 1)]
    largest = bound if full else min(bound, max(-(-total // amount), total * loads[0] // sum(loads)))
    least = 1 if total - largest >= amount - 1 else 0
    given, surplus = [largest] + [least] * (amount - 1), total - largest - least * (amount - 1)
    while surplus > 0:
        movable = [i for i in range(1, amount) if given[i] < largest] or [i for i in range(1, amount) if given[i] < bound]
        pool, budget = sum([loads[i] for i in movable]), surplus
        for i in movable:
            extra = min(bound - given[i], max(1, budget * loads[i] // pool), surplus)
            given[i] = given[i] + extra
            surplus = surplus - extra
    return np.array(given)


def gaussian(rng, extent, deviation, limit, cuts=(), kind=jnp.bfloat16):
    entries = deviation * jax.random.normal(rng, extent, jnp.float32)
    if cuts:
        entries = entries * shard_levels(rng, extent, cuts, -0.22, 0.18)
    return jnp.clip(entries, -limit, limit).astype(kind)


def setup_inputs(seed: int = 0) -> dict:
    splits = jax.random.split(jax.random.key(seed), 15)
    queries = gaussian(splits[0], (SEQS, SEQUENCE_LENGTH, HEAD_TOTAL * HD), 0.35, 2.0, ((1, 16), (2, 8)))
    keys = gaussian(splits[1], (SEQS, SEQUENCE_LENGTH, HEAD_TOTAL * HD), 0.35, 2.0, ((1, 16), (2, 8)))
    values = gaussian(splits[2], (SEQS, SEQUENCE_LENGTH, HEAD_TOTAL * HD), 1.0, 6.0, ((1, 16), (2, 8)))
    decay_log = draw_decay_log(jax.random.fold_in(splits[14], 71), 0)
    out_gate = gaussian(splits[4], (SEQS, SEQUENCE_LENGTH, HEAD_TOTAL * HD), 1.0, 6.0, ((1, 16), (2, 8)))
    head_gain = jnp.clip(1.0 + 0.18 * jax.random.normal(splits[5], (HEAD_TOTAL * HD,), jnp.float32), 0.1, 1.9)
    out_weight = gaussian(splits[6], (HEAD_TOTAL * HD, D), (HEAD_TOTAL * HD) ** -0.5, 0.0625, ((0, 8), (1, 16)))
    stream = gaussian(splits[7], (SEQS, SEQUENCE_LENGTH, D), 1.0, 6.0, ((1, 128),))
    norm_gain = jnp.clip(1.0 + 0.18 * jax.random.normal(splits[8], (D,), jnp.float32), 0.1, 1.9)
    expert_ids_keys = jax.random.split(jax.random.fold_in(splits[9], 1), GROUPS * TOK_DEV // TOK_DEV)
    expert_ids_turns = jax.random.permutation(jax.random.fold_in(splits[9], 3), GROUPS * TOK_DEV // TOK_DEV)
    expert_ids = jax.vmap(lambda own, number: routed_block(jax.random.fold_in(splits[9], 2), own, number, TOK_DEV, EXPERTS, 2, MOST, 2))(expert_ids_keys, expert_ids_turns).reshape((GROUPS, TOK_DEV, 2))
    expert_share = jnp.clip(0.2 + 0.8 * jax.random.uniform(splits[10], (GROUPS, TOK_DEV, 2), jnp.float32) ** shard_levels(splits[10], (GROUPS, TOK_DEV, 2), ((0, 128),), -0.2, 0.2), 0.2, 1.0)
    w_gate = gaussian(splits[11], (EXPERTS, D, HID), D ** -0.5, 0.078125, ((0, 8), (2, 16)))
    w_up = gaussian(splits[12], (EXPERTS, D, HID), D ** -0.5, 0.078125, ((0, 8), (2, 16)))
    w_down = gaussian(splits[13], (EXPERTS, HID, D), HID ** -0.5, 0.0625, ((0, 8), (1, 16)))
    return dict(queries=queries, keys=keys, values=values, decay_log=decay_log, out_gate=out_gate, head_gain=head_gain, out_weight=out_weight, stream=stream, norm_gain=norm_gain, expert_ids=expert_ids, expert_share=expert_share, w_gate=w_gate, w_up=w_up, w_down=w_down)


def reference(queries, keys, values, decay_log, out_gate, head_gain, out_weight, stream, norm_gain, expert_ids, expert_share, w_gate, w_up, w_down):
    split_shape = (SEQS, N_CTX, BLOCK, HEAD_TOTAL, HD)
    query_all = queries.astype(jnp.float32).reshape(split_shape)
    key_all = keys.astype(jnp.float32).reshape(split_shape)
    value_all = values.astype(jnp.float32).reshape(split_shape)
    cumulative = jnp.cumsum(decay_log.reshape(N_CTX, BLOCK, HEAD_TOTAL), axis=1)
    position = jnp.arange(BLOCK)
    causal = position[:, None] >= position[None, :]
    gap_log = cumulative[:, :, None, :] - cumulative[:, None, :, :]
    decay_grid = jnp.exp(jnp.where(causal[None, :, :, None], gap_log, -1e+30))
    scores = jnp.einsum('sbihd,sbjhd->sbijh', query_all, key_all)
    weights = (scores * decay_grid[None]).astype(jnp.bfloat16)
    within = jnp.einsum('sbijh,sbjhd->sbihd', weights.astype(jnp.float32), value_all)
    block_end = cumulative[:, -1, :]
    keys_faded = jnp.exp(block_end[:, None, :] - cumulative)[None, :, :, :, None] * key_all
    local_state = jnp.einsum('sbjhd,sbjhe->sbhde', keys_faded, value_all, precision=lax.Precision.HIGHEST)
    fading = jnp.exp(block_end)

    def advance(state_in, inputs):
        fade_now, local_now = inputs
        return (fade_now[None, :, None, None] * state_in + local_now, state_in)
    start_state = jnp.zeros((SEQS, HEAD_TOTAL, HD, HD), jnp.float32)
    _, incoming = lax.scan(advance, start_state, (fading, jnp.moveaxis(local_state, 1, 0)))
    incoming = jnp.moveaxis(incoming, 0, 1)
    carried = jnp.exp(cumulative)[None, :, :, :, None] * jnp.einsum('sbihd,sbhde->sbihe', query_all, incoming, precision=lax.Precision.HIGHEST)
    attended = within + carried
    mean_square = lax.optimization_barrier(jnp.mean(attended * attended, axis=-1, keepdims=True))
    gate_act = jax.nn.sigmoid(out_gate.astype(jnp.float32).reshape(split_shape))
    gated = attended * lax.rsqrt(mean_square + 1e-06) * head_gain.reshape(HEAD_TOTAL, HD) * gate_act
    mixed = gated.astype(jnp.bfloat16).reshape(SEQS * SEQUENCE_LENGTH, HEAD_TOTAL * HD)
    residual_sum = stream.astype(jnp.float32).reshape(SEQS * SEQUENCE_LENGTH, D) + jnp.dot(mixed, out_weight, preferred_element_type=jnp.float32)
    stream_square = lax.optimization_barrier(jnp.mean(residual_sum * residual_sum, axis=-1, keepdims=True))
    normed = (residual_sum * lax.rsqrt(stream_square + 1e-06) * norm_gain).astype(jnp.bfloat16)
    token_groups = normed.reshape(SEQS, GROUPS, SUB, D).transpose(1, 0, 2, 3).reshape(GROUPS, TOK_DEV, D)
    residual_groups = residual_sum.reshape(SEQS, GROUPS, SUB, D).transpose(1, 0, 2, 3).reshape(GROUPS, TOK_DEV, D)
    picks = expert_ids.reshape(GROUPS, 2 * TOK_DEV)
    one_hot = (picks[:, :, None] == jnp.arange(EXPERTS, dtype=jnp.int32)[None, None, :]).astype(jnp.int32)
    ranking = lax.optimization_barrier(jnp.sum(jnp.cumsum(one_hot, axis=1) * one_hot, axis=2)) - 1
    slot_of = (picks * MOST + ranking).astype(jnp.int32)
    copies = jnp.repeat(token_groups, 2, axis=1)

    def place_group(slot_row, copy_rows):
        return jnp.zeros((EXPERTS * MOST, D), jnp.bfloat16).at[slot_row].set(copy_rows)
    dispatch = jax.vmap(place_group)(slot_of, copies)
    per_expert = dispatch.reshape(GROUPS, EXPERTS, MOST, D).transpose(1, 0, 2, 3).reshape(EXPERTS, GROUPS * MOST, D)

    def run_expert(inputs):
        slot_rows, gate_part, up_part, down_part = inputs
        summed = jnp.zeros((GROUPS * MOST, D), jnp.float32)
        for group_no in range(N_CTX):
            lower_edge = group_no * HID_DEV
            gate_val = jnp.dot(slot_rows, gate_part[:, lower_edge:lower_edge + HID_DEV], preferred_element_type=jnp.float32)
            up_val = jnp.dot(slot_rows, up_part[:, lower_edge:lower_edge + HID_DEV], preferred_element_type=jnp.float32)
            hidden = (jax.nn.silu(gate_val) * up_val).astype(jnp.bfloat16)
            partial_value = jnp.dot(hidden, down_part[lower_edge:lower_edge + HID_DEV], preferred_element_type=jnp.float32).astype(jnp.bfloat16)
            summed = summed + partial_value.astype(jnp.float32)
        return summed.astype(jnp.bfloat16)
    expert_out = lax.map(run_expert, (per_expert, w_gate, w_up, w_down))
    returned = expert_out.reshape(EXPERTS, GROUPS, MOST, D).transpose(1, 0, 2, 3).reshape(GROUPS, EXPERTS * MOST, D)
    picked = jnp.take_along_axis(returned, slot_of[:, :, None], axis=1).astype(jnp.float32)
    shares = expert_share.reshape(GROUPS, 2 * TOK_DEV, 1)
    expert_mix = lax.optimization_barrier(jnp.sum((picked * shares).reshape(GROUPS, TOK_DEV, 2, D), axis=2))
    result = (residual_groups + expert_mix).astype(jnp.bfloat16)
    return result.reshape(GROUPS, SEQS, SUB, D).transpose(1, 0, 2, 3).reshape(SEQS, SEQUENCE_LENGTH, D)
```

```python
import jax
import jax.numpy as jnp
from jax import lax
from jax.sharding import Mesh, PartitionSpec as P

CTX = ("y", "x")
EXP = ("z", "c")


def incoming_states(local_state, block_end):
    pairs = local_state.shape[0] * local_state.shape[1]
    head_count = local_state.shape[1]
    n = lax.axis_size(CTX)
    per = pairs // n
    width = local_state.shape[-1]
    chunks = local_state.reshape(n, per, width, width).astype(jnp.bfloat16)
    got = lax.all_to_all(chunks, CTX, split_axis=0, concat_axis=0, tiled=True)
    ends = lax.all_gather(block_end, CTX)
    me = lax.axis_index(CTX)
    first = lax.rem(me * per, head_count)
    fade = jnp.exp(lax.dynamic_slice_in_dim(ends, first, per, 1))[:, :, None, None]
    state = jnp.zeros(got.shape[1:], jnp.float32)
    out = []
    for b in range(n):
        out.append(state.astype(jnp.bfloat16))
        state = fade[b] * state + got[b].astype(jnp.float32)
    back = lax.all_to_all(jnp.stack(out), CTX, split_axis=0, concat_axis=0, tiled=True)
    return back.reshape(local_state.shape)


def body(
    queries,
    keys,
    values,
    decay_log,
    out_gate,
    head_gain,
    out_weight,
    stream,
    norm_gain,
    expert_ids,
    expert_share,
    w_gate,
    w_up,
    w_down,
):
    seq_count, block_len, head_width = queries.shape
    head_count = decay_log.shape[1]
    head_dim = head_width // head_count
    split_shape = (seq_count, block_len, head_count, head_dim)
    query_heads = queries.reshape(split_shape)
    key_heads = keys.reshape(split_shape)
    value_heads = values.reshape(split_shape)
    position = jnp.arange(block_len)
    causal = position[:, None] >= position[None, :]
    cumulative = jnp.sum(jnp.where(causal[:, :, None], decay_log[None], 0.0), axis=1)
    gap_log = cumulative[:, None, :] - cumulative[None, :, :]
    decay_grid = jnp.exp(jnp.where(causal[:, :, None], gap_log, -1e30))
    block_end = cumulative[-1]
    keys_faded = jnp.exp(block_end[None, :] - cumulative)[None, :, :, None] * key_heads.astype(
        jnp.float32
    )
    local_state = jnp.einsum(
        "sjhd,sjhe->shde",
        keys_faded,
        value_heads.astype(jnp.float32),
        precision=lax.Precision.HIGHEST,
    )
    incoming = incoming_states(local_state, block_end)
    row_weight = lax.all_gather(out_weight, "y", axis=1, tiled=True)
    scores = jnp.einsum(
        "sihd,sjhd->sijh", query_heads, key_heads, preferred_element_type=jnp.float32
    )
    weights = (scores * decay_grid[None]).astype(jnp.bfloat16)
    within = jnp.einsum("sijh,sjhd->sihd", weights, value_heads, preferred_element_type=jnp.float32)
    carried = jnp.exp(cumulative)[None, :, :, None] * jnp.einsum(
        "sihd,shde->sihe", query_heads, incoming, preferred_element_type=jnp.float32
    )
    attended = within + carried
    mean_square = jnp.mean(attended * attended, axis=-1, keepdims=True)
    gate_act = jax.nn.sigmoid(out_gate.reshape(split_shape).astype(jnp.float32))
    gated = (
        attended
        * lax.rsqrt(mean_square + 1e-06)
        * head_gain.reshape(head_count, head_dim)
        * gate_act
    )
    mixed = gated.astype(jnp.bfloat16).reshape(seq_count, block_len, head_width)
    sub_len = stream.shape[1]
    model_width = stream.shape[2]
    exp_count = lax.axis_size(EXP)
    x_count = lax.axis_size("x")
    y_count = lax.axis_size("y")
    ctx_count = x_count * y_count
    tok_count = seq_count * sub_len
    ordered = (
        mixed.reshape(seq_count, exp_count, sub_len, head_width)
        .transpose(1, 0, 2, 3)
        .reshape(exp_count, tok_count, head_width)
    )
    row_tokens = lax.all_gather(ordered, "x", axis=1, tiled=True)
    part_width = row_weight.shape[1]
    product = jnp.dot(
        row_tokens.reshape(exp_count * x_count * tok_count, head_width),
        row_weight,
        preferred_element_type=jnp.float32,
    ).astype(jnp.bfloat16)
    column_part = lax.psum_scatter(product, EXP, scatter_dimension=0, tiled=True)
    projected = lax.all_to_all(
        column_part.reshape(x_count, tok_count, part_width), "x", split_axis=0, concat_axis=0, tiled=True
    )
    projected = (
        projected.reshape(x_count, tok_count, y_count, part_width // y_count)
        .transpose(1, 2, 0, 3)
        .reshape(tok_count, model_width)
        .astype(jnp.float32)
    )
    residual_sum = stream.reshape(tok_count, model_width).astype(jnp.float32) + projected
    stream_square = jnp.mean(residual_sum * residual_sum, axis=-1, keepdims=True)
    normed = (residual_sum * lax.rsqrt(stream_square + 1e-06) * norm_gain).astype(jnp.bfloat16)
    expert_count = exp_count
    capacity = max(2, (2 * tok_count + expert_count - 1) // expert_count + 1)
    slot_total = expert_count * capacity
    picks = expert_ids.reshape(2 * tok_count)
    copy_no = jnp.arange(2 * tok_count)
    earlier = (copy_no[None, :] < copy_no[:, None]) & (picks[None, :] == picks[:, None])
    ranking = jnp.sum(earlier.astype(jnp.int32), axis=1)
    slot_of = picks * capacity + ranking
    placing = slot_of[:, None] == jnp.arange(slot_total, dtype=jnp.int32)[None, :]
    token_placing = jnp.any(placing.reshape(tok_count, 2, slot_total), axis=1)
    dispatch = jnp.dot(
        token_placing.T.astype(jnp.bfloat16), normed, preferred_element_type=jnp.float32
    ).astype(jnp.bfloat16)
    dispatch = dispatch.reshape(exp_count, capacity, model_width)
    received = lax.all_to_all(dispatch, EXP, split_axis=0, concat_axis=0, tiled=True)
    piece = lax.all_gather(
        received.reshape(slot_total, model_width), CTX, axis=0, tiled=True
    )
    gate_part = jnp.dot(piece, w_gate[0], preferred_element_type=jnp.float32)
    up_part = jnp.dot(piece, w_up[0], preferred_element_type=jnp.float32)
    hidden_units = (jax.nn.silu(gate_part) * up_part).astype(jnp.bfloat16)
    terms = jnp.dot(hidden_units, w_down[0], preferred_element_type=jnp.float32).astype(
        jnp.bfloat16
    )
    summed = lax.psum_scatter(terms, CTX, scatter_dimension=0, tiled=True)
    returned = lax.all_to_all(
        summed.reshape(exp_count, capacity, model_width), EXP, split_axis=0, concat_axis=0, tiled=True
    ).reshape(slot_total, model_width)
    weighting = jnp.where(placing, expert_share.reshape(2 * tok_count, 1), 0.0)
    weighting = jnp.sum(weighting.reshape(tok_count, 2, slot_total), axis=1)
    expert_mix = jnp.dot(weighting, returned.astype(jnp.float32), precision=lax.Precision.HIGHEST)
    result = (residual_sum + expert_mix).astype(jnp.bfloat16)
    return result.reshape(seq_count, sub_len, model_width)


def solution(mesh):
    n_exp = mesh.shape["exp"]
    side = round(mesh.shape["ctx"] ** 0.5)
    fine = Mesh(mesh.devices.reshape(side, side, n_exp // 2, 2), ("y", "x", "z", "c"))
    return jax.shard_map(
        body,
        mesh=fine,
        in_specs=(
            P(None, CTX, EXP),
            P(None, CTX, EXP),
            P(None, CTX, EXP),
            P(CTX, EXP),
            P(None, CTX, EXP),
            P(EXP),
            P(EXP, CTX),
            P(None, CTX + EXP, None),
            P(),
            P(CTX + EXP, None, None),
            P(CTX + EXP, None, None),
            P(EXP, None, CTX),
            P(EXP, None, CTX),
            P(EXP, CTX, None),
        ),
        out_specs=P(None, CTX + EXP, None),
        check_vma=False,
    )
```

```python
import jax
import jax.numpy as jnp
from jax import lax
from jax.experimental import pallas as pl
from jax.experimental.pallas import tpu as pltpu
from jax.sharding import Mesh, PartitionSpec as P

CTX = ("y", "x")
EXP = ("z", "c")


MESH = pl.DeviceIdType.MESH
AXES = (("x", "y"), ("y", "x"))


def greet(pairs):
    barrier = pltpu.get_barrier_semaphore()
    for axis, to in pairs:
        pl.semaphore_signal(barrier, inc=1, device_id={axis: to}, device_id_type=MESH)
    pl.semaphore_wait(barrier, len(pairs))


def gather_kernel(
    rows_ref, wg_hbm, wu_hbm, hid_a, hid_b, buf_a, buf_b, wg, wu, xin, acc_g, acc_u, ssem, rsem, lsem
):
    n = 4
    count, width = rows_ref.shape
    half = width // 2
    quarter = half // 2
    hidden = wg.shape[0]
    buf = (buf_a, buf_b)
    place = {a: lax.axis_index(a) for a in ("x", "y")}

    def step(axis, by):
        return lax.rem(place[axis] + (by + n), n)

    load_g = pltpu.make_async_copy(wg_hbm, wg, lsem.at[0])
    load_u = pltpu.make_async_copy(wu_hbm, wu, lsem.at[1])
    load_g.start()
    load_u.start()
    greet([(a, step(a, d)) for a in ("x", "y") for d in (1, -1)])

    def row(h, fi, si):
        return buf[h].at[fi, pl.ds(pl.multiple_of(si * count, 8), count)]

    def cut(ref, k):
        return ref.at[:, pl.ds((k - 2) * quarter, quarter)] if k >= 2 else ref

    def send(h, stage, kind, axis, src, dst):
        to = step(axis, 1 if kind % 2 == 0 else -1)
        c = pltpu.make_async_remote_copy(
            src_ref=cut(src, kind),
            dst_ref=cut(dst, kind),
            send_sem=ssem.at[h, stage, kind],
            recv_sem=rsem.at[h, stage, kind],
            device_id={axis: to},
            device_id_type=MESH,
        )
        c.start()
        sent.append(c)

    def arrived(h, stage, kind, axis, dst):
        pltpu.make_async_remote_copy(
            src_ref=cut(dst, kind),
            dst_ref=cut(dst, kind),
            send_sem=ssem.at[h, stage, kind],
            recv_sem=rsem.at[h, stage, kind],
            device_id={axis: step(axis, 1)},
            device_id_type=MESH,
        ).wait_recv()

    sent = []
    shift = (0, -1, 1, 2)
    own = [rows_ref.at[:, pl.ds(h * half, half)] for h in range(2)]
    keep = []
    for h in range(2):
        first, second = AXES[h]
        mine = row(h, place[first], place[second])
        for kind in range(2):
            send(h, n, kind, first, own[h], mine)
    for h in range(2):
        first, second = AXES[h]
        mine = row(h, place[first], place[second])
        for kind in range(2):
            send(h, 0, kind, second, own[h], mine)
        keep.append(pltpu.make_async_copy(own[h], mine, lsem.at[2 + h]))
        keep[h].start()
    acc_g[...] = jnp.zeros_like(acc_g)
    acc_u[...] = jnp.zeros_like(acc_u)

    def spread(h, j):
        first, second = AXES[h]
        here = row(h, step(first, shift[j]), place[second])
        for kind in range(2):
            send(h, j, kind, second, here, here)

    def pass_on(h, stage, kind):
        first, second = AXES[h]
        by = -1 if kind == 0 else 1
        if stage == n:
            here = row(h, step(first, by), place[second])
            axis = first
        else:
            here = row(h, step(first, shift[stage]), step(second, by))
            axis = second
        arrived(h, stage, kind, axis, here)
        send(h, stage, kind + 2, axis, here, here)

    def far(h, stage):
        first, second = AXES[h]
        if stage == n:
            here, axis = row(h, step(first, 2), place[second]), first
        else:
            here, axis = row(h, step(first, shift[stage]), step(second, 2)), second
        for kind in (2, 3):
            arrived(h, stage, kind, axis, here)

    def load(h, j):
        return pltpu.make_async_copy(
            buf[h].at[step(AXES[h][0], shift[j])], xin.at[h], lsem.at[4 + h]
        )

    def multiply(h, j):
        load(h, j).wait()
        fi = step(AXES[h][0], shift[j])
        for w, acc in ((wg, acc_g), (wu, acc_u)):
            got = lax.dot_general(
                xin[h],
                w[:, pl.ds(h * half, half)],
                (((1,), (1,)), ((), ())),
                preferred_element_type=jnp.float32,
            ).reshape(n, count, hidden)
            if h == 0:
                acc[fi] += got
            else:
                acc[:, fi] += got

    for kind in range(2):
        for h in range(2):
            pass_on(h, n, kind)
            spread(h, 1 + kind)
    for kind in range(2):
        for h in range(2):
            pass_on(h, 0, kind)
    for h in range(2):
        far(h, n)
        spread(h, 3)
    load_g.wait()
    load_u.wait()
    for j in range(n):
        if j + 1 < n:
            for kind in range(2):
                for h in range(2):
                    pass_on(h, j + 1, kind)
        for h in range(2):
            if j == 0:
                keep[h].wait()
            far(h, j)
            load(h, j).start()
        for h in range(2):
            multiply(h, j)

    @pl.loop(0, n)
    def _(p):
        g = acc_g[p].reshape(n * count, hidden)
        u = acc_u[p].reshape(n * count, hidden)
        out = (g / (1.0 + jnp.exp(-g)) * u).astype(jnp.bfloat16)
        hid_a[pl.ds(pl.multiple_of(p * (n * count), 16), n * count), :] = out
        acc_g[p] = out.astype(jnp.float32).reshape(n, count, hidden)

    @pl.loop(0, n)
    def _(q):
        back = acc_g[:, pl.ds(q, 1)].reshape(n * count, hidden)
        hid_b[pl.ds(pl.multiple_of(q * (n * count), 16), n * count), :] = back.astype(jnp.bfloat16)

    for c in sent:
        c.wait_send()


def reduce_kernel(
    hid_a, hid_b, wd_hbm, out_ref, wd, t_a, t_b, r_opp, r_full, part, r_opp2, r_full2, ssem, rsem, lsem
):
    n = 4
    count, width = out_ref.shape
    half = width // 2
    quarter = half // 2
    block = min(512, quarter)
    hid = (hid_a, hid_b)
    t = (t_a, t_b)
    place = {a: lax.axis_index(a) for a in ("x", "y")}

    def step(axis, by):
        return lax.rem(place[axis] + (by + n), n)

    load = pltpu.make_async_copy(wd_hbm, wd, lsem.at[0])
    load.start()
    greet([(a, step(a, d)) for a in ("x", "y") for d in (1, -1)])
    load.wait()
    shift = (2, 1, -1, 0)
    sent = []

    def copy(h, stage, kind, axis, src, dst):
        return pltpu.make_async_remote_copy(
            src_ref=src,
            dst_ref=dst,
            send_sem=ssem.at[h, stage, kind],
            recv_sem=rsem.at[h, stage, kind],
            device_id={axis: step(axis, 1 if kind % 2 == 0 else -1)},
            device_id_type=MESH,
        )

    def send(*a):
        c = copy(*a)
        c.start()
        sent.append(c)

    def arrived(h, stage, kind, axis, dst):
        copy(h, stage, kind, axis, dst, dst).wait_recv()

    def multiply(h, j):
        lead = step(AXES[h][0], shift[j])
        x = hid[h].at[pl.ds(pl.multiple_of(lead * (n * count), 16), n * count), :]

        @pl.loop(0, half // block)
        def _(b):
            at = pl.multiple_of(b * block, 128)
            got = jnp.dot(
                x[...],
                wd[:, pl.ds(pl.multiple_of(h * half + at, 128), block)],
                preferred_element_type=jnp.float32,
            )
            t[h][j, :, :, pl.ds(at, block)] = got.reshape(n, count, block).astype(jnp.bfloat16)

        ring = AXES[h][1]
        for k in range(2):
            send(
                h,
                j,
                k,
                ring,
                t[h].at[j, step(ring, 2), :, pl.ds(k * quarter, quarter)],
                r_opp.at[h, j, k],
            )

    def add_to(ref, k, other):
        @pl.loop(0, quarter // block)
        def _(b):
            at = pl.multiple_of(b * block, 128)
            cols = pl.ds(pl.multiple_of(k * quarter + at, 128), block)
            ref[:, cols] = (
                ref[:, cols].astype(jnp.float32) + other[:, pl.ds(at, block)].astype(jnp.float32)
            ).astype(jnp.bfloat16)

    def total(dst, start, refs):
        @pl.loop(0, half // block)
        def _(b):
            at = pl.multiple_of(b * block, 128)
            s = refs[0][:, pl.ds(at, block)].astype(jnp.float32)
            for r in refs[1:]:
                s = s + r[:, pl.ds(at, block)].astype(jnp.float32)
            dst[:, pl.ds(pl.multiple_of(start + at, 128), block)] = s.astype(jnp.bfloat16)

    def near(h, j):
        ring = AXES[h][1]
        for k in range(2):
            arrived(h, j, k, ring, r_opp.at[h, j, k])
            mine = t[h].at[j, step(ring, 1 if k == 0 else -1)]
            add_to(mine, k, r_opp.at[h, j, k])
            send(h, j, 2 + k, ring, mine, r_full.at[h, j, k])

    def both(h, j):
        for k in range(2):
            arrived(h, j, 2 + k, AXES[h][1], r_full.at[h, j, k])

    def finish(h, j):
        both(h, j)
        total(
            part.at[h, j],
            0,
            [t[h].at[j, place[AXES[h][1]]], r_full.at[h, j, 0], r_full.at[h, j, 1]],
        )

    for j in range(2):
        for h in range(2):
            multiply(h, j)
    for j in range(n):
        for h in range(2):
            near(h, j)
        if j + 2 < n:
            for h in range(2):
                multiply(h, j + 2)
        if j == 1:
            for h in range(2):
                finish(h, 0)
                for k in range(2):
                    send(
                        h,
                        n,
                        k,
                        AXES[h][0],
                        part.at[h, 0, :, pl.ds(k * quarter, quarter)],
                        r_opp2.at[h, k],
                    )
    for j in (1, 2):
        for h in range(2):
            finish(h, j)
            k = j - 1
            arrived(h, n, k, AXES[h][0], r_opp2.at[h, k])
            add_to(part.at[h, j], k, r_opp2.at[h, k])
            send(h, n, 2 + k, AXES[h][0], part.at[h, j], r_full2.at[h, k])
    for h in range(2):
        both(h, 3)
        for k in range(2):
            arrived(h, n, 2 + k, AXES[h][0], r_full2.at[h, k])
        total(
            out_ref,
            h * half,
            [
                t[h].at[3, place[AXES[h][1]]],
                r_full.at[h, 3, 0],
                r_full.at[h, 3, 1],
                r_full2.at[h, 0],
                r_full2.at[h, 1],
            ],
        )
    for c in sent:
        c.wait_send()


def expert_terms(rows, w_gate, w_up):
    n = 4
    count, width = rows.shape
    hidden = w_gate.shape[0]
    half = width // 2
    any_spec = pl.BlockSpec(memory_space=pl.ANY)
    vmem = pl.BlockSpec(memory_space=pltpu.VMEM)
    bf16 = jnp.bfloat16
    return pl.pallas_call(
        gather_kernel,
        out_shape=[
            jax.ShapeDtypeStruct((n * n * count, hidden), bf16),
            jax.ShapeDtypeStruct((n * n * count, hidden), bf16),
            jax.ShapeDtypeStruct((n, n * count, half), bf16),
            jax.ShapeDtypeStruct((n, n * count, half), bf16),
        ],
        in_specs=[any_spec] * 3,
        out_specs=[vmem, vmem, any_spec, any_spec],
        scratch_shapes=[
            pltpu.VMEM((hidden, width), bf16),
            pltpu.VMEM((hidden, width), bf16),
            pltpu.VMEM((2, n * count, half), bf16),
            pltpu.VMEM((n, n, count, hidden), jnp.float32),
            pltpu.VMEM((n, n, count, hidden), jnp.float32),
            pltpu.SemaphoreType.DMA((2, n + 1, 4)),
            pltpu.SemaphoreType.DMA((2, n + 1, 4)),
            pltpu.SemaphoreType.DMA((6,)),
        ],
        compiler_params=pltpu.CompilerParams(
            collective_id=1, has_side_effects=True, vmem_limit_bytes=60 << 20
        ),
        name="gather_experts",
    )(rows, w_gate, w_up)[:2]


def expert_sum(hid_a, hid_b, w_down):
    n = 4
    hidden, width = w_down.shape
    count = hid_a.shape[0] // (n * n)
    half = width // 2
    any_spec = pl.BlockSpec(memory_space=pl.ANY)
    vmem = pl.BlockSpec(memory_space=pltpu.VMEM)
    bf16 = jnp.bfloat16
    return pl.pallas_call(
        reduce_kernel,
        out_shape=jax.ShapeDtypeStruct((count, width), bf16),
        in_specs=[vmem, vmem, any_spec],
        out_specs=vmem,
        scratch_shapes=[
            pltpu.VMEM((hidden, width), bf16),
            pltpu.VMEM((n, n, count, half), bf16),
            pltpu.VMEM((n, n, count, half), bf16),
            pltpu.VMEM((2, n, 2, count, half // 2), bf16),
            pltpu.VMEM((2, n, 2, count, half), bf16),
            pltpu.VMEM((2, 3, count, half), bf16),
            pltpu.VMEM((2, 2, count, half // 2), bf16),
            pltpu.VMEM((2, 2, count, half), bf16),
            pltpu.SemaphoreType.DMA((2, n + 1, 4)),
            pltpu.SemaphoreType.DMA((2, n + 1, 4)),
            pltpu.SemaphoreType.DMA((1,)),
        ],
        compiler_params=pltpu.CompilerParams(
            collective_id=2, has_side_effects=True, vmem_limit_bytes=60 << 20
        ),
        name="sum_experts",
    )(hid_a, hid_b, w_down)


def incoming_states(local_state, block_end):
    pairs = local_state.shape[0] * local_state.shape[1]
    head_count = local_state.shape[1]
    n = lax.axis_size(CTX)
    per = pairs // n
    width = local_state.shape[-1]
    chunks = local_state.reshape(n, per, width, width).astype(jnp.bfloat16)
    got = lax.all_to_all(chunks, CTX, split_axis=0, concat_axis=0, tiled=True)
    ends = lax.all_gather(block_end, CTX)
    me = lax.axis_index(CTX)
    first = lax.rem(me * per, head_count)
    fade = jnp.exp(lax.dynamic_slice_in_dim(ends, first, per, 1))[:, :, None, None]
    state = jnp.zeros(got.shape[1:], jnp.float32)
    out = []
    for b in range(n):
        out.append(state.astype(jnp.bfloat16))
        state = fade[b] * state + got[b].astype(jnp.float32)
    back = lax.all_to_all(jnp.stack(out), CTX, split_axis=0, concat_axis=0, tiled=True)
    return back.reshape(local_state.shape)


def body(
    queries,
    keys,
    values,
    decay_log,
    out_gate,
    head_gain,
    out_weight,
    stream,
    norm_gain,
    expert_ids,
    expert_share,
    w_gate,
    w_up,
    w_down,
):
    seq_count, block_len, head_width = queries.shape
    head_count = decay_log.shape[1]
    head_dim = head_width // head_count
    split_shape = (seq_count, block_len, head_count, head_dim)
    query_heads = queries.reshape(split_shape)
    key_heads = keys.reshape(split_shape)
    value_heads = values.reshape(split_shape)
    position = jnp.arange(block_len)
    causal = position[:, None] >= position[None, :]
    cumulative = jnp.sum(jnp.where(causal[:, :, None], decay_log[None], 0.0), axis=1)
    gap_log = cumulative[:, None, :] - cumulative[None, :, :]
    decay_grid = jnp.exp(jnp.where(causal[:, :, None], gap_log, -1e30))
    block_end = cumulative[-1]
    keys_faded = jnp.exp(block_end[None, :] - cumulative)[None, :, :, None] * key_heads.astype(
        jnp.float32
    )
    local_state = jnp.einsum(
        "sjhd,sjhe->shde",
        keys_faded,
        value_heads.astype(jnp.float32),
        precision=lax.Precision.HIGHEST,
    )
    incoming = incoming_states(local_state, block_end)
    row_weight = lax.all_gather(out_weight, "y", axis=1, tiled=True)
    scores = jnp.einsum(
        "sihd,sjhd->sijh", query_heads, key_heads, preferred_element_type=jnp.float32
    )
    weights = (scores * decay_grid[None]).astype(jnp.bfloat16)
    within = jnp.einsum("sijh,sjhd->sihd", weights, value_heads, preferred_element_type=jnp.float32)
    carried = jnp.exp(cumulative)[None, :, :, None] * jnp.einsum(
        "sihd,shde->sihe", query_heads, incoming, preferred_element_type=jnp.float32
    )
    attended = within + carried
    mean_square = jnp.mean(attended * attended, axis=-1, keepdims=True)
    gate_act = jax.nn.sigmoid(out_gate.reshape(split_shape).astype(jnp.float32))
    gated = (
        attended
        * lax.rsqrt(mean_square + 1e-06)
        * head_gain.reshape(head_count, head_dim)
        * gate_act
    )
    mixed = gated.astype(jnp.bfloat16).reshape(seq_count, block_len, head_width)
    sub_len = stream.shape[1]
    model_width = stream.shape[2]
    exp_count = lax.axis_size(EXP)
    x_count = lax.axis_size("x")
    y_count = lax.axis_size("y")
    ctx_count = x_count * y_count
    tok_count = seq_count * sub_len
    ordered = (
        mixed.reshape(seq_count, exp_count, sub_len, head_width)
        .transpose(1, 0, 2, 3)
        .reshape(exp_count, tok_count, head_width)
    )
    row_tokens = lax.all_gather(ordered, "x", axis=1, tiled=True)
    part_width = row_weight.shape[1]
    product = jnp.dot(
        row_tokens.reshape(exp_count * x_count * tok_count, head_width),
        row_weight,
        preferred_element_type=jnp.float32,
    ).astype(jnp.bfloat16)
    column_part = lax.psum_scatter(product, EXP, scatter_dimension=0, tiled=True)
    projected = lax.all_to_all(
        column_part.reshape(x_count, tok_count, part_width), "x", split_axis=0, concat_axis=0, tiled=True
    )
    projected = (
        projected.reshape(x_count, tok_count, y_count, part_width // y_count)
        .transpose(1, 2, 0, 3)
        .reshape(tok_count, model_width)
        .astype(jnp.float32)
    )
    residual_sum = stream.reshape(tok_count, model_width).astype(jnp.float32) + projected
    stream_square = jnp.mean(residual_sum * residual_sum, axis=-1, keepdims=True)
    normed = (residual_sum * lax.rsqrt(stream_square + 1e-06) * norm_gain).astype(jnp.bfloat16)
    expert_count = exp_count
    capacity = max(2, (2 * tok_count + expert_count - 1) // expert_count + 1)
    slot_total = expert_count * capacity
    picks = expert_ids.reshape(2 * tok_count)
    copy_no = jnp.arange(2 * tok_count)
    earlier = (copy_no[None, :] < copy_no[:, None]) & (picks[None, :] == picks[:, None])
    ranking = jnp.sum(earlier.astype(jnp.int32), axis=1)
    slot_of = picks * capacity + ranking
    placing = slot_of[:, None] == jnp.arange(slot_total, dtype=jnp.int32)[None, :]
    token_placing = jnp.any(placing.reshape(tok_count, 2, slot_total), axis=1)
    dispatch = jnp.dot(
        token_placing.T.astype(jnp.bfloat16), normed, preferred_element_type=jnp.float32
    ).astype(jnp.bfloat16)
    dispatch = dispatch.reshape(exp_count, capacity, model_width)
    received = lax.all_to_all(dispatch, EXP, split_axis=0, concat_axis=0, tiled=True)
    hid_a, hid_b = expert_terms(received.reshape(slot_total, model_width), w_gate[0].T, w_up[0].T)
    summed = expert_sum(hid_a, hid_b, w_down[0])
    returned = lax.all_to_all(
        summed.reshape(exp_count, capacity, model_width), EXP, split_axis=0, concat_axis=0, tiled=True
    ).reshape(slot_total, model_width)
    weighting = jnp.where(placing, expert_share.reshape(2 * tok_count, 1), 0.0)
    weighting = jnp.sum(weighting.reshape(tok_count, 2, slot_total), axis=1)
    expert_mix = jnp.dot(weighting, returned.astype(jnp.float32), precision=lax.Precision.HIGHEST)
    result = (residual_sum + expert_mix).astype(jnp.bfloat16)
    return result.reshape(seq_count, sub_len, model_width)


def solution(mesh):
    n_exp = mesh.shape["exp"]
    side = round(mesh.shape["ctx"] ** 0.5)
    fine = Mesh(mesh.devices.reshape(side, side, n_exp // 2, 2), ("y", "x", "z", "c"))
    return jax.shard_map(
        body,
        mesh=fine,
        in_specs=(
            P(None, CTX, EXP),
            P(None, CTX, EXP),
            P(None, CTX, EXP),
            P(CTX, EXP),
            P(None, CTX, EXP),
            P(EXP),
            P(EXP, CTX),
            P(None, CTX + EXP, None),
            P(),
            P(CTX + EXP, None, None),
            P(CTX + EXP, None, None),
            P(EXP, None, CTX),
            P(EXP, None, CTX),
            P(EXP, CTX, None),
        ),
        out_specs=P(None, CTX + EXP, None),
        check_vma=False,
    )
```

```python
import jax
import jax.numpy as jnp
from jax import lax
from jax.experimental import pallas as pl
from jax.experimental.pallas import tpu as pltpu
from jax.sharding import Mesh, PartitionSpec as P

CTX = ("y", "x")
EXP = ("z", "c")


MESH = pl.DeviceIdType.MESH
AXES = (("x", "y"), ("y", "x"))


def greet(pairs):
    barrier = pltpu.get_barrier_semaphore()
    for axis, to in pairs:
        pl.semaphore_signal(barrier, inc=1, device_id={axis: to}, device_id_type=MESH)
    pl.semaphore_wait(barrier, len(pairs))


def gather_kernel(
    rows_ref, wg_hbm, wu_hbm, hid_a, hid_b, buf_a, buf_b, wg, wu, xin, acc_g, acc_u, ssem, rsem, lsem
):
    n = 4
    count, width = rows_ref.shape
    half = width // 2
    quarter = half // 2
    hidden = wg.shape[0]
    buf = (buf_a, buf_b)
    place = {a: lax.axis_index(a) for a in ("x", "y")}

    def step(axis, by):
        return lax.rem(place[axis] + (by + n), n)

    load_g = pltpu.make_async_copy(wg_hbm, wg, lsem.at[0])
    load_u = pltpu.make_async_copy(wu_hbm, wu, lsem.at[1])
    load_g.start()
    load_u.start()
    greet([(a, step(a, d)) for a in ("x", "y") for d in (1, -1)])

    def row(h, fi, si):
        return buf[h].at[fi, pl.ds(pl.multiple_of(si * count, 8), count)]

    def cut(ref, k):
        return ref.at[:, pl.ds((k - 2) * quarter, quarter)] if k >= 2 else ref

    def send(h, stage, kind, axis, src, dst):
        to = step(axis, 1 if kind % 2 == 0 else -1)
        c = pltpu.make_async_remote_copy(
            src_ref=cut(src, kind),
            dst_ref=cut(dst, kind),
            send_sem=ssem.at[h, stage, kind],
            recv_sem=rsem.at[h, stage, kind],
            device_id={axis: to},
            device_id_type=MESH,
        )
        c.start()
        sent.append(c)

    def arrived(h, stage, kind, axis, dst):
        pltpu.make_async_remote_copy(
            src_ref=cut(dst, kind),
            dst_ref=cut(dst, kind),
            send_sem=ssem.at[h, stage, kind],
            recv_sem=rsem.at[h, stage, kind],
            device_id={axis: step(axis, 1)},
            device_id_type=MESH,
        ).wait_recv()

    sent = []
    shift = (0, -1, 1, 2)
    own = [rows_ref.at[:, pl.ds(h * half, half)] for h in range(2)]
    keep = []
    for h in range(2):
        first, second = AXES[h]
        mine = row(h, place[first], place[second])
        for kind in range(2):
            send(h, n, kind, first, own[h], mine)
    for h in range(2):
        first, second = AXES[h]
        mine = row(h, place[first], place[second])
        for kind in range(2):
            send(h, 0, kind, second, own[h], mine)
        keep.append(pltpu.make_async_copy(own[h], mine, lsem.at[2 + h]))
        keep[h].start()
    acc_g[...] = jnp.zeros_like(acc_g)
    acc_u[...] = jnp.zeros_like(acc_u)

    def spread(h, j):
        first, second = AXES[h]
        here = row(h, step(first, shift[j]), place[second])
        for kind in range(2):
            send(h, j, kind, second, here, here)

    def pass_on(h, stage, kind):
        first, second = AXES[h]
        by = -1 if kind == 0 else 1
        if stage == n:
            here = row(h, step(first, by), place[second])
            axis = first
        else:
            here = row(h, step(first, shift[stage]), step(second, by))
            axis = second
        arrived(h, stage, kind, axis, here)
        send(h, stage, kind + 2, axis, here, here)

    def far(h, stage):
        first, second = AXES[h]
        if stage == n:
            here, axis = row(h, step(first, 2), place[second]), first
        else:
            here, axis = row(h, step(first, shift[stage]), step(second, 2)), second
        for kind in (2, 3):
            arrived(h, stage, kind, axis, here)

    def load(h, j):
        return pltpu.make_async_copy(
            buf[h].at[step(AXES[h][0], shift[j])], xin.at[h], lsem.at[4 + h]
        )

    def multiply(h, j):
        load(h, j).wait()
        fi = step(AXES[h][0], shift[j])
        for w, acc in ((wg, acc_g), (wu, acc_u)):
            got = lax.dot_general(
                xin[h],
                w[:, pl.ds(h * half, half)],
                (((1,), (1,)), ((), ())),
                preferred_element_type=jnp.float32,
            ).reshape(n, count, hidden)
            if h == 0:
                acc[fi] += got
            else:
                acc[:, fi] += got

    for kind in range(2):
        for h in range(2):
            pass_on(h, n, kind)
            spread(h, 1 + kind)
    for kind in range(2):
        for h in range(2):
            pass_on(h, 0, kind)
    for h in range(2):
        far(h, n)
        spread(h, 3)
    load_g.wait()
    load_u.wait()
    for j in range(n):
        if j + 1 < n:
            for kind in range(2):
                for h in range(2):
                    pass_on(h, j + 1, kind)
        for h in range(2):
            if j == 0:
                keep[h].wait()
            far(h, j)
            load(h, j).start()
        for h in range(2):
            multiply(h, j)

    @pl.loop(0, n)
    def _(p):
        g = acc_g[p].reshape(n * count, hidden)
        u = acc_u[p].reshape(n * count, hidden)
        out = (g / (1.0 + jnp.exp(-g)) * u).astype(jnp.bfloat16)
        hid_a[pl.ds(pl.multiple_of(p * (n * count), 16), n * count), :] = out
        acc_g[p] = out.astype(jnp.float32).reshape(n, count, hidden)

    @pl.loop(0, n)
    def _(q):
        back = acc_g[:, pl.ds(q, 1)].reshape(n * count, hidden)
        hid_b[pl.ds(pl.multiple_of(q * (n * count), 16), n * count), :] = back.astype(jnp.bfloat16)

    for c in sent:
        c.wait_send()


def reduce_kernel(
    hid_a, hid_b, wd_hbm, out_ref, wd, t_a, t_b, r_opp, r_full, part, r_opp2, r_full2, ssem, rsem, lsem
):
    n = 4
    count, width = out_ref.shape
    half = width // 2
    quarter = half // 2
    block = min(512, quarter)
    hid = (hid_a, hid_b)
    t = (t_a, t_b)
    place = {a: lax.axis_index(a) for a in ("x", "y")}

    def step(axis, by):
        return lax.rem(place[axis] + (by + n), n)

    load = pltpu.make_async_copy(wd_hbm, wd, lsem.at[0])
    load.start()
    greet([(a, step(a, d)) for a in ("x", "y") for d in (1, -1)])
    load.wait()
    shift = (2, 1, -1, 0)
    sent = []

    def copy(h, stage, kind, axis, src, dst):
        return pltpu.make_async_remote_copy(
            src_ref=src,
            dst_ref=dst,
            send_sem=ssem.at[h, stage, kind],
            recv_sem=rsem.at[h, stage, kind],
            device_id={axis: step(axis, 1 if kind % 2 == 0 else -1)},
            device_id_type=MESH,
        )

    def send(*a):
        c = copy(*a)
        c.start()
        sent.append(c)

    def arrived(h, stage, kind, axis, dst):
        copy(h, stage, kind, axis, dst, dst).wait_recv()

    def multiply(h, j):
        lead = step(AXES[h][0], shift[j])
        x = hid[h].at[pl.ds(pl.multiple_of(lead * (n * count), 16), n * count), :]

        @pl.loop(0, half // block)
        def _(b):
            at = pl.multiple_of(b * block, 128)
            got = jnp.dot(
                x[...],
                wd[:, pl.ds(pl.multiple_of(h * half + at, 128), block)],
                preferred_element_type=jnp.float32,
            )
            t[h][j, :, :, pl.ds(at, block)] = got.reshape(n, count, block).astype(jnp.bfloat16)

        ring = AXES[h][1]
        for k in range(2):
            send(
                h,
                j,
                k,
                ring,
                t[h].at[j, step(ring, 2), :, pl.ds(k * quarter, quarter)],
                r_opp.at[h, j, k],
            )

    def add_to(ref, k, other):
        @pl.loop(0, quarter // block)
        def _(b):
            at = pl.multiple_of(b * block, 128)
            cols = pl.ds(pl.multiple_of(k * quarter + at, 128), block)
            ref[:, cols] = (
                ref[:, cols].astype(jnp.float32) + other[:, pl.ds(at, block)].astype(jnp.float32)
            ).astype(jnp.bfloat16)

    def total(dst, start, refs):
        @pl.loop(0, half // block)
        def _(b):
            at = pl.multiple_of(b * block, 128)
            s = refs[0][:, pl.ds(at, block)].astype(jnp.float32)
            for r in refs[1:]:
                s = s + r[:, pl.ds(at, block)].astype(jnp.float32)
            dst[:, pl.ds(pl.multiple_of(start + at, 128), block)] = s.astype(jnp.bfloat16)

    def near(h, j):
        ring = AXES[h][1]
        for k in range(2):
            arrived(h, j, k, ring, r_opp.at[h, j, k])
            mine = t[h].at[j, step(ring, 1 if k == 0 else -1)]
            add_to(mine, k, r_opp.at[h, j, k])
            send(h, j, 2 + k, ring, mine, r_full.at[h, j, k])

    def both(h, j):
        for k in range(2):
            arrived(h, j, 2 + k, AXES[h][1], r_full.at[h, j, k])

    def finish(h, j):
        both(h, j)
        total(
            part.at[h, j],
            0,
            [t[h].at[j, place[AXES[h][1]]], r_full.at[h, j, 0], r_full.at[h, j, 1]],
        )

    for j in range(2):
        for h in range(2):
            multiply(h, j)
    for j in range(n):
        for h in range(2):
            near(h, j)
        if j + 2 < n:
            for h in range(2):
                multiply(h, j + 2)
        if j == 1:
            for h in range(2):
                finish(h, 0)
                for k in range(2):
                    send(
                        h,
                        n,
                        k,
                        AXES[h][0],
                        part.at[h, 0, :, pl.ds(k * quarter, quarter)],
                        r_opp2.at[h, k],
                    )
    for j in (1, 2):
        for h in range(2):
            finish(h, j)
            k = j - 1
            arrived(h, n, k, AXES[h][0], r_opp2.at[h, k])
            add_to(part.at[h, j], k, r_opp2.at[h, k])
            send(h, n, 2 + k, AXES[h][0], part.at[h, j], r_full2.at[h, k])
    for h in range(2):
        both(h, 3)
        for k in range(2):
            arrived(h, n, 2 + k, AXES[h][0], r_full2.at[h, k])
        total(
            out_ref,
            h * half,
            [
                t[h].at[3, place[AXES[h][1]]],
                r_full.at[h, 3, 0],
                r_full.at[h, 3, 1],
                r_full2.at[h, 0],
                r_full2.at[h, 1],
            ],
        )
    for c in sent:
        c.wait_send()


def expert_terms(rows, w_gate, w_up):
    n = 4
    count, width = rows.shape
    hidden = w_gate.shape[0]
    half = width // 2
    any_spec = pl.BlockSpec(memory_space=pl.ANY)
    vmem = pl.BlockSpec(memory_space=pltpu.VMEM)
    bf16 = jnp.bfloat16
    return pl.pallas_call(
        gather_kernel,
        out_shape=[
            jax.ShapeDtypeStruct((n * n * count, hidden), bf16),
            jax.ShapeDtypeStruct((n * n * count, hidden), bf16),
            jax.ShapeDtypeStruct((n, n * count, half), bf16),
            jax.ShapeDtypeStruct((n, n * count, half), bf16),
        ],
        in_specs=[any_spec] * 3,
        out_specs=[vmem, vmem, any_spec, any_spec],
        scratch_shapes=[
            pltpu.VMEM((hidden, width), bf16),
            pltpu.VMEM((hidden, width), bf16),
            pltpu.VMEM((2, n * count, half), bf16),
            pltpu.VMEM((n, n, count, hidden), jnp.float32),
            pltpu.VMEM((n, n, count, hidden), jnp.float32),
            pltpu.SemaphoreType.DMA((2, n + 1, 4)),
            pltpu.SemaphoreType.DMA((2, n + 1, 4)),
            pltpu.SemaphoreType.DMA((6,)),
        ],
        compiler_params=pltpu.CompilerParams(
            collective_id=1, has_side_effects=True, vmem_limit_bytes=60 << 20
        ),
        name="gather_experts",
    )(rows, w_gate, w_up)[:2]


def expert_sum(hid_a, hid_b, w_down):
    n = 4
    hidden, width = w_down.shape
    count = hid_a.shape[0] // (n * n)
    half = width // 2
    any_spec = pl.BlockSpec(memory_space=pl.ANY)
    vmem = pl.BlockSpec(memory_space=pltpu.VMEM)
    bf16 = jnp.bfloat16
    return pl.pallas_call(
        reduce_kernel,
        out_shape=jax.ShapeDtypeStruct((count, width), bf16),
        in_specs=[vmem, vmem, any_spec],
        out_specs=vmem,
        scratch_shapes=[
            pltpu.VMEM((hidden, width), bf16),
            pltpu.VMEM((n, n, count, half), bf16),
            pltpu.VMEM((n, n, count, half), bf16),
            pltpu.VMEM((2, n, 2, count, half // 2), bf16),
            pltpu.VMEM((2, n, 2, count, half), bf16),
            pltpu.VMEM((2, 3, count, half), bf16),
            pltpu.VMEM((2, 2, count, half // 2), bf16),
            pltpu.VMEM((2, 2, count, half), bf16),
            pltpu.SemaphoreType.DMA((2, n + 1, 4)),
            pltpu.SemaphoreType.DMA((2, n + 1, 4)),
            pltpu.SemaphoreType.DMA((1,)),
        ],
        compiler_params=pltpu.CompilerParams(
            collective_id=2, has_side_effects=True, vmem_limit_bytes=60 << 20
        ),
        name="sum_experts",
    )(hid_a, hid_b, w_down)


def state_kernel(chunks, fades, out_ref, got, got_fade, held, ssem, rsem):
    n = chunks.shape[0]
    side = 4
    per = chunks.shape[1]
    heads = fades.shape[0]
    me = lax.axis_index("y") * side + lax.axis_index("x")

    def where(t):
        return {"y": t // side, "x": lax.rem(t, side)}

    def copy(kind, d, src, dst, t):
        return pltpu.make_async_remote_copy(
            src_ref=src,
            dst_ref=dst,
            send_sem=ssem.at[kind, d],
            recv_sem=rsem.at[kind, d],
            device_id=where(t),
            device_id_type=MESH,
        )

    def fade_of(t):
        return fades.at[pl.ds(lax.rem(t * per, heads), per)]

    barrier = pltpu.get_barrier_semaphore()

    @pl.loop(1, n)
    def _(d):
        pl.semaphore_signal(
            barrier, inc=1, device_id=where(lax.rem(me + d, n)), device_id_type=MESH
        )

    pl.semaphore_wait(barrier, n - 1)

    @pl.loop(1, n)
    def _(d):
        t = lax.rem(me + d, n)
        copy(0, d, chunks.at[t], got.at[me], t).start()
        copy(1, d, fade_of(t), got_fade.at[me], t).start()

    got[me] = chunks[me]
    got_fade[me] = fade_of(me)[...]

    @pl.loop(1, n)
    def _(d):
        t = lax.rem(me + d, n)
        frm = lax.rem(me - d + n, n)
        copy(0, d, chunks.at[t], got.at[frm], t).wait()
        copy(1, d, fade_of(t), got_fade.at[frm], t).wait()

    def advance(b, state):
        held[b] = state.astype(jnp.bfloat16)
        d = lax.rem(b - me + n, n)

        @pl.when(d != 0)
        def _():
            copy(2, d, held.at[b], out_ref.at[me], b).start()

        return got_fade[b][:, :1, :] * state + got[b].astype(jnp.float32)

    lax.fori_loop(0, n, advance, jnp.zeros(got.shape[1:], jnp.float32))
    out_ref[me] = held[me]

    @pl.loop(1, n)
    def _(d):
        t = lax.rem(me + d, n)
        frm = lax.rem(me - d + n, n)
        copy(2, d, held.at[t], out_ref.at[frm], t).wait()


def incoming_states(local_state, block_end):
    seqs, heads, width, _ = local_state.shape
    n = lax.axis_size(CTX)
    per = seqs * heads // n
    chunks = local_state.reshape(n, per, width, width).astype(jnp.bfloat16)
    fades = jnp.broadcast_to(jnp.exp(block_end)[:, None, None], (heads, 8, width))
    vmem = pl.BlockSpec(memory_space=pltpu.VMEM)
    out = pl.pallas_call(
        state_kernel,
        out_shape=jax.ShapeDtypeStruct(chunks.shape, jnp.bfloat16),
        in_specs=[vmem] * 2,
        out_specs=vmem,
        scratch_shapes=[
            pltpu.VMEM(chunks.shape, jnp.bfloat16),
            pltpu.VMEM((n, per, 8, width), jnp.float32),
            pltpu.VMEM(chunks.shape, jnp.bfloat16),
            pltpu.SemaphoreType.DMA((3, n)),
            pltpu.SemaphoreType.DMA((3, n)),
        ],
        compiler_params=pltpu.CompilerParams(
            collective_id=3, has_side_effects=True, vmem_limit_bytes=32 << 20
        ),
        name="carry_states",
    )(chunks, fades)
    return out.reshape(local_state.shape)


def project_kernel(
    tok_ref, w_hbm, out_ref, w, tok, prod, other, ring_opp, ring_full, done, ssem, rsem, lsem
):
    n = 4
    cores, zs, count, width = prod.shape[1:]
    feats = tok_ref.shape[1]
    half_f = feats // 2
    half = width // 2
    block = min(512, width)
    x = lax.axis_index("x")
    z = lax.axis_index("z")
    c = lax.axis_index("c")

    def xs(by):
        return lax.rem(x + (by + n), n)

    def zz(by):
        return lax.rem(z + (by + n), n)

    load = pltpu.make_async_copy(w_hbm, w, lsem.at[0])
    load.start()
    greet(
        [("x", xs(1)), ("x", xs(-1)), ("x", xs(2)), ("z", zz(1)), ("z", zz(-1)), ("c", 1 - c)]
    )
    sent = []

    def copy(j, kind, src, dst, axis, to):
        return pltpu.make_async_remote_copy(
            src_ref=src,
            dst_ref=dst,
            send_sem=ssem.at[j, kind],
            recv_sem=rsem.at[j, kind],
            device_id={axis: to},
            device_id_type=MESH,
        )

    def send(*a):
        cp = copy(*a)
        cp.start()
        sent.append(cp)

    def arrived(j, kind, dst, axis):
        copy(j, kind, dst, dst, axis, xs(1) if axis == "x" else zz(1) if axis == "z" else 1 - c).wait_recv()

    shift = (0, -1, 1, 2)
    send(0, 0, tok_ref, tok.at[0], "x", xs(1))
    send(0, 1, tok_ref, tok.at[1], "x", xs(-1))
    load.wait()

    def dot(j):
        src = tok_ref if j == 0 else tok.at[j - 1]

        @pl.loop(0, width // block)
        def _(b):
            cols = pl.ds(pl.multiple_of(b * block, 128), block)
            got = jnp.dot(src[...], w[:, cols], preferred_element_type=jnp.float32)
            prod[j, :, :, :, cols] = got.reshape(cores, zs, count, block).astype(jnp.bfloat16)

        send(j, 2, prod.at[j, 1 - c], other.at[j], "c", 1 - c)

    def core_add(j):
        arrived(j, 2, other.at[j], "c")
        mine = prod.at[j, c]

        @pl.loop(0, width // block)
        def _(b):
            cols = pl.ds(pl.multiple_of(b * block, 128), block)
            mine[:, :, cols] = (
                mine[:, :, cols].astype(jnp.float32) + other[j, :, :, cols].astype(jnp.float32)
            ).astype(jnp.bfloat16)

        for k in range(2):
            send(
                j,
                3 + k,
                mine.at[zz(2), :, pl.ds(k * half, half)],
                ring_opp.at[j, k],
                "z",
                zz(1 if k == 0 else -1),
            )

    def near(j):
        for k in range(2):
            arrived(j, 3 + k, ring_opp.at[j, k], "z")
            to = zz(1 if k == 0 else -1)
            mine = prod.at[j, c, to]
            cols = pl.ds(k * half, half)
            mine[:, cols] = (
                mine[:, cols].astype(jnp.float32) + ring_opp[j, k].astype(jnp.float32)
            ).astype(jnp.bfloat16)
            send(j, 5 + k, mine, ring_full.at[j, k], "z", to)

    def finish(j):
        for k in range(2):
            arrived(j, 5 + k, ring_full.at[j, k], "z")
        s = (
            prod[j, c, z].astype(jnp.float32)
            + ring_full[j, 0].astype(jnp.float32)
            + ring_full[j, 1].astype(jnp.float32)
        ).astype(jnp.bfloat16)
        if j == 0:
            out_ref[x] = s
        else:
            done[j] = s
            send(j, 7, done.at[j], out_ref.at[x], "x", xs(shift[j]))

    dot(0)
    for k in range(2):
        arrived(0, k, tok.at[k], "x")
        cols = pl.ds(k * half_f, half_f)
        send(1, k, tok.at[k, :, cols], tok.at[2, :, cols], "x", xs(1 if k == 0 else -1))
    dot(1)
    core_add(0)
    dot(2)
    core_add(1)
    near(0)
    for k in range(2):
        arrived(1, k, tok.at[2, :, pl.ds(k * half_f, half_f)], "x")
    dot(3)
    core_add(2)
    near(1)
    core_add(3)
    finish(0)
    near(2)
    finish(1)
    near(3)
    finish(2)
    finish(3)
    for j in (1, 2, 3):
        arrived(j, 7, out_ref.at[xs(-shift[j])], "x")
    for cp in sent:
        cp.wait_send()


def project(tokens, weight):
    n = 4
    rows, feats = tokens.shape
    width = weight.shape[1]
    cores, zs = lax.axis_size("c"), lax.axis_size("z")
    count = rows // (cores * zs)
    bf16 = jnp.bfloat16
    vmem = pl.BlockSpec(memory_space=pltpu.VMEM)
    return pl.pallas_call(
        project_kernel,
        out_shape=jax.ShapeDtypeStruct((n, count, width), bf16),
        in_specs=[vmem, pl.BlockSpec(memory_space=pl.ANY)],
        out_specs=vmem,
        scratch_shapes=[
            pltpu.VMEM((feats, width), bf16),
            pltpu.VMEM((3, rows, feats), bf16),
            pltpu.VMEM((n, cores, zs, count, width), bf16),
            pltpu.VMEM((n, zs, count, width), bf16),
            pltpu.VMEM((n, 2, count, width // 2), bf16),
            pltpu.VMEM((n, 2, count, width), bf16),
            pltpu.VMEM((n, count, width), bf16),
            pltpu.SemaphoreType.DMA((n, 8)),
            pltpu.SemaphoreType.DMA((n, 8)),
            pltpu.SemaphoreType.DMA((1,)),
        ],
        compiler_params=pltpu.CompilerParams(
            collective_id=4, has_side_effects=True, vmem_limit_bytes=48 << 20
        ),
        name="project",
    )(tokens, weight)


def fold(rows, parts):
    slots, width = rows.shape
    main = slots // parts - 1
    body_rows = rows[: parts * main].reshape(parts, main, width)
    last_rows = rows[parts * main :].reshape(parts, main, width // main)
    return jnp.concatenate([body_rows, last_rows], axis=2)


def unfold(folded):
    parts, main, wide = folded.shape
    width = wide * main // (main + 1)
    body_rows = folded[:, :, :width].reshape(parts * main, width)
    last_rows = folded[:, :, width:].reshape(parts, width)
    return jnp.concatenate([body_rows, last_rows], axis=0)


def body(
    queries,
    keys,
    values,
    decay_log,
    out_gate,
    head_gain,
    out_weight,
    stream,
    norm_gain,
    expert_ids,
    expert_share,
    w_gate,
    w_up,
    w_down,
):
    seq_count, block_len, head_width = queries.shape
    head_count = decay_log.shape[1]
    head_dim = head_width // head_count
    split_shape = (seq_count, block_len, head_count, head_dim)
    query_heads = queries.reshape(split_shape)
    key_heads = keys.reshape(split_shape)
    value_heads = values.reshape(split_shape)
    position = jnp.arange(block_len)
    causal = position[:, None] >= position[None, :]
    cumulative = jnp.sum(jnp.where(causal[:, :, None], decay_log[None], 0.0), axis=1)
    gap_log = cumulative[:, None, :] - cumulative[None, :, :]
    decay_grid = jnp.exp(jnp.where(causal[:, :, None], gap_log, -1e30))
    block_end = cumulative[-1]
    keys_faded = jnp.exp(block_end[None, :] - cumulative)[None, :, :, None] * key_heads.astype(
        jnp.float32
    )
    local_state = jnp.einsum(
        "sjhd,sjhe->shde",
        keys_faded,
        value_heads.astype(jnp.float32),
        precision=lax.Precision.HIGHEST,
    )
    incoming = incoming_states(local_state, block_end)
    row_weight = lax.all_gather(out_weight, "y", axis=1, tiled=True)
    scores = jnp.einsum(
        "sihd,sjhd->sijh", query_heads, key_heads, preferred_element_type=jnp.float32
    )
    weights = (scores * decay_grid[None]).astype(jnp.bfloat16)
    within = jnp.einsum("sijh,sjhd->sihd", weights, value_heads, preferred_element_type=jnp.float32)
    carried = jnp.exp(cumulative)[None, :, :, None] * jnp.einsum(
        "sihd,shde->sihe", query_heads, incoming, preferred_element_type=jnp.float32
    )
    attended = within + carried
    mean_square = jnp.mean(attended * attended, axis=-1, keepdims=True)
    gate_act = jax.nn.sigmoid(out_gate.reshape(split_shape).astype(jnp.float32))
    gated = (
        attended
        * lax.rsqrt(mean_square + 1e-06)
        * head_gain.reshape(head_count, head_dim)
        * gate_act
    )
    mixed = gated.astype(jnp.bfloat16).reshape(seq_count, block_len, head_width)
    sub_len = stream.shape[1]
    model_width = stream.shape[2]
    exp_count = lax.axis_size(EXP)
    x_count = lax.axis_size("x")
    y_count = lax.axis_size("y")
    ctx_count = x_count * y_count
    tok_count = seq_count * sub_len
    ordered = (
        mixed.reshape(seq_count, exp_count // 2, 2, sub_len, head_width)
        .transpose(2, 1, 0, 3, 4)
        .reshape(exp_count * tok_count, head_width)
    )
    projected = project(ordered, row_weight)
    part_width = row_weight.shape[1]
    projected = (
        projected.reshape(x_count, tok_count, y_count, part_width // y_count)
        .transpose(1, 2, 0, 3)
        .reshape(tok_count, model_width)
        .astype(jnp.float32)
    )
    residual_sum = stream.reshape(tok_count, model_width).astype(jnp.float32) + projected
    stream_square = jnp.mean(residual_sum * residual_sum, axis=-1, keepdims=True)
    normed = (residual_sum * lax.rsqrt(stream_square + 1e-06) * norm_gain).astype(jnp.bfloat16)
    expert_count = exp_count
    capacity = max(2, (2 * tok_count + expert_count - 1) // expert_count + 1)
    slot_total = expert_count * capacity
    picks = expert_ids.reshape(2 * tok_count)
    copy_no = jnp.arange(2 * tok_count)
    earlier = (copy_no[None, :] < copy_no[:, None]) & (picks[None, :] == picks[:, None])
    ranking = jnp.sum(earlier.astype(jnp.int32), axis=1)
    main = capacity - 1
    slot_of = jnp.where(ranking < main, picks * main + ranking, expert_count * main + picks)
    placing = slot_of[:, None] == jnp.arange(slot_total, dtype=jnp.int32)[None, :]
    token_placing = jnp.any(placing.reshape(tok_count, 2, slot_total), axis=1)
    dispatch = jnp.dot(
        token_placing.T.astype(jnp.bfloat16), normed, preferred_element_type=jnp.float32
    ).astype(jnp.bfloat16)
    received = unfold(lax.all_to_all(fold(dispatch, exp_count), EXP, split_axis=0, concat_axis=0, tiled=True))
    hid_a, hid_b = expert_terms(received, w_gate[0].T, w_up[0].T)
    summed = expert_sum(hid_a, hid_b, w_down[0])
    returned = unfold(lax.all_to_all(fold(summed, exp_count), EXP, split_axis=0, concat_axis=0, tiled=True))
    weighting = jnp.where(placing, expert_share.reshape(2 * tok_count, 1), 0.0)
    weighting = jnp.sum(weighting.reshape(tok_count, 2, slot_total), axis=1)
    expert_mix = jnp.dot(weighting, returned.astype(jnp.float32), precision=lax.Precision.HIGHEST)
    result = (residual_sum + expert_mix).astype(jnp.bfloat16)
    return result.reshape(seq_count, sub_len, model_width)


def solution(mesh):
    n_exp = mesh.shape["exp"]
    side = round(mesh.shape["ctx"] ** 0.5)
    fine = Mesh(mesh.devices.reshape(side, side, n_exp // 2, 2), ("y", "x", "z", "c"))
    return jax.shard_map(
        body,
        mesh=fine,
        in_specs=(
            P(None, CTX, EXP),
            P(None, CTX, EXP),
            P(None, CTX, EXP),
            P(CTX, EXP),
            P(None, CTX, EXP),
            P(EXP),
            P(EXP, CTX),
            P(None, CTX + EXP, None),
            P(),
            P(CTX + EXP, None, None),
            P(CTX + EXP, None, None),
            P(EXP, None, CTX),
            P(EXP, None, CTX),
            P(EXP, CTX, None),
        ),
        out_specs=P(None, CTX + EXP, None),
        check_vma=False,
    )
```

```python
import jax
import jax.numpy as jnp
from jax import lax
from jax.experimental import pallas as pl
from jax.experimental.pallas import tpu as pltpu
from jax.sharding import Mesh, PartitionSpec as P

CTX = ("y", "x")
EXP = ("z", "c")


MESH = pl.DeviceIdType.MESH
AXES = (("x", "y"), ("y", "x"))


def greet(others):
    barrier = pltpu.get_barrier_semaphore()
    for where in others:
        pl.semaphore_signal(barrier, inc=1, device_id=where, device_id_type=MESH)
    pl.semaphore_wait(barrier, len(others))


def expert_place(t):
    return {"z": t // 2, "c": lax.rem(t, 2)}


def gather_kernel(
    main_ref,
    last_ref,
    wg_hbm,
    wu_hbm,
    hid_ref,
    buf_a,
    buf_b,
    rows_ref,
    wg,
    wu,
    xin,
    acc_g,
    acc_u,
    last_in,
    last_out,
    ssem,
    rsem,
    lsem,
    esend,
    erecv,
):
    n = 4
    experts, main, _ = main_ref.shape
    mine_e = lax.axis_index("z") * 2 + lax.axis_index("c")
    count, width = rows_ref.shape
    half = width // 2
    quarter = half // 2
    hidden = wg.shape[0]
    buf = (buf_a, buf_b)
    place = {a: lax.axis_index(a) for a in ("x", "y")}

    def step(axis, by):
        return lax.rem(place[axis] + (by + n), n)

    load_g = pltpu.make_async_copy(wg_hbm, wg, lsem.at[0])
    load_u = pltpu.make_async_copy(wu_hbm, wu, lsem.at[1])
    load_g.start()
    load_u.start()
    greet(
        [{a: step(a, d)} for a in ("x", "y") for d in (1, -1)]
        + [expert_place(lax.rem(mine_e + d, experts)) for d in range(1, experts)]
    )

    def main_rows(e):
        return rows_ref.at[pl.ds(pl.multiple_of(e * main, 8), main)]

    def deal(d, to, frm):
        return [
            pltpu.make_async_remote_copy(
                src_ref=src,
                dst_ref=dst,
                send_sem=esend.at[k, d],
                recv_sem=erecv.at[k, d],
                device_id=expert_place(to),
                device_id_type=MESH,
            )
            for k, (src, dst) in enumerate(
                ((main_ref.at[to], main_rows(frm)), (last_ref.at[to], last_in.at[frm]))
            )
        ]

    @pl.loop(1, experts)
    def _(d):
        for c in deal(d, lax.rem(mine_e + d, experts), mine_e):
            c.start()

    own_main = pltpu.make_async_copy(main_ref.at[mine_e], main_rows(mine_e), lsem.at[6])
    own_last = pltpu.make_async_copy(last_ref.at[mine_e], last_in.at[mine_e], lsem.at[7])
    own_main.start()
    own_last.start()
    acc_g[...] = jnp.zeros_like(acc_g)
    acc_u[...] = jnp.zeros_like(acc_u)
    own_main.wait()
    own_last.wait()

    @pl.loop(1, experts)
    def _(d):
        for c in deal(d, lax.rem(mine_e + d, experts), lax.rem(mine_e - d + experts, experts)):
            c.wait()

    last_out[...] = last_in[...].reshape(last_out.shape).astype(jnp.bfloat16)
    put_last = pltpu.make_async_copy(
        last_out, rows_ref.at[pl.ds(experts * main, experts)], lsem.at[6]
    )
    put_last.start()
    put_last.wait()

    def row(h, fi, si):
        return buf[h].at[fi, pl.ds(pl.multiple_of(si * count, 8), count)]

    def cut(ref, k):
        return ref.at[:, pl.ds((k - 2) * quarter, quarter)] if k >= 2 else ref

    def send(h, stage, kind, axis, src, dst):
        to = step(axis, 1 if kind % 2 == 0 else -1)
        c = pltpu.make_async_remote_copy(
            src_ref=cut(src, kind),
            dst_ref=cut(dst, kind),
            send_sem=ssem.at[h, stage, kind],
            recv_sem=rsem.at[h, stage, kind],
            device_id={axis: to},
            device_id_type=MESH,
        )
        c.start()
        sent.append(c)

    def arrived(h, stage, kind, axis, dst):
        pltpu.make_async_remote_copy(
            src_ref=cut(dst, kind),
            dst_ref=cut(dst, kind),
            send_sem=ssem.at[h, stage, kind],
            recv_sem=rsem.at[h, stage, kind],
            device_id={axis: step(axis, 1)},
            device_id_type=MESH,
        ).wait_recv()

    sent = []
    shift = (0, -1, 1, 2)
    own = [rows_ref.at[:, pl.ds(h * half, half)] for h in range(2)]
    keep = []
    for h in range(2):
        first, second = AXES[h]
        mine = row(h, place[first], place[second])
        for kind in range(2):
            send(h, n, kind, first, own[h], mine)
    for h in range(2):
        first, second = AXES[h]
        mine = row(h, place[first], place[second])
        for kind in range(2):
            send(h, 0, kind, second, own[h], mine)
        keep.append(pltpu.make_async_copy(own[h], mine, lsem.at[2 + h]))
        keep[h].start()

    def spread(h, j):
        first, second = AXES[h]
        here = row(h, step(first, shift[j]), place[second])
        for kind in range(2):
            send(h, j, kind, second, here, here)

    def pass_on(h, stage, kind):
        first, second = AXES[h]
        by = -1 if kind == 0 else 1
        if stage == n:
            here = row(h, step(first, by), place[second])
            axis = first
        else:
            here = row(h, step(first, shift[stage]), step(second, by))
            axis = second
        arrived(h, stage, kind, axis, here)
        send(h, stage, kind + 2, axis, here, here)

    def far(h, stage):
        first, second = AXES[h]
        if stage == n:
            here, axis = row(h, step(first, 2), place[second]), first
        else:
            here, axis = row(h, step(first, shift[stage]), step(second, 2)), second
        for kind in (2, 3):
            arrived(h, stage, kind, axis, here)

    def load(h, j):
        return pltpu.make_async_copy(
            buf[h].at[step(AXES[h][0], shift[j])], xin.at[h], lsem.at[4 + h]
        )

    def multiply(h, j):
        load(h, j).wait()
        fi = step(AXES[h][0], shift[j])
        for w, acc in ((wg, acc_g), (wu, acc_u)):
            got = lax.dot_general(
                xin[h],
                w[:, pl.ds(h * half, half)],
                (((1,), (1,)), ((), ())),
                preferred_element_type=jnp.float32,
            ).reshape(n, count, hidden)
            if h == 0:
                acc[fi] += got
            else:
                acc[:, fi] += got

    def activate(p, q):
        g = acc_g[p, q]
        out = (g / (1.0 + jnp.exp(-g)) * acc_u[p, q]).astype(jnp.bfloat16)
        hid_ref[p, q] = out.astype(jnp.float32)

    for kind in range(2):
        for h in range(2):
            pass_on(h, n, kind)
            spread(h, 1 + kind)
    for kind in range(2):
        for h in range(2):
            pass_on(h, 0, kind)
    for h in range(2):
        far(h, n)
        spread(h, 3)
    load_g.wait()
    load_u.wait()
    for j in range(n):
        if j + 1 < n:
            for kind in range(2):
                for h in range(2):
                    pass_on(h, j + 1, kind)
        for h in range(2):
            if j == 0:
                keep[h].wait()
            far(h, j)
            load(h, j).start()
        for h in range(2):
            multiply(h, j)
        if j == 2:

            @pl.loop(0, 9)
            def _(k):
                a, b = k // 3, lax.rem(k, 3)
                activate(step("x", a + a // 2), step("y", b + b // 2))

    @pl.loop(0, n)
    def _(k):
        activate(step("x", 2), step("y", k))

    @pl.loop(0, n - 1)
    def _(k):
        activate(step("x", k + k // 2), step("y", 2))

    for c in sent:
        c.wait_send()


def reduce_kernel(
    hid_ref,
    wd_hbm,
    back_main,
    back_last,
    wd,
    rows,
    t_a,
    t_b,
    r_opp,
    r_full,
    part,
    r_opp2,
    r_full2,
    out_main,
    out_last,
    ssem,
    rsem,
    lsem,
    esend,
    erecv,
):
    n = 4
    experts, main, width = out_main.shape
    count = experts * (main + 1)
    mine_e = lax.axis_index("z") * 2 + lax.axis_index("c")
    half = width // 2
    quarter = half // 2
    block = min(512, quarter)
    t = (t_a, t_b)
    place = {a: lax.axis_index(a) for a in ("x", "y")}

    def step(axis, by):
        return lax.rem(place[axis] + (by + n), n)

    load = pltpu.make_async_copy(wd_hbm, wd, lsem.at[0])
    load.start()
    greet(
        [{a: step(a, d)} for a in ("x", "y") for d in (1, -1)]
        + [expert_place(lax.rem(mine_e + d, experts)) for d in range(1, experts)]
    )
    load.wait()
    shift = (2, 1, -1, 0)
    sent = []

    def copy(h, stage, kind, axis, src, dst):
        return pltpu.make_async_remote_copy(
            src_ref=src,
            dst_ref=dst,
            send_sem=ssem.at[h, stage, kind],
            recv_sem=rsem.at[h, stage, kind],
            device_id={axis: step(axis, 1 if kind % 2 == 0 else -1)},
            device_id_type=MESH,
        )

    def send(*a):
        c = copy(*a)
        c.start()
        sent.append(c)

    def arrived(h, stage, kind, axis, dst):
        copy(h, stage, kind, axis, dst, dst).wait_recv()

    def multiply(h, j):
        lead = step(AXES[h][0], shift[j])
        taken = hid_ref[lead] if h == 0 else hid_ref[:, pl.ds(lead, 1)]
        rows[...] = taken.reshape(rows.shape).astype(jnp.bfloat16)

        @pl.loop(0, half // block)
        def _(b):
            at = pl.multiple_of(b * block, 128)
            got = jnp.dot(
                rows[...],
                wd[:, pl.ds(pl.multiple_of(h * half + at, 128), block)],
                preferred_element_type=jnp.float32,
            )
            t[h][j, :, :, pl.ds(at, block)] = got.reshape(n, count, block).astype(jnp.bfloat16)

        ring = AXES[h][1]
        for k in range(2):
            send(
                h,
                j,
                k,
                ring,
                t[h].at[j, step(ring, 2), :, pl.ds(k * quarter, quarter)],
                r_opp.at[h, j, k],
            )

    def add_to(ref, k, other):
        @pl.loop(0, quarter // block)
        def _(b):
            at = pl.multiple_of(b * block, 128)
            cols = pl.ds(pl.multiple_of(k * quarter + at, 128), block)
            ref[:, cols] = (
                ref[:, cols].astype(jnp.float32) + other[:, pl.ds(at, block)].astype(jnp.float32)
            ).astype(jnp.bfloat16)

    def add_up(refs, at):
        s = refs[0][:, pl.ds(at, block)].astype(jnp.float32)
        for r in refs[1:]:
            s = s + r[:, pl.ds(at, block)].astype(jnp.float32)
        return s

    def total(dst, refs):
        @pl.loop(0, half // block)
        def _(b):
            at = pl.multiple_of(b * block, 128)
            dst[:, pl.ds(at, block)] = add_up(refs, at).astype(jnp.bfloat16)

    def settle(h, refs):
        @pl.loop(0, half // block)
        def _(b):
            at = pl.multiple_of(b * block, 128)
            cols = pl.ds(pl.multiple_of(h * half + at, 128), block)
            s = add_up(refs, at)
            out_main[:, :, cols] = (
                s[: experts * main].reshape(experts, main, block).astype(jnp.bfloat16)
            )
            out_last[:, :, cols] = s[experts * main :].reshape(experts, 1, block)

    def give(k, d, to, frm):
        if k == 2:
            src, dst = out_last.at[to], back_last.at[frm]
        else:
            cols = pl.ds(k * half, half)
            src, dst = out_main.at[to, :, cols], back_main.at[frm, :, cols]
        return pltpu.make_async_remote_copy(
            src_ref=src,
            dst_ref=dst,
            send_sem=esend.at[k, d],
            recv_sem=erecv.at[k, d],
            device_id=expert_place(to),
            device_id_type=MESH,
        )

    def near(h, j):
        ring = AXES[h][1]
        for k in range(2):
            arrived(h, j, k, ring, r_opp.at[h, j, k])
            mine = t[h].at[j, step(ring, 1 if k == 0 else -1)]
            add_to(mine, k, r_opp.at[h, j, k])
            send(h, j, 2 + k, ring, mine, r_full.at[h, j, k])

    def both(h, j):
        for k in range(2):
            arrived(h, j, 2 + k, AXES[h][1], r_full.at[h, j, k])

    def finish(h, j):
        both(h, j)
        total(
            part.at[h, j],
            [t[h].at[j, place[AXES[h][1]]], r_full.at[h, j, 0], r_full.at[h, j, 1]],
        )

    for j in range(2):
        for h in range(2):
            multiply(h, j)
    for j in range(n):
        for h in range(2):
            near(h, j)
        if j + 2 < n:
            for h in range(2):
                multiply(h, j + 2)
        if j == 1:
            for h in range(2):
                finish(h, 0)
                for k in range(2):
                    send(
                        h,
                        n,
                        k,
                        AXES[h][0],
                        part.at[h, 0, :, pl.ds(k * quarter, quarter)],
                        r_opp2.at[h, k],
                    )
    for j in (1, 2):
        for h in range(2):
            finish(h, j)
            k = j - 1
            arrived(h, n, k, AXES[h][0], r_opp2.at[h, k])
            add_to(part.at[h, j], k, r_opp2.at[h, k])
            send(h, n, 2 + k, AXES[h][0], part.at[h, j], r_full2.at[h, k])
    for h in range(2):
        both(h, 3)
        for k in range(2):
            arrived(h, n, 2 + k, AXES[h][0], r_full2.at[h, k])
        settle(
            h,
            [
                t[h].at[3, place[AXES[h][1]]],
                r_full.at[h, 3, 0],
                r_full.at[h, 3, 1],
                r_full2.at[h, 0],
                r_full2.at[h, 1],
            ],
        )

        @pl.loop(1, experts)
        def _(d):
            for k in (h,) if h == 0 else (1, 2):
                give(k, d, lax.rem(mine_e + d, experts), mine_e).start()

    back_main[mine_e] = out_main[mine_e]
    back_last[mine_e] = out_last[mine_e]

    @pl.loop(1, experts)
    def _(d):
        for k in range(3):
            give(
                k, d, lax.rem(mine_e + d, experts), lax.rem(mine_e - d + experts, experts)
            ).wait()

    for c in sent:
        c.wait_send()


def expert_terms(main_rows, last_rows, w_gate, w_up):
    n = 4
    experts, main, width = main_rows.shape
    count = experts * (main + 1)
    hidden = w_gate.shape[0]
    half = width // 2
    any_spec = pl.BlockSpec(memory_space=pl.ANY)
    vmem = pl.BlockSpec(memory_space=pltpu.VMEM)
    bf16 = jnp.bfloat16
    return pl.pallas_call(
        gather_kernel,
        out_shape=[
            jax.ShapeDtypeStruct((n, n, count, hidden), jnp.float32),
            jax.ShapeDtypeStruct((n, n * count, half), bf16),
            jax.ShapeDtypeStruct((n, n * count, half), bf16),
            jax.ShapeDtypeStruct((count, width), bf16),
        ],
        in_specs=[any_spec] * 4,
        out_specs=[vmem, any_spec, any_spec, any_spec],
        scratch_shapes=[
            pltpu.VMEM((hidden, width), bf16),
            pltpu.VMEM((hidden, width), bf16),
            pltpu.VMEM((2, n * count, half), bf16),
            pltpu.VMEM((n, n, count, hidden), jnp.float32),
            pltpu.VMEM((n, n, count, hidden), jnp.float32),
            pltpu.VMEM((experts, 1, width), jnp.float32),
            pltpu.VMEM((experts, width), bf16),
            pltpu.SemaphoreType.DMA((2, n + 1, 4)),
            pltpu.SemaphoreType.DMA((2, n + 1, 4)),
            pltpu.SemaphoreType.DMA((8,)),
            pltpu.SemaphoreType.DMA((2, experts)),
            pltpu.SemaphoreType.DMA((2, experts)),
        ],
        compiler_params=pltpu.CompilerParams(
            collective_id=1, has_side_effects=True, vmem_limit_bytes=60 << 20
        ),
        name="gather_experts",
    )(main_rows, last_rows, w_gate, w_up)[0]


def expert_sum(hid, w_down, experts):
    n = 4
    hidden, width = w_down.shape
    count = hid.shape[2]
    main = count // experts - 1
    half = width // 2
    any_spec = pl.BlockSpec(memory_space=pl.ANY)
    vmem = pl.BlockSpec(memory_space=pltpu.VMEM)
    bf16 = jnp.bfloat16
    return pl.pallas_call(
        reduce_kernel,
        out_shape=[
            jax.ShapeDtypeStruct((experts, main, width), bf16),
            jax.ShapeDtypeStruct((experts, 1, width), jnp.float32),
        ],
        in_specs=[vmem, any_spec],
        out_specs=[vmem, vmem],
        scratch_shapes=[
            pltpu.VMEM((hidden, width), bf16),
            pltpu.VMEM((n * count, hidden), bf16),
            pltpu.VMEM((n, n, count, half), bf16),
            pltpu.VMEM((n, n, count, half), bf16),
            pltpu.VMEM((2, n, 2, count, half // 2), bf16),
            pltpu.VMEM((2, n, 2, count, half), bf16),
            pltpu.VMEM((2, 3, count, half), bf16),
            pltpu.VMEM((2, 2, count, half // 2), bf16),
            pltpu.VMEM((2, 2, count, half), bf16),
            pltpu.VMEM((experts, main, width), bf16),
            pltpu.VMEM((experts, 1, width), jnp.float32),
            pltpu.SemaphoreType.DMA((2, n + 1, 4)),
            pltpu.SemaphoreType.DMA((2, n + 1, 4)),
            pltpu.SemaphoreType.DMA((1,)),
            pltpu.SemaphoreType.DMA((3, experts)),
            pltpu.SemaphoreType.DMA((3, experts)),
        ],
        compiler_params=pltpu.CompilerParams(
            collective_id=2, has_side_effects=True, vmem_limit_bytes=60 << 20
        ),
        name="sum_experts",
    )(hid, w_down)


def state_kernel(
    chunks, fades, weight, out_ref, w_left, w_right, got, got_fade, held, ssem, rsem, wsend, wrecv
):
    n = chunks.shape[0]
    side = 4
    per = chunks.shape[1]
    heads = fades.shape[0]
    me = lax.axis_index("y") * side + lax.axis_index("x")

    def where(t):
        return {"y": t // side, "x": lax.rem(t, side)}

    def copy(kind, d, src, dst, t):
        return pltpu.make_async_remote_copy(
            src_ref=src,
            dst_ref=dst,
            send_sem=ssem.at[kind, d],
            recv_sem=rsem.at[kind, d],
            device_id=where(t),
            device_id_type=MESH,
        )

    def fade_of(t):
        return fades.at[pl.ds(lax.rem(t * per, heads), per)]

    barrier = pltpu.get_barrier_semaphore()

    @pl.loop(1, n)
    def _(d):
        pl.semaphore_signal(
            barrier, inc=1, device_id=where(lax.rem(me + d, n)), device_id_type=MESH
        )

    pl.semaphore_wait(barrier, n - 1)

    @pl.loop(1, n)
    def _(d):
        t = lax.rem(me + d, n)
        copy(0, d, chunks.at[t], got.at[me], t).start()
        copy(1, d, fade_of(t), got_fade.at[me], t).start()

    y = lax.axis_index("y")
    moves = [
        pltpu.make_async_remote_copy(
            src_ref=weight,
            dst_ref=dst,
            send_sem=wsend.at[k],
            recv_sem=wrecv.at[k],
            device_id={"y": lax.rem(y + by, side)},
            device_id_type=MESH,
        )
        for k, (dst, by) in enumerate(((w_left, 1), (w_right, side - 1)))
    ]
    for m in moves:
        m.start()
    got[me] = chunks[me]
    got_fade[me] = fade_of(me)[...]

    @pl.loop(1, n)
    def _(d):
        t = lax.rem(me + d, n)
        frm = lax.rem(me - d + n, n)
        copy(0, d, chunks.at[t], got.at[frm], t).wait()
        copy(1, d, fade_of(t), got_fade.at[frm], t).wait()

    def advance(b, state):
        held[b] = state.astype(jnp.bfloat16)
        d = lax.rem(b - me + n, n)

        @pl.when(d != 0)
        def _():
            copy(2, d, held.at[b], out_ref.at[me], b).start()

        return got_fade[b][:, :1, :] * state + got[b].astype(jnp.float32)

    lax.fori_loop(0, n, advance, jnp.zeros(got.shape[1:], jnp.float32))
    out_ref[me] = held[me]

    @pl.loop(1, n)
    def _(d):
        t = lax.rem(me + d, n)
        frm = lax.rem(me - d + n, n)
        copy(2, d, held.at[t], out_ref.at[frm], t).wait()

    for m in moves:
        m.wait()


def incoming_states(local_state, block_end, out_weight):
    seqs, heads, width, _ = local_state.shape
    n = lax.axis_size(CTX)
    per = seqs * heads // n
    chunks = local_state.reshape(n, per, width, width).astype(jnp.bfloat16)
    fades = jnp.broadcast_to(jnp.exp(block_end)[:, None, None], (heads, 8, width))
    vmem = pl.BlockSpec(memory_space=pltpu.VMEM)
    any_spec = pl.BlockSpec(memory_space=pl.ANY)
    beside = jax.ShapeDtypeStruct(out_weight.shape, out_weight.dtype)
    out, w_left, w_right = pl.pallas_call(
        state_kernel,
        out_shape=[jax.ShapeDtypeStruct(chunks.shape, jnp.bfloat16), beside, beside],
        in_specs=[vmem, vmem, any_spec],
        out_specs=[vmem, any_spec, any_spec],
        scratch_shapes=[
            pltpu.VMEM(chunks.shape, jnp.bfloat16),
            pltpu.VMEM((n, per, 8, width), jnp.float32),
            pltpu.VMEM(chunks.shape, jnp.bfloat16),
            pltpu.SemaphoreType.DMA((3, n)),
            pltpu.SemaphoreType.DMA((3, n)),
            pltpu.SemaphoreType.DMA((2,)),
            pltpu.SemaphoreType.DMA((2,)),
        ],
        compiler_params=pltpu.CompilerParams(
            collective_id=3, has_side_effects=True, vmem_limit_bytes=32 << 20
        ),
        name="carry_states",
    )(chunks, fades, out_weight)
    return out.reshape(local_state.shape), w_left, w_right


def project_kernel(
    tok_ref, w_own, w_left, w_right, out_ref, w, tok, prod, other, ring_opp, ring_full, done, ssem, rsem, lsem, wsend, wrecv
):
    n = 4
    cores, zs, count, width = prod.shape[1:]
    feats = tok_ref.shape[1]
    half_f = feats // 2
    half = width // 2
    block = width // n
    half_w = feats // 2
    x = lax.axis_index("x")
    y = lax.axis_index("y")
    z = lax.axis_index("z")
    c = lax.axis_index("c")

    def xs(by):
        return lax.rem(x + (by + n), n)

    def zz(by):
        return lax.rem(z + (by + n), n)

    def yy(by):
        return lax.rem(y + (by + n), n)

    loads = [
        pltpu.make_async_copy(src, w.at[yy(by)], lsem.at[k])
        for k, (src, by) in enumerate(((w_own, 0), (w_left, -1), (w_right, 1)))
    ]
    for load in loads:
        load.start()
    greet(
        [{"x": xs(1)}, {"x": xs(-1)}, {"x": xs(2)}, {"z": zz(1)}, {"z": zz(-1)}, {"c": 1 - c}]
        + [{"y": yy(1)}, {"y": yy(-1)}]
    )
    sent = []

    def copy(j, kind, src, dst, axis, to):
        return pltpu.make_async_remote_copy(
            src_ref=src,
            dst_ref=dst,
            send_sem=ssem.at[j, kind],
            recv_sem=rsem.at[j, kind],
            device_id={axis: to},
            device_id_type=MESH,
        )

    def send(*a):
        cp = copy(*a)
        cp.start()
        sent.append(cp)

    def arrived(j, kind, dst, axis):
        copy(j, kind, dst, dst, axis, xs(1) if axis == "x" else zz(1) if axis == "z" else 1 - c).wait_recv()

    shift = (0, -1, 1, 2)
    send(0, 0, tok_ref, tok.at[0], "x", xs(1))
    send(0, 1, tok_ref, tok.at[1], "x", xs(-1))

    def far_weight(k, by, frm):
        src = (w_left, w_right)[k]
        rows = pl.ds(k * half_w, half_w)
        return pltpu.make_async_remote_copy(
            src_ref=src.at[rows],
            dst_ref=w.at[frm, rows],
            send_sem=wsend.at[k],
            recv_sem=wrecv.at[k],
            device_id={"y": yy(by)},
            device_id_type=MESH,
        )

    for k, by in ((0, 1), (1, -1)):
        far_weight(k, by, yy(-by)).start()
    for load in loads:
        load.wait()

    def dot_part(j, g):
        src = tok_ref if j == 0 else tok.at[j - 1]
        cols = pl.ds(pl.multiple_of(g * block, 128), block)
        got = jnp.dot(src[...], w[g], preferred_element_type=jnp.float32)
        prod[j, :, :, :, cols] = got.reshape(cores, zs, count, block).astype(jnp.bfloat16)

    def dot(j):
        if j == 0:

            @pl.loop(0, n - 1)
            def _(i):
                dot_part(0, yy(i + i // 2))

        elif j == 1:
            for k, by in ((0, 1), (1, -1)):
                far_weight(k, by, yy(2)).wait()
            dot_part(0, yy(2))
            exchange(0)
        if j > 0:

            @pl.loop(0, n)
            def _(i):
                dot_part(j, i)

            exchange(j)

    def exchange(j):
        send(j, 2, prod.at[j, 1 - c], other.at[j], "c", 1 - c)

    def core_add(j):
        arrived(j, 2, other.at[j], "c")
        mine = prod.at[j, c]

        @pl.loop(0, width // block)
        def _(b):
            cols = pl.ds(pl.multiple_of(b * block, 128), block)
            mine[:, :, cols] = (
                mine[:, :, cols].astype(jnp.float32) + other[j, :, :, cols].astype(jnp.float32)
            ).astype(jnp.bfloat16)

        for k in range(2):
            send(
                j,
                3 + k,
                mine.at[zz(2), :, pl.ds(k * half, half)],
                ring_opp.at[j, k],
                "z",
                zz(1 if k == 0 else -1),
            )

    def near(j):
        for k in range(2):
            arrived(j, 3 + k, ring_opp.at[j, k], "z")
            to = zz(1 if k == 0 else -1)
            mine = prod.at[j, c, to]
            cols = pl.ds(k * half, half)
            mine[:, cols] = (
                mine[:, cols].astype(jnp.float32) + ring_opp[j, k].astype(jnp.float32)
            ).astype(jnp.bfloat16)
            send(j, 5 + k, mine, ring_full.at[j, k], "z", to)

    def finish(j):
        for k in range(2):
            arrived(j, 5 + k, ring_full.at[j, k], "z")
        s = (
            prod[j, c, z].astype(jnp.float32)
            + ring_full[j, 0].astype(jnp.float32)
            + ring_full[j, 1].astype(jnp.float32)
        ).astype(jnp.bfloat16)
        if j == 0:
            out_ref[x] = s
        else:
            done[j] = s
            send(j, 7, done.at[j], out_ref.at[x], "x", xs(shift[j]))

    dot(0)
    for k in range(2):
        arrived(0, k, tok.at[k], "x")
        cols = pl.ds(k * half_f, half_f)
        send(1, k, tok.at[k, :, cols], tok.at[2, :, cols], "x", xs(1 if k == 0 else -1))
    dot(1)
    core_add(0)
    dot(2)
    core_add(1)
    near(0)
    for k in range(2):
        arrived(1, k, tok.at[2, :, pl.ds(k * half_f, half_f)], "x")
    dot(3)
    core_add(2)
    near(1)
    core_add(3)
    finish(0)
    near(2)
    finish(1)
    near(3)
    finish(2)
    finish(3)
    for j in (1, 2, 3):
        arrived(j, 7, out_ref.at[xs(-shift[j])], "x")
    for cp in sent:
        cp.wait_send()


def project(tokens, weight, w_left, w_right):
    n = 4
    rows, feats = tokens.shape
    width = weight.shape[1] * n
    cores, zs = lax.axis_size("c"), lax.axis_size("z")
    count = rows // (cores * zs)
    bf16 = jnp.bfloat16
    vmem = pl.BlockSpec(memory_space=pltpu.VMEM)
    return pl.pallas_call(
        project_kernel,
        out_shape=jax.ShapeDtypeStruct((n, count, width), bf16),
        in_specs=[vmem] + [pl.BlockSpec(memory_space=pl.ANY)] * 3,
        out_specs=vmem,
        scratch_shapes=[
            pltpu.VMEM((n, feats, width // n), bf16),
            pltpu.VMEM((3, rows, feats), bf16),
            pltpu.VMEM((n, cores, zs, count, width), bf16),
            pltpu.VMEM((n, zs, count, width), bf16),
            pltpu.VMEM((n, 2, count, width // 2), bf16),
            pltpu.VMEM((n, 2, count, width), bf16),
            pltpu.VMEM((n, count, width), bf16),
            pltpu.SemaphoreType.DMA((n, 8)),
            pltpu.SemaphoreType.DMA((n, 8)),
            pltpu.SemaphoreType.DMA((3,)),
            pltpu.SemaphoreType.DMA((2,)),
            pltpu.SemaphoreType.DMA((2,)),
        ],
        compiler_params=pltpu.CompilerParams(
            collective_id=4, has_side_effects=True, vmem_limit_bytes=48 << 20
        ),
        name="project",
    )(tokens, weight, w_left, w_right)


def body(
    queries,
    keys,
    values,
    decay_log,
    out_gate,
    head_gain,
    out_weight,
    stream,
    norm_gain,
    expert_ids,
    expert_share,
    w_gate,
    w_up,
    w_down,
):
    seq_count, block_len, head_width = queries.shape
    head_count = decay_log.shape[1]
    head_dim = head_width // head_count
    split_shape = (seq_count, block_len, head_count, head_dim)
    query_heads = queries.reshape(split_shape)
    key_heads = keys.reshape(split_shape)
    value_heads = values.reshape(split_shape)
    position = jnp.arange(block_len)
    causal = position[:, None] >= position[None, :]
    cumulative = jnp.sum(jnp.where(causal[:, :, None], decay_log[None], 0.0), axis=1)
    gap_log = cumulative[:, None, :] - cumulative[None, :, :]
    decay_grid = jnp.exp(jnp.where(causal[:, :, None], gap_log, -1e30))
    block_end = cumulative[-1]
    keys_faded = jnp.exp(block_end[None, :] - cumulative)[None, :, :, None] * key_heads.astype(
        jnp.float32
    )
    local_state = jnp.einsum(
        "sjhd,sjhe->shde",
        keys_faded,
        value_heads.astype(jnp.float32),
        precision=lax.Precision.HIGHEST,
    )
    incoming, w_left, w_right = incoming_states(local_state, block_end, out_weight)
    scores = jnp.einsum(
        "sihd,sjhd->sijh", query_heads, key_heads, preferred_element_type=jnp.float32
    )
    weights = (scores * decay_grid[None]).astype(jnp.bfloat16)
    within = jnp.einsum("sijh,sjhd->sihd", weights, value_heads, preferred_element_type=jnp.float32)
    carried = jnp.exp(cumulative)[None, :, :, None] * jnp.einsum(
        "sihd,shde->sihe", query_heads, incoming, preferred_element_type=jnp.float32
    )
    attended = within + carried
    mean_square = jnp.mean(attended * attended, axis=-1, keepdims=True)
    gate_act = jax.nn.sigmoid(out_gate.reshape(split_shape).astype(jnp.float32))
    gated = (
        attended
        * lax.rsqrt(mean_square + 1e-06)
        * head_gain.reshape(head_count, head_dim)
        * gate_act
    )
    mixed = gated.astype(jnp.bfloat16).reshape(seq_count, block_len, head_width)
    sub_len = stream.shape[1]
    model_width = stream.shape[2]
    exp_count = lax.axis_size(EXP)
    x_count = lax.axis_size("x")
    y_count = lax.axis_size("y")
    ctx_count = x_count * y_count
    tok_count = seq_count * sub_len
    ordered = (
        mixed.reshape(seq_count, exp_count // 2, 2, sub_len, head_width)
        .transpose(2, 1, 0, 3, 4)
        .reshape(exp_count * tok_count, head_width)
    )
    projected = project(ordered, out_weight, w_left, w_right)
    part_width = out_weight.shape[1] * y_count
    projected = (
        projected.reshape(x_count, tok_count, y_count, part_width // y_count)
        .transpose(1, 2, 0, 3)
        .reshape(tok_count, model_width)
        .astype(jnp.float32)
    )
    residual_sum = stream.reshape(tok_count, model_width).astype(jnp.float32) + projected
    stream_square = jnp.mean(residual_sum * residual_sum, axis=-1, keepdims=True)
    normed = (residual_sum * lax.rsqrt(stream_square + 1e-06) * norm_gain).astype(jnp.bfloat16)
    expert_count = exp_count
    capacity = max(2, (2 * tok_count + expert_count - 1) // expert_count + 1)
    slot_total = expert_count * capacity
    picks = expert_ids.reshape(2 * tok_count)
    copy_no = jnp.arange(2 * tok_count)
    earlier = (copy_no[None, :] < copy_no[:, None]) & (picks[None, :] == picks[:, None])
    ranking = jnp.sum(earlier.astype(jnp.int32), axis=1)
    main = capacity - 1
    slot_of = jnp.where(ranking < main, picks * main + ranking, expert_count * main + picks)
    placing = slot_of[:, None] == jnp.arange(slot_total, dtype=jnp.int32)[None, :]
    token_placing = jnp.any(placing.reshape(tok_count, 2, slot_total), axis=1)
    to_slots = token_placing.T.astype(jnp.bfloat16)
    main_total = expert_count * main
    main_rows = jnp.dot(
        to_slots[:main_total], normed, preferred_element_type=jnp.float32
    ).astype(jnp.bfloat16)
    last_rows = jnp.dot(to_slots[main_total:], normed, preferred_element_type=jnp.float32)
    hid = expert_terms(
        main_rows.reshape(expert_count, main, model_width),
        last_rows.reshape(expert_count, 1, model_width),
        w_gate[0].T,
        w_up[0].T,
    )
    back_main, back_last = expert_sum(hid, w_down[0], expert_count)
    returned = jnp.concatenate(
        [
            back_main.reshape(main_total, model_width).astype(jnp.float32),
            back_last.reshape(expert_count, model_width),
        ],
        axis=0,
    )
    weighting = jnp.where(placing, expert_share.reshape(2 * tok_count, 1), 0.0)
    weighting = jnp.sum(weighting.reshape(tok_count, 2, slot_total), axis=1)
    expert_mix = jnp.dot(weighting, returned, precision=lax.Precision.HIGHEST)
    result = (residual_sum + expert_mix).astype(jnp.bfloat16)
    return result.reshape(seq_count, sub_len, model_width)


def solution(mesh):
    n_exp = mesh.shape["exp"]
    side = round(mesh.shape["ctx"] ** 0.5)
    fine = Mesh(mesh.devices.reshape(side, side, n_exp // 2, 2), ("y", "x", "z", "c"))
    return jax.shard_map(
        body,
        mesh=fine,
        in_specs=(
            P(None, CTX, EXP),
            P(None, CTX, EXP),
            P(None, CTX, EXP),
            P(CTX, EXP),
            P(None, CTX, EXP),
            P(EXP),
            P(EXP, CTX),
            P(None, CTX + EXP, None),
            P(),
            P(CTX + EXP, None, None),
            P(CTX + EXP, None, None),
            P(EXP, None, CTX),
            P(EXP, None, CTX),
            P(EXP, CTX, None),
        ),
        out_specs=P(None, CTX + EXP, None),
        check_vma=False,
    )
```

```python
import jax
import jax.numpy as jnp
from jax import lax
from jax.experimental import pallas as pl
from jax.experimental.pallas import tpu as pltpu
from jax.sharding import Mesh, PartitionSpec as P

CTX = ("y", "x")
EXP = ("z", "c")


MESH = pl.DeviceIdType.MESH
AXES = (("x", "y"), ("y", "x"))


def greet(others):
    barrier = pltpu.get_barrier_semaphore()
    for where in others:
        pl.semaphore_signal(barrier, inc=1, device_id=where, device_id_type=MESH)
    pl.semaphore_wait(barrier, len(others))


def expert_place(t):
    return {"z": t // 2, "c": lax.rem(t, 2)}


def gather_kernel(
    main_ref,
    last_ref,
    wg_hbm,
    wu_hbm,
    hid_ref,
    buf_a,
    buf_b,
    rows_ref,
    wg,
    wu,
    xin,
    acc_g,
    acc_u,
    last_in,
    last_out,
    ssem,
    rsem,
    lsem,
    esend,
    erecv,
):
    n = 4
    experts, main, _ = main_ref.shape
    mine_e = lax.axis_index("z") * 2 + lax.axis_index("c")
    count, width = rows_ref.shape
    half = width // 2
    quarter = half // 2
    hidden = wg.shape[0]
    buf = (buf_a, buf_b)
    place = {a: lax.axis_index(a) for a in ("x", "y")}

    def step(axis, by):
        return lax.rem(place[axis] + (by + n), n)

    load_g = pltpu.make_async_copy(wg_hbm, wg, lsem.at[0])
    load_u = pltpu.make_async_copy(wu_hbm, wu, lsem.at[1])
    load_g.start()
    load_u.start()
    greet(
        [{a: step(a, d)} for a in ("x", "y") for d in (1, -1)]
        + [expert_place(lax.rem(mine_e + d, experts)) for d in range(1, experts)]
    )

    def main_rows(e):
        return rows_ref.at[pl.ds(pl.multiple_of(e * main, 8), main)]

    def deal(d, to, frm):
        return [
            pltpu.make_async_remote_copy(
                src_ref=src,
                dst_ref=dst,
                send_sem=esend.at[k, d],
                recv_sem=erecv.at[k, d],
                device_id=expert_place(to),
                device_id_type=MESH,
            )
            for k, (src, dst) in enumerate(
                ((main_ref.at[to], main_rows(frm)), (last_ref.at[to], last_in.at[frm]))
            )
        ]

    @pl.loop(1, experts)
    def _(d):
        for c in deal(d, lax.rem(mine_e + d, experts), mine_e):
            c.start()

    own_main = pltpu.make_async_copy(main_ref.at[mine_e], main_rows(mine_e), lsem.at[6])
    own_last = pltpu.make_async_copy(last_ref.at[mine_e], last_in.at[mine_e], lsem.at[7])
    own_main.start()
    own_last.start()
    acc_g[...] = jnp.zeros_like(acc_g)
    acc_u[...] = jnp.zeros_like(acc_u)
    own_main.wait()
    own_last.wait()

    @pl.loop(1, experts)
    def _(d):
        for c in deal(d, lax.rem(mine_e + d, experts), lax.rem(mine_e - d + experts, experts)):
            c.wait()

    last_out[...] = last_in[...].reshape(last_out.shape).astype(jnp.bfloat16)
    put_last = pltpu.make_async_copy(
        last_out, rows_ref.at[pl.ds(experts * main, experts)], lsem.at[6]
    )
    put_last.start()
    put_last.wait()

    def row(h, fi, si):
        return buf[h].at[fi, pl.ds(pl.multiple_of(si * count, 8), count)]

    def cut(ref, k):
        return ref.at[:, pl.ds((k - 2) * quarter, quarter)] if k >= 2 else ref

    def send(h, stage, kind, axis, src, dst):
        to = step(axis, 1 if kind % 2 == 0 else -1)
        c = pltpu.make_async_remote_copy(
            src_ref=cut(src, kind),
            dst_ref=cut(dst, kind),
            send_sem=ssem.at[h, stage, kind],
            recv_sem=rsem.at[h, stage, kind],
            device_id={axis: to},
            device_id_type=MESH,
        )
        c.start()
        sent.append(c)

    def arrived(h, stage, kind, axis, dst):
        pltpu.make_async_remote_copy(
            src_ref=cut(dst, kind),
            dst_ref=cut(dst, kind),
            send_sem=ssem.at[h, stage, kind],
            recv_sem=rsem.at[h, stage, kind],
            device_id={axis: step(axis, 1)},
            device_id_type=MESH,
        ).wait_recv()

    sent = []
    shift = (0, -1, 1, 2)
    own = [rows_ref.at[:, pl.ds(h * half, half)] for h in range(2)]
    keep = []
    for h in range(2):
        first, second = AXES[h]
        mine = row(h, place[first], place[second])
        for kind in range(2):
            send(h, n, kind, first, own[h], mine)
    for h in range(2):
        first, second = AXES[h]
        mine = row(h, place[first], place[second])
        for kind in range(2):
            send(h, 0, kind, second, own[h], mine)
        keep.append(pltpu.make_async_copy(own[h], mine, lsem.at[2 + h]))
        keep[h].start()

    def spread(h, j):
        first, second = AXES[h]
        here = row(h, step(first, shift[j]), place[second])
        for kind in range(2):
            send(h, j, kind, second, here, here)

    def pass_on(h, stage, kind):
        first, second = AXES[h]
        by = -1 if kind == 0 else 1
        if stage == n:
            here = row(h, step(first, by), place[second])
            axis = first
        else:
            here = row(h, step(first, shift[stage]), step(second, by))
            axis = second
        arrived(h, stage, kind, axis, here)
        send(h, stage, kind + 2, axis, here, here)

    def far(h, stage):
        first, second = AXES[h]
        if stage == n:
            here, axis = row(h, step(first, 2), place[second]), first
        else:
            here, axis = row(h, step(first, shift[stage]), step(second, 2)), second
        for kind in (2, 3):
            arrived(h, stage, kind, axis, here)

    def load(h, j):
        return pltpu.make_async_copy(
            buf[h].at[step(AXES[h][0], shift[j])], xin.at[h], lsem.at[4 + h]
        )

    def multiply(h, j):
        load(h, j).wait()
        fi = step(AXES[h][0], shift[j])
        for w, acc in ((wg, acc_g), (wu, acc_u)):
            got = lax.dot_general(
                xin[h],
                w[:, pl.ds(h * half, half)],
                (((1,), (1,)), ((), ())),
                preferred_element_type=jnp.float32,
            ).reshape(n, count, hidden)
            if h == 0:
                acc[fi] += got
            else:
                acc[:, fi] += got

    def activate(p, q):
        g = acc_g[p, q]
        out = (g / (1.0 + jnp.exp(-g)) * acc_u[p, q]).astype(jnp.bfloat16)
        hid_ref[p, q] = out.astype(jnp.float32)

    for kind in range(2):
        for h in range(2):
            pass_on(h, n, kind)
            spread(h, 1 + kind)
    for kind in range(2):
        for h in range(2):
            pass_on(h, 0, kind)
    for h in range(2):
        far(h, n)
        spread(h, 3)
    load_g.wait()
    load_u.wait()
    for j in range(n):
        if j + 1 < n:
            for kind in range(2):
                for h in range(2):
                    pass_on(h, j + 1, kind)
        for h in range(2):
            if j == 0:
                keep[h].wait()
            far(h, j)
            load(h, j).start()
        for h in range(2):
            multiply(h, j)
        if j == 2:

            @pl.loop(0, 9)
            def _(k):
                a, b = k // 3, lax.rem(k, 3)
                activate(step("x", a + a // 2), step("y", b + b // 2))

    @pl.loop(0, n)
    def _(k):
        activate(step("x", 2), step("y", k))

    @pl.loop(0, n - 1)
    def _(k):
        activate(step("x", k + k // 2), step("y", 2))

    for c in sent:
        c.wait_send()


def reduce_kernel(
    hid_ref,
    wd_hbm,
    back_main,
    back_last,
    wd,
    rows,
    t_a,
    t_b,
    r_opp,
    r_full,
    part,
    r_opp2,
    r_full2,
    out_main,
    out_last,
    ssem,
    rsem,
    lsem,
    esend,
    erecv,
):
    n = 4
    experts, main, width = out_main.shape
    count = experts * (main + 1)
    mine_e = lax.axis_index("z") * 2 + lax.axis_index("c")
    half = width // 2
    quarter = half // 2
    block = min(512, quarter)
    t = (t_a, t_b)
    place = {a: lax.axis_index(a) for a in ("x", "y")}

    def step(axis, by):
        return lax.rem(place[axis] + (by + n), n)

    load = pltpu.make_async_copy(wd_hbm, wd, lsem.at[0])
    load.start()
    greet(
        [{a: step(a, d)} for a in ("x", "y") for d in (1, -1)]
        + [expert_place(lax.rem(mine_e + d, experts)) for d in range(1, experts)]
    )
    load.wait()
    shift = (2, 1, -1, 0)
    sent = []

    def copy(h, stage, kind, axis, src, dst):
        return pltpu.make_async_remote_copy(
            src_ref=src,
            dst_ref=dst,
            send_sem=ssem.at[h, stage, kind],
            recv_sem=rsem.at[h, stage, kind],
            device_id={axis: step(axis, 1 if kind % 2 == 0 else -1)},
            device_id_type=MESH,
        )

    def send(*a):
        c = copy(*a)
        c.start()
        sent.append(c)

    def arrived(h, stage, kind, axis, dst):
        copy(h, stage, kind, axis, dst, dst).wait_recv()

    def multiply(h, j):
        lead = step(AXES[h][0], shift[j])
        taken = hid_ref[lead] if h == 0 else hid_ref[:, pl.ds(lead, 1)]
        rows[...] = taken.reshape(rows.shape).astype(jnp.bfloat16)

        @pl.loop(0, half // block)
        def _(b):
            at = pl.multiple_of(b * block, 128)
            got = jnp.dot(
                rows[...],
                wd[:, pl.ds(pl.multiple_of(h * half + at, 128), block)],
                preferred_element_type=jnp.float32,
            )
            t[h][j, :, :, pl.ds(at, block)] = got.reshape(n, count, block).astype(jnp.bfloat16)

        ring = AXES[h][1]
        for k in range(2):
            send(
                h,
                j,
                k,
                ring,
                t[h].at[j, step(ring, 2), :, pl.ds(k * quarter, quarter)],
                r_opp.at[h, j, k],
            )

    def add_to(ref, k, other):
        @pl.loop(0, quarter // block)
        def _(b):
            at = pl.multiple_of(b * block, 128)
            cols = pl.ds(pl.multiple_of(k * quarter + at, 128), block)
            ref[:, cols] = (
                ref[:, cols].astype(jnp.float32) + other[:, pl.ds(at, block)].astype(jnp.float32)
            ).astype(jnp.bfloat16)

    def add_up(refs, at):
        s = refs[0][:, pl.ds(at, block)].astype(jnp.float32)
        for r in refs[1:]:
            s = s + r[:, pl.ds(at, block)].astype(jnp.float32)
        return s

    def total(dst, refs):
        @pl.loop(0, half // block)
        def _(b):
            at = pl.multiple_of(b * block, 128)
            dst[:, pl.ds(at, block)] = add_up(refs, at).astype(jnp.bfloat16)

    def settle(h, refs):
        @pl.loop(0, half // block)
        def _(b):
            at = pl.multiple_of(b * block, 128)
            cols = pl.ds(pl.multiple_of(h * half + at, 128), block)
            s = add_up(refs, at)
            out_main[:, :, cols] = (
                s[: experts * main].reshape(experts, main, block).astype(jnp.bfloat16)
            )
            out_last[:, :, cols] = s[experts * main :].reshape(experts, 1, block)

    def give(k, d, to, frm):
        if k == 2:
            src, dst = out_last.at[to], back_last.at[frm]
        else:
            cols = pl.ds(k * half, half)
            src, dst = out_main.at[to, :, cols], back_main.at[frm, :, cols]
        return pltpu.make_async_remote_copy(
            src_ref=src,
            dst_ref=dst,
            send_sem=esend.at[k, d],
            recv_sem=erecv.at[k, d],
            device_id=expert_place(to),
            device_id_type=MESH,
        )

    def near(h, j):
        ring = AXES[h][1]
        for k in range(2):
            arrived(h, j, k, ring, r_opp.at[h, j, k])
            mine = t[h].at[j, step(ring, 1 if k == 0 else -1)]
            add_to(mine, k, r_opp.at[h, j, k])
            send(h, j, 2 + k, ring, mine, r_full.at[h, j, k])

    def both(h, j):
        for k in range(2):
            arrived(h, j, 2 + k, AXES[h][1], r_full.at[h, j, k])

    def finish(h, j):
        both(h, j)
        total(
            part.at[h, j],
            [t[h].at[j, place[AXES[h][1]]], r_full.at[h, j, 0], r_full.at[h, j, 1]],
        )

    for j in range(2):
        for h in range(2):
            multiply(h, j)
    for j in range(n):
        for h in range(2):
            near(h, j)
        if j + 2 < n:
            for h in range(2):
                multiply(h, j + 2)
        if j == 1:
            for h in range(2):
                finish(h, 0)
                for k in range(2):
                    send(
                        h,
                        n,
                        k,
                        AXES[h][0],
                        part.at[h, 0, :, pl.ds(k * quarter, quarter)],
                        r_opp2.at[h, k],
                    )
    for j in (1, 2):
        for h in range(2):
            finish(h, j)
            k = j - 1
            arrived(h, n, k, AXES[h][0], r_opp2.at[h, k])
            add_to(part.at[h, j], k, r_opp2.at[h, k])
            send(h, n, 2 + k, AXES[h][0], part.at[h, j], r_full2.at[h, k])
    for h in range(2):
        both(h, 3)
        for k in range(2):
            arrived(h, n, 2 + k, AXES[h][0], r_full2.at[h, k])
        settle(
            h,
            [
                t[h].at[3, place[AXES[h][1]]],
                r_full.at[h, 3, 0],
                r_full.at[h, 3, 1],
                r_full2.at[h, 0],
                r_full2.at[h, 1],
            ],
        )

        @pl.loop(1, experts)
        def _(d):
            for k in (h,) if h == 0 else (1, 2):
                give(k, d, lax.rem(mine_e + d, experts), mine_e).start()

    back_main[mine_e] = out_main[mine_e]
    back_last[mine_e] = out_last[mine_e]

    @pl.loop(1, experts)
    def _(d):
        for k in range(3):
            give(
                k, d, lax.rem(mine_e + d, experts), lax.rem(mine_e - d + experts, experts)
            ).wait()

    for c in sent:
        c.wait_send()


def expert_terms(main_rows, last_rows, w_gate, w_up):
    n = 4
    experts, main, width = main_rows.shape
    count = experts * (main + 1)
    hidden = w_gate.shape[0]
    half = width // 2
    any_spec = pl.BlockSpec(memory_space=pl.ANY)
    vmem = pl.BlockSpec(memory_space=pltpu.VMEM)
    bf16 = jnp.bfloat16
    return pl.pallas_call(
        gather_kernel,
        out_shape=[
            jax.ShapeDtypeStruct((n, n, count, hidden), jnp.float32),
            jax.ShapeDtypeStruct((n, n * count, half), bf16),
            jax.ShapeDtypeStruct((n, n * count, half), bf16),
            jax.ShapeDtypeStruct((count, width), bf16),
        ],
        in_specs=[any_spec] * 4,
        out_specs=[vmem, any_spec, any_spec, any_spec],
        scratch_shapes=[
            pltpu.VMEM((hidden, width), bf16),
            pltpu.VMEM((hidden, width), bf16),
            pltpu.VMEM((2, n * count, half), bf16),
            pltpu.VMEM((n, n, count, hidden), jnp.float32),
            pltpu.VMEM((n, n, count, hidden), jnp.float32),
            pltpu.VMEM((experts, 1, width), jnp.float32),
            pltpu.VMEM((experts, width), bf16),
            pltpu.SemaphoreType.DMA((2, n + 1, 4)),
            pltpu.SemaphoreType.DMA((2, n + 1, 4)),
            pltpu.SemaphoreType.DMA((8,)),
            pltpu.SemaphoreType.DMA((2, experts)),
            pltpu.SemaphoreType.DMA((2, experts)),
        ],
        compiler_params=pltpu.CompilerParams(
            collective_id=1, has_side_effects=True, vmem_limit_bytes=60 << 20
        ),
        name="gather_experts",
    )(main_rows, last_rows, w_gate, w_up)[0]


def expert_sum(hid, w_down, experts):
    n = 4
    hidden, width = w_down.shape
    count = hid.shape[2]
    main = count // experts - 1
    half = width // 2
    any_spec = pl.BlockSpec(memory_space=pl.ANY)
    vmem = pl.BlockSpec(memory_space=pltpu.VMEM)
    bf16 = jnp.bfloat16
    return pl.pallas_call(
        reduce_kernel,
        out_shape=[
            jax.ShapeDtypeStruct((experts, main, width), bf16),
            jax.ShapeDtypeStruct((experts, 1, width), jnp.float32),
        ],
        in_specs=[vmem, any_spec],
        out_specs=[vmem, vmem],
        scratch_shapes=[
            pltpu.VMEM((hidden, width), bf16),
            pltpu.VMEM((n * count, hidden), bf16),
            pltpu.VMEM((n, n, count, half), bf16),
            pltpu.VMEM((n, n, count, half), bf16),
            pltpu.VMEM((2, n, 2, count, half // 2), bf16),
            pltpu.VMEM((2, n, 2, count, half), bf16),
            pltpu.VMEM((2, 3, count, half), bf16),
            pltpu.VMEM((2, 2, count, half // 2), bf16),
            pltpu.VMEM((2, 2, count, half), bf16),
            pltpu.VMEM((experts, main, width), bf16),
            pltpu.VMEM((experts, 1, width), jnp.float32),
            pltpu.SemaphoreType.DMA((2, n + 1, 4)),
            pltpu.SemaphoreType.DMA((2, n + 1, 4)),
            pltpu.SemaphoreType.DMA((1,)),
            pltpu.SemaphoreType.DMA((3, experts)),
            pltpu.SemaphoreType.DMA((3, experts)),
        ],
        compiler_params=pltpu.CompilerParams(
            collective_id=2, has_side_effects=True, vmem_limit_bytes=60 << 20
        ),
        name="sum_experts",
    )(hid, w_down)


def front_kernel(
    chunks,
    fades,
    q_ref,
    k_ref,
    v_ref,
    gate_ref,
    gain_ref,
    cum_ref,
    cum_t_ref,
    weight,
    out_ref,
    got,
    got_fade,
    held,
    incoming,
    decay,
    inner,
    scale,
    spread_tok,
    own_tok,
    tok,
    w,
    prod,
    other,
    ring_opp,
    ring_full,
    done,
    asend,
    arecv,
    wsend,
    wrecv,
    ssem,
    rsem,
    lsem,
):
    n = 4
    blocks, per, head_dim, _ = chunks.shape
    seqs, length, feats = q_ref.shape
    heads = fades.shape[0]
    cores, zs, count, width = prod.shape[1:]
    sub = length // (cores * zs)
    half_f = feats // 2
    half = width // 2
    block = width // n
    x = lax.axis_index("x")
    y = lax.axis_index("y")
    z = lax.axis_index("z")
    c = lax.axis_index("c")
    me = y * n + x

    def xs(by):
        return lax.rem(x + (by + n), n)

    def yy(by):
        return lax.rem(y + (by + n), n)

    def zz(by):
        return lax.rem(z + (by + n), n)

    def where(t):
        return {"y": t // n, "x": lax.rem(t, n)}

    load = pltpu.make_async_copy(weight, w.at[y], lsem.at[0])
    load.start()
    barrier = pltpu.get_barrier_semaphore()

    @pl.loop(1, blocks)
    def _(d):
        pl.semaphore_signal(
            barrier, inc=1, device_id=where(lax.rem(me + d, blocks)), device_id_type=MESH
        )

    for there in ({"z": zz(1)}, {"z": zz(-1)}, {"c": 1 - c}):
        pl.semaphore_signal(barrier, inc=1, device_id=there, device_id_type=MESH)
    pl.semaphore_wait(barrier, blocks + 2)

    def state_copy(kind, d, src, dst, t):
        return pltpu.make_async_remote_copy(
            src_ref=src,
            dst_ref=dst,
            send_sem=asend.at[kind, d],
            recv_sem=arecv.at[kind, d],
            device_id=where(t),
            device_id_type=MESH,
        )

    def fade_of(t):
        return fades.at[pl.ds(lax.rem(t * per, heads), per)]

    @pl.loop(1, blocks)
    def _(d):
        t = lax.rem(me + d, blocks)
        state_copy(0, d, chunks.at[t], got.at[me], t).start()
        state_copy(1, d, fade_of(t), got_fade.at[me], t).start()

    got[me] = chunks[me]
    got_fade[me] = fade_of(me)[...]

    row = lax.broadcasted_iota(jnp.int32, (length, length), 0)
    col = lax.broadcasted_iota(jnp.int32, (length, length), 1)
    for h in range(heads):
        gap = cum_ref[:, h : h + 1] - cum_t_ref[h : h + 1, :]
        decay[h] = jnp.exp(jnp.where(row >= col, gap, -1e30))

    @pl.loop(0, seqs)
    def _(s):
        g = gate_ref[s].astype(jnp.float32)
        scale[s] = gain_ref[...] / (1.0 + jnp.exp(-g))
        for h in range(heads):
            cols = pl.ds(h * head_dim, head_dim)
            scores = lax.dot_general(
                q_ref[s, :, cols],
                k_ref[s, :, cols],
                (((1,), (1,)), ((), ())),
                preferred_element_type=jnp.float32,
            )
            mix = (scores * decay[h]).astype(jnp.bfloat16)
            inner[s, :, cols] = jnp.dot(
                mix, v_ref[s, :, cols], preferred_element_type=jnp.float32
            )

    @pl.loop(1, blocks)
    def _(d):
        t = lax.rem(me + d, blocks)
        frm = lax.rem(me - d + blocks, blocks)
        state_copy(0, d, chunks.at[t], got.at[frm], t).wait()
        state_copy(1, d, fade_of(t), got_fade.at[frm], t).wait()

    def advance(b, state):
        held[b] = state.astype(jnp.bfloat16)
        d = lax.rem(b - me + blocks, blocks)

        @pl.when(d != 0)
        def _():
            state_copy(2, d, held.at[b], incoming.at[me], b).start()

        return got_fade[b][:, :1, :] * state + got[b].astype(jnp.float32)

    lax.fori_loop(0, blocks, advance, jnp.zeros(got.shape[1:], jnp.float32))
    incoming[me] = held[me]
    load.wait()
    rows_of = [pl.ds(k * half_f, half_f) for k in range(2)]

    def weight_copy(k, src, dst, by):
        return pltpu.make_async_remote_copy(
            src_ref=src,
            dst_ref=dst,
            send_sem=wsend.at[k],
            recv_sem=wrecv.at[k],
            device_id={"y": yy(by)},
            device_id_type=MESH,
        )

    sent = []
    for k, by in ((0, 1), (1, -1)):
        sent.append(weight_copy(k, weight, w.at[y], by))
        sent[-1].start()

    @pl.loop(1, blocks)
    def _(d):
        t = lax.rem(me + d, blocks)
        frm = lax.rem(me - d + blocks, blocks)
        state_copy(2, d, held.at[t], incoming.at[frm], t).wait()

    @pl.loop(0, seqs)
    def _(s):
        for h in range(heads):
            cols = pl.ds(h * head_dim, head_dim)
            pair = s * heads + h
            state = incoming[pair // per, lax.rem(pair, per)]
            carried = jnp.dot(q_ref[s, :, cols], state, preferred_element_type=jnp.float32)
            attended = inner[s, :, cols] + jnp.exp(cum_ref[:, h : h + 1]) * carried
            square = jnp.mean(attended * attended, axis=-1, keepdims=True)
            mixed = attended * lax.rsqrt(square + 1e-06) * scale[s, :, cols]
            parted = mixed.reshape(zs, cores, sub, head_dim)
            for k in range(cores):
                spread_tok[k, :, pl.ds(s, 1), :, cols] = parted[:, k : k + 1]

    own_tok[...] = spread_tok[...].reshape(own_tok.shape).astype(jnp.bfloat16)

    def copy(j, kind, src, dst, axis, to):
        return pltpu.make_async_remote_copy(
            src_ref=src,
            dst_ref=dst,
            send_sem=ssem.at[j, kind],
            recv_sem=rsem.at[j, kind],
            device_id={axis: to},
            device_id_type=MESH,
        )

    def send(*a):
        cp = copy(*a)
        cp.start()
        sent.append(cp)

    def arrived(j, kind, dst, axis):
        to = xs(1) if axis == "x" else zz(1) if axis == "z" else 1 - c
        copy(j, kind, dst, dst, axis, to).wait_recv()

    shift = (0, -1, 1, 2)
    send(0, 0, own_tok, tok.at[0], "x", xs(1))
    send(0, 1, own_tok, tok.at[1], "x", xs(-1))

    def dot_part(j, g):
        src = own_tok if j == 0 else tok.at[j - 1]
        cols = pl.ds(pl.multiple_of(g * block, 128), block)
        part = jnp.dot(src[...], w[g], preferred_element_type=jnp.float32)
        prod[j, :, :, :, cols] = part.reshape(cores, zs, count, block).astype(jnp.bfloat16)

    def near_groups(j):
        @pl.loop(0, n - 1)
        def _(i):
            dot_part(j, yy(i + i // 2))

    def exchange(j):
        send(j, 2, prod.at[j, 1 - c], other.at[j], "c", 1 - c)

    def core_add(j):
        arrived(j, 2, other.at[j], "c")
        mine = prod.at[j, c]

        @pl.loop(0, n)
        def _(b):
            cols = pl.ds(pl.multiple_of(b * block, 128), block)
            mine[:, :, cols] = (
                mine[:, :, cols].astype(jnp.float32) + other[j, :, :, cols].astype(jnp.float32)
            ).astype(jnp.bfloat16)

        for k in range(2):
            send(
                j,
                3 + k,
                mine.at[zz(2), :, pl.ds(k * half, half)],
                ring_opp.at[j, k],
                "z",
                zz(1 if k == 0 else -1),
            )

    def near(j):
        for k in range(2):
            arrived(j, 3 + k, ring_opp.at[j, k], "z")
            to = zz(1 if k == 0 else -1)
            mine = prod.at[j, c, to]
            cols = pl.ds(k * half, half)
            mine[:, cols] = (
                mine[:, cols].astype(jnp.float32) + ring_opp[j, k].astype(jnp.float32)
            ).astype(jnp.bfloat16)
            send(j, 5 + k, mine, ring_full.at[j, k], "z", to)

    def finish(j):
        for k in range(2):
            arrived(j, 5 + k, ring_full.at[j, k], "z")
        s = (
            prod[j, c, z].astype(jnp.float32)
            + ring_full[j, 0].astype(jnp.float32)
            + ring_full[j, 1].astype(jnp.float32)
        ).astype(jnp.bfloat16)
        if j == 0:
            out_ref[x] = s
        else:
            done[j] = s
            send(j, 7, done.at[j], out_ref.at[x], "x", xs(shift[j]))

    for k, by in ((0, 1), (1, -1)):
        weight_copy(k, weight, w.at[yy(-by)], by).wait_recv()
        part_w = w.at[yy(-by), rows_of[k]]
        sent.append(weight_copy(2 + k, part_w, part_w, by))
        sent[-1].start()
    near_groups(0)
    for k in range(2):
        arrived(0, k, tok.at[k], "x")
        cols = pl.ds(k * half_f, half_f)
        send(1, k, tok.at[k, :, cols], tok.at[2, :, cols], "x", xs(1 if k == 0 else -1))
    near_groups(1)
    for k, by in ((0, 1), (1, -1)):
        far_w = w.at[yy(2), rows_of[k]]
        weight_copy(2 + k, far_w, far_w, by).wait_recv()
    for j in range(2):
        dot_part(j, yy(2))
        exchange(j)
    near_groups(2)
    dot_part(2, yy(2))
    exchange(2)
    core_add(0)
    core_add(1)
    near(0)
    for k in range(2):
        arrived(1, k, tok.at[2, :, pl.ds(k * half_f, half_f)], "x")
    near_groups(3)
    dot_part(3, yy(2))
    exchange(3)
    core_add(2)
    near(1)
    core_add(3)
    finish(0)
    near(2)
    finish(1)
    near(3)
    finish(2)
    finish(3)
    for j in (1, 2, 3):
        arrived(j, 7, out_ref.at[xs(-shift[j])], "x")


    for cp in sent:
        cp.wait_send()


def front(local_state, cumulative, queries, keys, values, out_gate, head_gain, out_weight):
    n = 4
    seqs, heads, width, _ = local_state.shape
    blocks = n * n
    per = seqs * heads // blocks
    length, feats = queries.shape[1:]
    cores, zs = lax.axis_size("c"), lax.axis_size("z")
    count = seqs * length // (cores * zs)
    rows = seqs * length
    columns = out_weight.shape[1] * n
    bf16, f32 = jnp.bfloat16, jnp.float32
    chunks = local_state.reshape(blocks, per, width, width).astype(bf16)
    fades = jnp.broadcast_to(jnp.exp(cumulative[-1])[:, None, None], (heads, 8, width))
    vmem = pl.BlockSpec(memory_space=pltpu.VMEM)
    return pl.pallas_call(
        front_kernel,
        out_shape=jax.ShapeDtypeStruct((n, count, columns), bf16),
        in_specs=[vmem] * 9 + [pl.BlockSpec(memory_space=pl.ANY)],
        out_specs=vmem,
        scratch_shapes=[
            pltpu.VMEM(chunks.shape, bf16),
            pltpu.VMEM((blocks, per, 8, width), f32),
            pltpu.VMEM(chunks.shape, bf16),
            pltpu.VMEM(chunks.shape, bf16),
            pltpu.VMEM((heads, length, length), f32),
            pltpu.VMEM(queries.shape, f32),
            pltpu.VMEM(queries.shape, f32),
            pltpu.VMEM((cores, zs, seqs, length // (cores * zs), feats), f32),
            pltpu.VMEM((rows, feats), bf16),
            pltpu.VMEM((3, rows, feats), bf16),
            pltpu.VMEM((n, feats, columns // n), bf16),
            pltpu.VMEM((n, cores, zs, count, columns), bf16),
            pltpu.VMEM((n, zs, count, columns), bf16),
            pltpu.VMEM((n, 2, count, columns // 2), bf16),
            pltpu.VMEM((n, 2, count, columns), bf16),
            pltpu.VMEM((n, count, columns), bf16),
            pltpu.SemaphoreType.DMA((3, blocks)),
            pltpu.SemaphoreType.DMA((3, blocks)),
            pltpu.SemaphoreType.DMA((4,)),
            pltpu.SemaphoreType.DMA((4,)),
            pltpu.SemaphoreType.DMA((n, 8)),
            pltpu.SemaphoreType.DMA((n, 8)),
            pltpu.SemaphoreType.DMA((1,)),
        ],
        compiler_params=pltpu.CompilerParams(
            collective_id=3, has_side_effects=True, vmem_limit_bytes=56 << 20
        ),
        name="attend_project",
    )(
        chunks,
        fades,
        queries,
        keys,
        values,
        out_gate,
        head_gain.reshape(1, feats),
        cumulative,
        cumulative.T,
        out_weight,
    )


def body(
    queries,
    keys,
    values,
    decay_log,
    out_gate,
    head_gain,
    out_weight,
    stream,
    norm_gain,
    expert_ids,
    expert_share,
    w_gate,
    w_up,
    w_down,
):
    seq_count, block_len, head_width = queries.shape
    head_count = decay_log.shape[1]
    head_dim = head_width // head_count
    split_shape = (seq_count, block_len, head_count, head_dim)
    key_heads = keys.reshape(split_shape)
    value_heads = values.reshape(split_shape)
    position = jnp.arange(block_len)
    causal = position[:, None] >= position[None, :]
    cumulative = jnp.sum(jnp.where(causal[:, :, None], decay_log[None], 0.0), axis=1)
    block_end = cumulative[-1]
    keys_faded = jnp.exp(block_end[None, :] - cumulative)[None, :, :, None] * key_heads.astype(
        jnp.float32
    )
    local_state = jnp.einsum(
        "sjhd,sjhe->shde",
        keys_faded,
        value_heads.astype(jnp.float32),
        precision=lax.Precision.HIGHEST,
    )
    sub_len = stream.shape[1]
    model_width = stream.shape[2]
    exp_count = lax.axis_size(EXP)
    x_count = lax.axis_size("x")
    y_count = lax.axis_size("y")
    ctx_count = x_count * y_count
    tok_count = seq_count * sub_len
    projected = front(
        local_state, cumulative, queries, keys, values, out_gate, head_gain, out_weight
    )
    part_width = out_weight.shape[1] * y_count
    projected = (
        projected.reshape(x_count, tok_count, y_count, part_width // y_count)
        .transpose(1, 2, 0, 3)
        .reshape(tok_count, model_width)
        .astype(jnp.float32)
    )
    residual_sum = stream.reshape(tok_count, model_width).astype(jnp.float32) + projected
    stream_square = jnp.mean(residual_sum * residual_sum, axis=-1, keepdims=True)
    normed = (residual_sum * lax.rsqrt(stream_square + 1e-06) * norm_gain).astype(jnp.bfloat16)
    expert_count = exp_count
    capacity = max(2, (2 * tok_count + expert_count - 1) // expert_count + 1)
    slot_total = expert_count * capacity
    picks = expert_ids.reshape(2 * tok_count)
    copy_no = jnp.arange(2 * tok_count)
    earlier = (copy_no[None, :] < copy_no[:, None]) & (picks[None, :] == picks[:, None])
    ranking = jnp.sum(earlier.astype(jnp.int32), axis=1)
    main = capacity - 1
    slot_of = jnp.where(ranking < main, picks * main + ranking, expert_count * main + picks)
    placing = slot_of[:, None] == jnp.arange(slot_total, dtype=jnp.int32)[None, :]
    token_placing = jnp.any(placing.reshape(tok_count, 2, slot_total), axis=1)
    to_slots = token_placing.T.astype(jnp.bfloat16)
    main_total = expert_count * main
    main_rows = jnp.dot(
        to_slots[:main_total], normed, preferred_element_type=jnp.float32
    ).astype(jnp.bfloat16)
    last_rows = jnp.dot(to_slots[main_total:], normed, preferred_element_type=jnp.float32)
    hid = expert_terms(
        main_rows.reshape(expert_count, main, model_width),
        last_rows.reshape(expert_count, 1, model_width),
        w_gate[0].T,
        w_up[0].T,
    )
    back_main, back_last = expert_sum(hid, w_down[0], expert_count)
    returned = jnp.concatenate(
        [
            back_main.reshape(main_total, model_width).astype(jnp.float32),
            back_last.reshape(expert_count, model_width),
        ],
        axis=0,
    )
    weighting = jnp.where(placing, expert_share.reshape(2 * tok_count, 1), 0.0)
    weighting = jnp.sum(weighting.reshape(tok_count, 2, slot_total), axis=1)
    expert_mix = jnp.dot(weighting, returned, precision=lax.Precision.HIGHEST)
    result = (residual_sum + expert_mix).astype(jnp.bfloat16)
    return result.reshape(seq_count, sub_len, model_width)


def solution(mesh):
    n_exp = mesh.shape["exp"]
    side = round(mesh.shape["ctx"] ** 0.5)
    fine = Mesh(mesh.devices.reshape(side, side, n_exp // 2, 2), ("y", "x", "z", "c"))
    return jax.shard_map(
        body,
        mesh=fine,
        in_specs=(
            P(None, CTX, EXP),
            P(None, CTX, EXP),
            P(None, CTX, EXP),
            P(CTX, EXP),
            P(None, CTX, EXP),
            P(EXP),
            P(EXP, CTX),
            P(None, CTX + EXP, None),
            P(),
            P(CTX + EXP, None, None),
            P(CTX + EXP, None, None),
            P(EXP, None, CTX),
            P(EXP, None, CTX),
            P(EXP, CTX, None),
        ),
        out_specs=P(None, CTX + EXP, None),
        check_vma=False,
    )
```

```python
import jax
import jax.numpy as jnp
from jax import lax
from jax.experimental import pallas as pl
from jax.experimental.pallas import tpu as pltpu
from jax.sharding import Mesh, PartitionSpec as P

CTX = ("y", "x")
EXP = ("z", "c")


MESH = pl.DeviceIdType.MESH
AXES = (("x", "y"), ("y", "x"))


def greet(others):
    barrier = pltpu.get_barrier_semaphore()
    for where in others:
        pl.semaphore_signal(barrier, inc=1, device_id=where, device_id_type=MESH)
    pl.semaphore_wait(barrier, len(others))


def signal_others(others):
    barrier = pltpu.get_barrier_semaphore()
    for where in others:
        pl.semaphore_signal(barrier, inc=1, device_id=where, device_id_type=MESH)
    return barrier


def expert_place(t):
    return {"z": t // 2, "c": lax.rem(t, 2)}


def gather_kernel(
    main_ref,
    last_ref,
    wg_hbm,
    wu_hbm,
    hid_ref,
    buf_a,
    buf_b,
    rows_ref,
    wg,
    wu,
    xin,
    acc_g,
    acc_u,
    last_in,
    last_out,
    ssem,
    rsem,
    lsem,
    esend,
    erecv,
):
    n = 4
    experts, main, _ = main_ref.shape
    mine_e = lax.axis_index("z") * 2 + lax.axis_index("c")
    count, width = rows_ref.shape
    half = width // 2
    quarter = half // 2
    hidden = wg.shape[0]
    buf = (buf_a, buf_b)
    place = {a: lax.axis_index(a) for a in ("x", "y")}

    def step(axis, by):
        return lax.rem(place[axis] + (by + n), n)

    load_g = pltpu.make_async_copy(wg_hbm, wg, lsem.at[0])
    load_u = pltpu.make_async_copy(wu_hbm, wu, lsem.at[1])
    load_g.start()
    load_u.start()
    greet(
        [{a: step(a, d)} for a in ("x", "y") for d in (1, -1)]
        + [expert_place(lax.rem(mine_e + d, experts)) for d in range(1, experts)]
    )

    def main_rows(e):
        return rows_ref.at[pl.ds(pl.multiple_of(e * main, 8), main)]

    def deal(d, to, frm):
        return [
            pltpu.make_async_remote_copy(
                src_ref=src,
                dst_ref=dst,
                send_sem=esend.at[k, d],
                recv_sem=erecv.at[k, d],
                device_id=expert_place(to),
                device_id_type=MESH,
            )
            for k, (src, dst) in enumerate(
                ((main_ref.at[to], main_rows(frm)), (last_ref.at[to], last_in.at[frm]))
            )
        ]

    @pl.loop(1, experts)
    def _(d):
        for c in deal(d, lax.rem(mine_e + d, experts), mine_e):
            c.start()

    own_main = pltpu.make_async_copy(main_ref.at[mine_e], main_rows(mine_e), lsem.at[6])
    own_last = pltpu.make_async_copy(last_ref.at[mine_e], last_in.at[mine_e], lsem.at[7])
    own_main.start()
    own_last.start()
    acc_g[...] = jnp.zeros_like(acc_g)
    acc_u[...] = jnp.zeros_like(acc_u)
    own_main.wait()
    own_last.wait()

    @pl.loop(1, experts)
    def _(d):
        for c in deal(d, lax.rem(mine_e + d, experts), lax.rem(mine_e - d + experts, experts)):
            c.wait()

    last_out[...] = last_in[...].reshape(last_out.shape).astype(jnp.bfloat16)
    put_last = pltpu.make_async_copy(
        last_out, rows_ref.at[pl.ds(experts * main, experts)], lsem.at[6]
    )
    put_last.start()
    put_last.wait()

    def row(h, fi, si):
        return buf[h].at[fi, pl.ds(pl.multiple_of(si * count, 8), count)]

    def cut(ref, k):
        return ref.at[:, pl.ds((k - 2) * quarter, quarter)] if k >= 2 else ref

    def send(h, stage, kind, axis, src, dst):
        to = step(axis, 1 if kind % 2 == 0 else -1)
        c = pltpu.make_async_remote_copy(
            src_ref=cut(src, kind),
            dst_ref=cut(dst, kind),
            send_sem=ssem.at[h, stage, kind],
            recv_sem=rsem.at[h, stage, kind],
            device_id={axis: to},
            device_id_type=MESH,
        )
        c.start()
        sent.append(c)

    def arrived(h, stage, kind, axis, dst):
        pltpu.make_async_remote_copy(
            src_ref=cut(dst, kind),
            dst_ref=cut(dst, kind),
            send_sem=ssem.at[h, stage, kind],
            recv_sem=rsem.at[h, stage, kind],
            device_id={axis: step(axis, 1)},
            device_id_type=MESH,
        ).wait_recv()

    sent = []
    shift = (0, -1, 1, 2)
    own = [rows_ref.at[:, pl.ds(h * half, half)] for h in range(2)]
    keep = []
    for h in range(2):
        first, second = AXES[h]
        mine = row(h, place[first], place[second])
        for kind in range(2):
            send(h, n, kind, first, own[h], mine)
    for h in range(2):
        first, second = AXES[h]
        mine = row(h, place[first], place[second])
        for kind in range(2):
            send(h, 0, kind, second, own[h], mine)
        keep.append(pltpu.make_async_copy(own[h], mine, lsem.at[2 + h]))
        keep[h].start()

    def spread(h, j):
        first, second = AXES[h]
        here = row(h, step(first, shift[j]), place[second])
        for kind in range(2):
            send(h, j, kind, second, here, here)

    def pass_on(h, stage, kind):
        first, second = AXES[h]
        by = -1 if kind == 0 else 1
        if stage == n:
            here = row(h, step(first, by), place[second])
            axis = first
        else:
            here = row(h, step(first, shift[stage]), step(second, by))
            axis = second
        arrived(h, stage, kind, axis, here)
        send(h, stage, kind + 2, axis, here, here)

    def far(h, stage):
        first, second = AXES[h]
        if stage == n:
            here, axis = row(h, step(first, 2), place[second]), first
        else:
            here, axis = row(h, step(first, shift[stage]), step(second, 2)), second
        for kind in (2, 3):
            arrived(h, stage, kind, axis, here)

    def load(h, j):
        return pltpu.make_async_copy(
            buf[h].at[step(AXES[h][0], shift[j])], xin.at[h], lsem.at[4 + h]
        )

    def multiply(h, j):
        load(h, j).wait()
        fi = step(AXES[h][0], shift[j])
        for w, acc in ((wg, acc_g), (wu, acc_u)):
            got = lax.dot_general(
                xin[h],
                w[:, pl.ds(h * half, half)],
                (((1,), (1,)), ((), ())),
                preferred_element_type=jnp.float32,
            ).reshape(n, count, hidden)
            if h == 0:
                acc[fi] += got
            else:
                acc[:, fi] += got

    def activate(p, q):
        g = acc_g[p, q]
        out = (g / (1.0 + jnp.exp(-g)) * acc_u[p, q]).astype(jnp.bfloat16)
        hid_ref[p, q] = out.astype(jnp.float32)

    for kind in range(2):
        for h in range(2):
            pass_on(h, n, kind)
            spread(h, 1 + kind)
    for kind in range(2):
        for h in range(2):
            pass_on(h, 0, kind)
    for h in range(2):
        far(h, n)
        spread(h, 3)
    load_g.wait()
    load_u.wait()
    for j in range(n):
        if j + 1 < n:
            for kind in range(2):
                for h in range(2):
                    pass_on(h, j + 1, kind)
        for h in range(2):
            if j == 0:
                keep[h].wait()
            far(h, j)
            load(h, j).start()
        for h in range(2):
            multiply(h, j)
        if j == 2:

            @pl.loop(0, 9)
            def _(k):
                a, b = k // 3, lax.rem(k, 3)
                activate(step("x", a + a // 2), step("y", b + b // 2))

    @pl.loop(0, n)
    def _(k):
        activate(step("x", 2), step("y", k))

    @pl.loop(0, n - 1)
    def _(k):
        activate(step("x", k + k // 2), step("y", 2))

    for c in sent:
        c.wait_send()


def reduce_kernel(
    hid_ref,
    wd_hbm,
    back_main,
    back_last,
    wd,
    rows,
    t_a,
    t_b,
    r_opp,
    r_full,
    part,
    r_opp2,
    r_full2,
    out_main,
    out_last,
    ssem,
    rsem,
    lsem,
    esend,
    erecv,
):
    n = 4
    experts, main, width = out_main.shape
    count = experts * (main + 1)
    mine_e = lax.axis_index("z") * 2 + lax.axis_index("c")
    half = width // 2
    quarter = half // 2
    block = min(512, quarter)
    t = (t_a, t_b)
    place = {a: lax.axis_index(a) for a in ("x", "y")}

    def step(axis, by):
        return lax.rem(place[axis] + (by + n), n)

    load = pltpu.make_async_copy(wd_hbm, wd, lsem.at[0])
    load.start()
    others = [{a: step(a, d)} for a in ("x", "y") for d in (1, -1)]
    others += [expert_place(lax.rem(mine_e + d, experts)) for d in range(1, experts)]
    barrier = signal_others(others)
    load.wait()
    shift = (2, 1, -1, 0)
    sent = []

    def copy(h, stage, kind, axis, src, dst):
        return pltpu.make_async_remote_copy(
            src_ref=src,
            dst_ref=dst,
            send_sem=ssem.at[h, stage, kind],
            recv_sem=rsem.at[h, stage, kind],
            device_id={axis: step(axis, 1 if kind % 2 == 0 else -1)},
            device_id_type=MESH,
        )

    def send(*a):
        c = copy(*a)
        c.start()
        sent.append(c)

    def arrived(h, stage, kind, axis, dst):
        copy(h, stage, kind, axis, dst, dst).wait_recv()

    def multiply(h, j):
        lead = step(AXES[h][0], shift[j])
        taken = hid_ref[lead] if h == 0 else hid_ref[:, pl.ds(lead, 1)]
        rows[...] = taken.reshape(rows.shape).astype(jnp.bfloat16)

        @pl.loop(0, half // block)
        def _(b):
            at = pl.multiple_of(b * block, 128)
            got = jnp.dot(
                rows[...],
                wd[:, pl.ds(pl.multiple_of(h * half + at, 128), block)],
                preferred_element_type=jnp.float32,
            )
            t[h][j, :, :, pl.ds(at, block)] = got.reshape(n, count, block).astype(jnp.bfloat16)

    def far_out(h, j):
        ring = AXES[h][1]
        for k in range(2):
            send(
                h,
                j,
                k,
                ring,
                t[h].at[j, step(ring, 2), :, pl.ds(k * quarter, quarter)],
                r_opp.at[h, j, k],
            )

    def add_to(ref, k, other):
        @pl.loop(0, quarter // block)
        def _(b):
            at = pl.multiple_of(b * block, 128)
            cols = pl.ds(pl.multiple_of(k * quarter + at, 128), block)
            ref[:, cols] = (
                ref[:, cols].astype(jnp.float32) + other[:, pl.ds(at, block)].astype(jnp.float32)
            ).astype(jnp.bfloat16)

    def add_up(refs, at):
        s = refs[0][:, pl.ds(at, block)].astype(jnp.float32)
        for r in refs[1:]:
            s = s + r[:, pl.ds(at, block)].astype(jnp.float32)
        return s

    def total(dst, refs):
        @pl.loop(0, half // block)
        def _(b):
            at = pl.multiple_of(b * block, 128)
            dst[:, pl.ds(at, block)] = add_up(refs, at).astype(jnp.bfloat16)

    def settle(h, refs):
        @pl.loop(0, half // block)
        def _(b):
            at = pl.multiple_of(b * block, 128)
            cols = pl.ds(pl.multiple_of(h * half + at, 128), block)
            s = add_up(refs, at)
            out_main[:, :, cols] = (
                s[: experts * main].reshape(experts, main, block).astype(jnp.bfloat16)
            )
            out_last[:, :, cols] = s[experts * main :].reshape(experts, 1, block)

    def give(k, d, to, frm):
        if k == 2:
            src, dst = out_last.at[to], back_last.at[frm]
        else:
            cols = pl.ds(k * half, half)
            src, dst = out_main.at[to, :, cols], back_main.at[frm, :, cols]
        return pltpu.make_async_remote_copy(
            src_ref=src,
            dst_ref=dst,
            send_sem=esend.at[k, d],
            recv_sem=erecv.at[k, d],
            device_id=expert_place(to),
            device_id_type=MESH,
        )

    def near(h, j):
        ring = AXES[h][1]
        for k in range(2):
            arrived(h, j, k, ring, r_opp.at[h, j, k])
            mine = t[h].at[j, step(ring, 1 if k == 0 else -1)]
            add_to(mine, k, r_opp.at[h, j, k])
            send(h, j, 2 + k, ring, mine, r_full.at[h, j, k])

    def both(h, j):
        for k in range(2):
            arrived(h, j, 2 + k, AXES[h][1], r_full.at[h, j, k])

    def finish(h, j):
        both(h, j)
        total(
            part.at[h, j],
            [t[h].at[j, place[AXES[h][1]]], r_full.at[h, j, 0], r_full.at[h, j, 1]],
        )

    for j in range(2):
        for h in range(2):
            multiply(h, j)
            if j == 0 and h == 0:
                pl.semaphore_wait(barrier, len(others))
            far_out(h, j)
    for j in range(n):
        for h in range(2):
            near(h, j)
        if j + 2 < n:
            for h in range(2):
                multiply(h, j + 2)
                far_out(h, j + 2)
        if j == 1:
            for h in range(2):
                finish(h, 0)
                for k in range(2):
                    send(
                        h,
                        n,
                        k,
                        AXES[h][0],
                        part.at[h, 0, :, pl.ds(k * quarter, quarter)],
                        r_opp2.at[h, k],
                    )
    for j in (1, 2):
        for h in range(2):
            finish(h, j)
            k = j - 1
            arrived(h, n, k, AXES[h][0], r_opp2.at[h, k])
            add_to(part.at[h, j], k, r_opp2.at[h, k])
            send(h, n, 2 + k, AXES[h][0], part.at[h, j], r_full2.at[h, k])
    for h in range(2):
        both(h, 3)
        for k in range(2):
            arrived(h, n, 2 + k, AXES[h][0], r_full2.at[h, k])
        settle(
            h,
            [
                t[h].at[3, place[AXES[h][1]]],
                r_full.at[h, 3, 0],
                r_full.at[h, 3, 1],
                r_full2.at[h, 0],
                r_full2.at[h, 1],
            ],
        )

        @pl.loop(1, experts)
        def _(d):
            for k in (h,) if h == 0 else (1, 2):
                give(k, d, lax.rem(mine_e + d, experts), mine_e).start()

    back_main[mine_e] = out_main[mine_e]
    back_last[mine_e] = out_last[mine_e]

    @pl.loop(1, experts)
    def _(d):
        for k in range(3):
            give(
                k, d, lax.rem(mine_e + d, experts), lax.rem(mine_e - d + experts, experts)
            ).wait()

    for c in sent:
        c.wait_send()


def expert_terms(main_rows, last_rows, w_gate, w_up):
    n = 4
    experts, main, width = main_rows.shape
    count = experts * (main + 1)
    hidden = w_gate.shape[0]
    half = width // 2
    any_spec = pl.BlockSpec(memory_space=pl.ANY)
    vmem = pl.BlockSpec(memory_space=pltpu.VMEM)
    bf16 = jnp.bfloat16
    return pl.pallas_call(
        gather_kernel,
        out_shape=[
            jax.ShapeDtypeStruct((n, n, count, hidden), jnp.float32),
            jax.ShapeDtypeStruct((n, n * count, half), bf16),
            jax.ShapeDtypeStruct((n, n * count, half), bf16),
            jax.ShapeDtypeStruct((count, width), bf16),
        ],
        in_specs=[any_spec] * 4,
        out_specs=[vmem, any_spec, any_spec, any_spec],
        scratch_shapes=[
            pltpu.VMEM((hidden, width), bf16),
            pltpu.VMEM((hidden, width), bf16),
            pltpu.VMEM((2, n * count, half), bf16),
            pltpu.VMEM((n, n, count, hidden), jnp.float32),
            pltpu.VMEM((n, n, count, hidden), jnp.float32),
            pltpu.VMEM((experts, 1, width), jnp.float32),
            pltpu.VMEM((experts, width), bf16),
            pltpu.SemaphoreType.DMA((2, n + 1, 4)),
            pltpu.SemaphoreType.DMA((2, n + 1, 4)),
            pltpu.SemaphoreType.DMA((8,)),
            pltpu.SemaphoreType.DMA((2, experts)),
            pltpu.SemaphoreType.DMA((2, experts)),
        ],
        compiler_params=pltpu.CompilerParams(
            collective_id=1, has_side_effects=True, vmem_limit_bytes=60 << 20
        ),
        name="gather_experts",
    )(main_rows, last_rows, w_gate, w_up)[0]


def expert_sum(hid, w_down, experts):
    n = 4
    hidden, width = w_down.shape
    count = hid.shape[2]
    main = count // experts - 1
    half = width // 2
    any_spec = pl.BlockSpec(memory_space=pl.ANY)
    vmem = pl.BlockSpec(memory_space=pltpu.VMEM)
    bf16 = jnp.bfloat16
    return pl.pallas_call(
        reduce_kernel,
        out_shape=[
            jax.ShapeDtypeStruct((experts, main, width), bf16),
            jax.ShapeDtypeStruct((experts, 1, width), jnp.float32),
        ],
        in_specs=[vmem, any_spec],
        out_specs=[vmem, vmem],
        scratch_shapes=[
            pltpu.VMEM((hidden, width), bf16),
            pltpu.VMEM((n * count, hidden), bf16),
            pltpu.VMEM((n, n, count, half), bf16),
            pltpu.VMEM((n, n, count, half), bf16),
            pltpu.VMEM((2, n, 2, count, half // 2), bf16),
            pltpu.VMEM((2, n, 2, count, half), bf16),
            pltpu.VMEM((2, 3, count, half), bf16),
            pltpu.VMEM((2, 2, count, half // 2), bf16),
            pltpu.VMEM((2, 2, count, half), bf16),
            pltpu.VMEM((experts, main, width), bf16),
            pltpu.VMEM((experts, 1, width), jnp.float32),
            pltpu.SemaphoreType.DMA((2, n + 1, 4)),
            pltpu.SemaphoreType.DMA((2, n + 1, 4)),
            pltpu.SemaphoreType.DMA((1,)),
            pltpu.SemaphoreType.DMA((3, experts)),
            pltpu.SemaphoreType.DMA((3, experts)),
        ],
        compiler_params=pltpu.CompilerParams(
            collective_id=2, has_side_effects=True, vmem_limit_bytes=60 << 20
        ),
        name="sum_experts",
    )(hid, w_down)


def front_kernel(
    chunks,
    fades,
    q_ref,
    k_ref,
    v_ref,
    gate_ref,
    gain_ref,
    cum_ref,
    cum_t_ref,
    stream_ref,
    norm_gain_ref,
    slots_ref,
    weight,
    residual_ref,
    main_ref,
    last_ref,
    out_ref,
    got,
    got_fade,
    held,
    incoming,
    decay,
    inner,
    scale,
    spread_tok,
    own_tok,
    tok,
    w,
    prod,
    other,
    ring_opp,
    ring_full,
    done,
    asend,
    arecv,
    wsend,
    wrecv,
    ssem,
    rsem,
    lsem,
):
    n = 4
    blocks, per, head_dim, _ = chunks.shape
    seqs, length, feats = q_ref.shape
    heads = fades.shape[0]
    cores, zs, count, width = prod.shape[1:]
    sub = length // (cores * zs)
    half_f = feats // 2
    half = width // 2
    block = width // n
    x = lax.axis_index("x")
    y = lax.axis_index("y")
    z = lax.axis_index("z")
    c = lax.axis_index("c")
    me = y * n + x

    def xs(by):
        return lax.rem(x + (by + n), n)

    def yy(by):
        return lax.rem(y + (by + n), n)

    def zz(by):
        return lax.rem(z + (by + n), n)

    def where(t):
        return {"y": t // n, "x": lax.rem(t, n)}

    load = pltpu.make_async_copy(weight, w.at[y], lsem.at[0])
    load.start()
    barrier = pltpu.get_barrier_semaphore()

    @pl.loop(1, blocks)
    def _(d):
        pl.semaphore_signal(
            barrier, inc=1, device_id=where(lax.rem(me + d, blocks)), device_id_type=MESH
        )

    for there in ({"z": zz(1)}, {"z": zz(-1)}, {"c": 1 - c}):
        pl.semaphore_signal(barrier, inc=1, device_id=there, device_id_type=MESH)
    pl.semaphore_wait(barrier, blocks + 2)

    def state_copy(kind, d, src, dst, t):
        return pltpu.make_async_remote_copy(
            src_ref=src,
            dst_ref=dst,
            send_sem=asend.at[kind, d],
            recv_sem=arecv.at[kind, d],
            device_id=where(t),
            device_id_type=MESH,
        )

    def fade_of(t):
        return fades.at[pl.ds(lax.rem(t * per, heads), per)]

    @pl.loop(1, blocks)
    def _(d):
        t = lax.rem(me + d, blocks)
        state_copy(0, d, chunks.at[t], got.at[me], t).start()
        state_copy(1, d, fade_of(t), got_fade.at[me], t).start()

    got[me] = chunks[me]
    got_fade[me] = fade_of(me)[...]

    row = lax.broadcasted_iota(jnp.int32, (length, length), 0)
    col = lax.broadcasted_iota(jnp.int32, (length, length), 1)
    for h in range(heads):
        gap = cum_ref[:, h : h + 1] - cum_t_ref[h : h + 1, :]
        decay[h] = jnp.exp(jnp.where(row >= col, gap, -1e30))

    @pl.loop(0, seqs)
    def _(s):
        g = gate_ref[s].astype(jnp.float32)
        scale[s] = gain_ref[...] / (1.0 + jnp.exp(-g))
        for h in range(heads):
            cols = pl.ds(h * head_dim, head_dim)
            scores = lax.dot_general(
                q_ref[s, :, cols],
                k_ref[s, :, cols],
                (((1,), (1,)), ((), ())),
                preferred_element_type=jnp.float32,
            )
            mix = (scores * decay[h]).astype(jnp.bfloat16)
            inner[s, :, cols] = jnp.dot(
                mix, v_ref[s, :, cols], preferred_element_type=jnp.float32
            )

    @pl.loop(1, blocks)
    def _(d):
        t = lax.rem(me + d, blocks)
        frm = lax.rem(me - d + blocks, blocks)
        state_copy(0, d, chunks.at[t], got.at[frm], t).wait()
        state_copy(1, d, fade_of(t), got_fade.at[frm], t).wait()

    def advance(b, state):
        held[b] = state.astype(jnp.bfloat16)
        d = lax.rem(b - me + blocks, blocks)

        @pl.when(d != 0)
        def _():
            state_copy(2, d, held.at[b], incoming.at[me], b).start()

        return got_fade[b][:, :1, :] * state + got[b].astype(jnp.float32)

    lax.fori_loop(0, blocks, advance, jnp.zeros(got.shape[1:], jnp.float32))
    incoming[me] = held[me]
    load.wait()
    rows_of = [pl.ds(k * half_f, half_f) for k in range(2)]

    def weight_copy(k, src, dst, by):
        return pltpu.make_async_remote_copy(
            src_ref=src,
            dst_ref=dst,
            send_sem=wsend.at[k],
            recv_sem=wrecv.at[k],
            device_id={"y": yy(by)},
            device_id_type=MESH,
        )

    sent = []
    for k, by in ((0, 1), (1, -1)):
        sent.append(weight_copy(k, weight, w.at[y], by))
        sent[-1].start()

    @pl.loop(1, blocks)
    def _(d):
        t = lax.rem(me + d, blocks)
        frm = lax.rem(me - d + blocks, blocks)
        state_copy(2, d, held.at[t], incoming.at[frm], t).wait()

    @pl.loop(0, seqs)
    def _(s):
        for h in range(heads):
            cols = pl.ds(h * head_dim, head_dim)
            pair = s * heads + h
            state = incoming[pair // per, lax.rem(pair, per)]
            carried = jnp.dot(q_ref[s, :, cols], state, preferred_element_type=jnp.float32)
            attended = inner[s, :, cols] + jnp.exp(cum_ref[:, h : h + 1]) * carried
            square = jnp.mean(attended * attended, axis=-1, keepdims=True)
            mixed = attended * lax.rsqrt(square + 1e-06) * scale[s, :, cols]
            parted = mixed.reshape(zs, cores, sub, head_dim)
            for k in range(cores):
                spread_tok[k, :, pl.ds(s, 1), :, cols] = parted[:, k : k + 1]

    own_tok[...] = spread_tok[...].reshape(own_tok.shape).astype(jnp.bfloat16)

    def copy(j, kind, src, dst, axis, to):
        return pltpu.make_async_remote_copy(
            src_ref=src,
            dst_ref=dst,
            send_sem=ssem.at[j, kind],
            recv_sem=rsem.at[j, kind],
            device_id={axis: to},
            device_id_type=MESH,
        )

    def send(*a):
        cp = copy(*a)
        cp.start()
        sent.append(cp)

    def arrived(j, kind, dst, axis):
        to = xs(1) if axis == "x" else zz(1) if axis == "z" else 1 - c
        copy(j, kind, dst, dst, axis, to).wait_recv()

    shift = (0, -1, 1, 2)
    send(0, 0, own_tok, tok.at[0], "x", xs(1))
    send(0, 1, own_tok, tok.at[1], "x", xs(-1))

    def dot_part(j, g):
        src = own_tok if j == 0 else tok.at[j - 1]
        cols = pl.ds(pl.multiple_of(g * block, 128), block)
        part = jnp.dot(src[...], w[g], preferred_element_type=jnp.float32)
        prod[j, :, :, :, cols] = part.reshape(cores, zs, count, block).astype(jnp.bfloat16)

    def near_groups(j):
        @pl.loop(0, n - 1)
        def _(i):
            dot_part(j, yy(i + i // 2))

    def exchange(j):
        send(j, 2, prod.at[j, 1 - c], other.at[j], "c", 1 - c)

    def core_add(j):
        arrived(j, 2, other.at[j], "c")
        mine = prod.at[j, c]

        @pl.loop(0, n)
        def _(b):
            cols = pl.ds(pl.multiple_of(b * block, 128), block)
            mine[:, :, cols] = (
                mine[:, :, cols].astype(jnp.float32) + other[j, :, :, cols].astype(jnp.float32)
            ).astype(jnp.bfloat16)

        for k in range(2):
            send(
                j,
                3 + k,
                mine.at[zz(2), :, pl.ds(k * half, half)],
                ring_opp.at[j, k],
                "z",
                zz(1 if k == 0 else -1),
            )

    def near(j):
        for k in range(2):
            arrived(j, 3 + k, ring_opp.at[j, k], "z")
            to = zz(1 if k == 0 else -1)
            mine = prod.at[j, c, to]
            cols = pl.ds(k * half, half)
            mine[:, cols] = (
                mine[:, cols].astype(jnp.float32) + ring_opp[j, k].astype(jnp.float32)
            ).astype(jnp.bfloat16)
            send(j, 5 + k, mine, ring_full.at[j, k], "z", to)

    def finish(j):
        for k in range(2):
            arrived(j, 5 + k, ring_full.at[j, k], "z")
        s = (
            prod[j, c, z].astype(jnp.float32)
            + ring_full[j, 0].astype(jnp.float32)
            + ring_full[j, 1].astype(jnp.float32)
        ).astype(jnp.bfloat16)
        if j == 0:
            out_ref[x] = s
        else:
            done[j] = s
            send(j, 7, done.at[j], out_ref.at[x], "x", xs(shift[j]))

    for k, by in ((0, 1), (1, -1)):
        weight_copy(k, weight, w.at[yy(-by)], by).wait_recv()
        part_w = w.at[yy(-by), rows_of[k]]
        sent.append(weight_copy(2 + k, part_w, part_w, by))
        sent[-1].start()
    near_groups(0)
    for k in range(2):
        arrived(0, k, tok.at[k], "x")
        cols = pl.ds(k * half_f, half_f)
        send(1, k, tok.at[k, :, cols], tok.at[2, :, cols], "x", xs(1 if k == 0 else -1))
    near_groups(1)
    for k, by in ((0, 1), (1, -1)):
        far_w = w.at[yy(2), rows_of[k]]
        weight_copy(2 + k, far_w, far_w, by).wait_recv()
    for j in range(2):
        dot_part(j, yy(2))
        exchange(j)
    near_groups(2)
    dot_part(2, yy(2))
    exchange(2)
    core_add(0)
    core_add(1)
    near(0)
    for k in range(2):
        arrived(1, k, tok.at[2, :, pl.ds(k * half_f, half_f)], "x")
    near_groups(3)
    dot_part(3, yy(2))
    exchange(3)
    core_add(2)
    near(1)
    core_add(3)
    finish(0)
    near(2)
    finish(1)
    near(3)
    finish(2)
    finish(3)
    for j in (1, 2, 3):
        arrived(j, 7, out_ref.at[xs(-shift[j])], "x")

    tokens, model = residual_ref.shape
    experts, main, _ = main_ref.shape
    total = jnp.zeros((tokens, 1), jnp.float32)
    for i in range(n):
        for k in range(n):
            cols = pl.ds((i * n + k) * block, block)
            r = stream_ref[:, :, cols].astype(jnp.float32).reshape(tokens, block)
            r = r + out_ref[k, :, pl.ds(i * block, block)].astype(jnp.float32)
            residual_ref[:, cols] = r
            total = total + jnp.sum(r * r, axis=-1, keepdims=True)
    inverse = lax.rsqrt(total / model + 1e-06)

    @pl.loop(0, n * n)
    def _(i):
        cols = pl.ds(pl.multiple_of(i * block, 128), block)
        normed = (residual_ref[:, cols] * inverse * norm_gain_ref[:, cols]).astype(jnp.bfloat16)
        placed = jnp.dot(slots_ref[...], normed, preferred_element_type=jnp.float32)
        main_ref[:, :, cols] = (
            placed[: experts * main].reshape(experts, main, block).astype(jnp.bfloat16)
        )
        last_ref[:, :, cols] = placed[experts * main :].reshape(experts, 1, block)

    for cp in sent:
        cp.wait_send()


def front(
    local_state,
    cumulative,
    queries,
    keys,
    values,
    out_gate,
    head_gain,
    out_weight,
    stream,
    norm_gain,
    slots,
    experts,
):
    n = 4
    seqs, heads, width, _ = local_state.shape
    blocks = n * n
    per = seqs * heads // blocks
    length, feats = queries.shape[1:]
    cores, zs = lax.axis_size("c"), lax.axis_size("z")
    count = seqs * length // (cores * zs)
    rows = seqs * length
    columns = out_weight.shape[1] * n
    model = stream.shape[2]
    bf16, f32 = jnp.bfloat16, jnp.float32
    chunks = local_state.reshape(blocks, per, width, width).astype(bf16)
    fades = jnp.broadcast_to(jnp.exp(cumulative[-1])[:, None, None], (heads, 8, width))
    vmem = pl.BlockSpec(memory_space=pltpu.VMEM)
    return pl.pallas_call(
        front_kernel,
        out_shape=[
            jax.ShapeDtypeStruct((count, model), f32),
            jax.ShapeDtypeStruct((experts, slots.shape[0] // experts - 1, model), bf16),
            jax.ShapeDtypeStruct((experts, 1, model), f32),
        ],
        in_specs=[vmem] * 12 + [pl.BlockSpec(memory_space=pl.ANY)],
        out_specs=[vmem] * 3,
        scratch_shapes=[
            pltpu.VMEM((n, count, columns), bf16),
            pltpu.VMEM(chunks.shape, bf16),
            pltpu.VMEM((blocks, per, 8, width), f32),
            pltpu.VMEM(chunks.shape, bf16),
            pltpu.VMEM(chunks.shape, bf16),
            pltpu.VMEM((heads, length, length), f32),
            pltpu.VMEM(queries.shape, f32),
            pltpu.VMEM(queries.shape, f32),
            pltpu.VMEM((cores, zs, seqs, length // (cores * zs), feats), f32),
            pltpu.VMEM((rows, feats), bf16),
            pltpu.VMEM((3, rows, feats), bf16),
            pltpu.VMEM((n, feats, columns // n), bf16),
            pltpu.VMEM((n, cores, zs, count, columns), bf16),
            pltpu.VMEM((n, zs, count, columns), bf16),
            pltpu.VMEM((n, 2, count, columns // 2), bf16),
            pltpu.VMEM((n, 2, count, columns), bf16),
            pltpu.VMEM((n, count, columns), bf16),
            pltpu.SemaphoreType.DMA((3, blocks)),
            pltpu.SemaphoreType.DMA((3, blocks)),
            pltpu.SemaphoreType.DMA((4,)),
            pltpu.SemaphoreType.DMA((4,)),
            pltpu.SemaphoreType.DMA((n, 8)),
            pltpu.SemaphoreType.DMA((n, 8)),
            pltpu.SemaphoreType.DMA((1,)),
        ],
        compiler_params=pltpu.CompilerParams(
            collective_id=3, has_side_effects=True, vmem_limit_bytes=56 << 20
        ),
        name="front",
    )(
        chunks,
        fades,
        queries,
        keys,
        values,
        out_gate,
        head_gain.reshape(1, feats),
        cumulative,
        cumulative.T,
        stream,
        norm_gain.reshape(1, model),
        slots,
        out_weight,
    )


def body(
    queries,
    keys,
    values,
    decay_log,
    out_gate,
    head_gain,
    out_weight,
    stream,
    norm_gain,
    expert_ids,
    expert_share,
    w_gate,
    w_up,
    w_down,
):
    seq_count, block_len, head_width = queries.shape
    head_count = decay_log.shape[1]
    head_dim = head_width // head_count
    split_shape = (seq_count, block_len, head_count, head_dim)
    key_heads = keys.reshape(split_shape)
    value_heads = values.reshape(split_shape)
    position = jnp.arange(block_len)
    causal = position[:, None] >= position[None, :]
    cumulative = jnp.sum(jnp.where(causal[:, :, None], decay_log[None], 0.0), axis=1)
    block_end = cumulative[-1]
    keys_faded = jnp.exp(block_end[None, :] - cumulative)[None, :, :, None] * key_heads.astype(
        jnp.float32
    )
    local_state = jnp.einsum(
        "sjhd,sjhe->shde",
        keys_faded.astype(jnp.bfloat16),
        value_heads,
        preferred_element_type=jnp.float32,
    )
    sub_len = stream.shape[1]
    model_width = stream.shape[2]
    exp_count = lax.axis_size(EXP)
    tok_count = seq_count * sub_len
    expert_count = exp_count
    capacity = max(2, (2 * tok_count + expert_count - 1) // expert_count + 1)
    slot_total = expert_count * capacity
    picks = expert_ids.reshape(2 * tok_count)
    copy_no = jnp.arange(2 * tok_count)
    earlier = (copy_no[None, :] < copy_no[:, None]) & (picks[None, :] == picks[:, None])
    ranking = jnp.sum(earlier.astype(jnp.int32), axis=1)
    main = capacity - 1
    slot_of = jnp.where(ranking < main, picks * main + ranking, expert_count * main + picks)
    placing = slot_of[:, None] == jnp.arange(slot_total, dtype=jnp.int32)[None, :]
    token_placing = jnp.any(placing.reshape(tok_count, 2, slot_total), axis=1)
    main_total = expert_count * main
    residual_sum, main_rows, last_rows = front(
        local_state,
        cumulative,
        queries,
        keys,
        values,
        out_gate,
        head_gain,
        out_weight,
        stream,
        norm_gain,
        token_placing.T.astype(jnp.bfloat16),
        expert_count,
    )
    hid = expert_terms(main_rows, last_rows, w_gate[0].T, w_up[0].T)
    back_main, back_last = expert_sum(hid, w_down[0], expert_count)
    returned = jnp.concatenate(
        [
            back_main.reshape(main_total, model_width).astype(jnp.float32),
            back_last.reshape(expert_count, model_width),
        ],
        axis=0,
    )
    weighting = jnp.where(placing, expert_share.reshape(2 * tok_count, 1), 0.0)
    weighting = jnp.sum(weighting.reshape(tok_count, 2, slot_total), axis=1)
    expert_mix = jnp.dot(weighting, returned, precision=lax.Precision.HIGHEST)
    result = (residual_sum + expert_mix).astype(jnp.bfloat16)
    return result.reshape(seq_count, sub_len, model_width)


def solution(mesh):
    n_exp = mesh.shape["exp"]
    side = round(mesh.shape["ctx"] ** 0.5)
    fine = Mesh(mesh.devices.reshape(side, side, n_exp // 2, 2), ("y", "x", "z", "c"))
    return jax.shard_map(
        body,
        mesh=fine,
        in_specs=(
            P(None, CTX, EXP),
            P(None, CTX, EXP),
            P(None, CTX, EXP),
            P(CTX, EXP),
            P(None, CTX, EXP),
            P(EXP),
            P(EXP, CTX),
            P(None, CTX + EXP, None),
            P(),
            P(CTX + EXP, None, None),
            P(CTX + EXP, None, None),
            P(EXP, None, CTX),
            P(EXP, None, CTX),
            P(EXP, CTX, None),
        ),
        out_specs=P(None, CTX + EXP, None),
        check_vma=False,
    )
```

```python
import jax
import jax.numpy as jnp
from jax import lax
from jax.experimental import pallas as pl
from jax.experimental.pallas import tpu as pltpu
from jax.sharding import Mesh, PartitionSpec as P

CTX = ("y", "x")
EXP = ("z", "c")


MESH = pl.DeviceIdType.MESH
AXES = (("x", "y"), ("y", "x"))


def greet(others):
    barrier = pltpu.get_barrier_semaphore()
    for where in others:
        pl.semaphore_signal(barrier, inc=1, device_id=where, device_id_type=MESH)
    pl.semaphore_wait(barrier, len(others))


def signal_others(others):
    barrier = pltpu.get_barrier_semaphore()
    for where in others:
        pl.semaphore_signal(barrier, inc=1, device_id=where, device_id_type=MESH)
    return barrier


def expert_place(t):
    return {"z": t // 2, "c": lax.rem(t, 2)}


def gather_kernel(
    main_ref,
    last_ref,
    wg_hbm,
    wu_hbm,
    hid_ref,
    buf_a,
    buf_b,
    rows_ref,
    wg,
    wu,
    xin,
    acc_g,
    acc_u,
    last_in,
    last_out,
    ssem,
    rsem,
    lsem,
    esend,
    erecv,
):
    n = 4
    experts, main, _ = main_ref.shape
    mine_e = lax.axis_index("z") * 2 + lax.axis_index("c")
    count, width = rows_ref.shape
    half = width // 2
    quarter = half // 2
    hidden = wg.shape[0]
    buf = (buf_a, buf_b)
    place = {a: lax.axis_index(a) for a in ("x", "y")}

    def step(axis, by):
        return lax.rem(place[axis] + (by + n), n)

    load_g = pltpu.make_async_copy(wg_hbm, wg, lsem.at[0])
    load_u = pltpu.make_async_copy(wu_hbm, wu, lsem.at[1])
    load_g.start()
    load_u.start()
    greet(
        [{a: step(a, d)} for a in ("x", "y") for d in (1, -1)]
        + [expert_place(lax.rem(mine_e + d, experts)) for d in range(1, experts)]
    )

    def main_rows(e):
        return rows_ref.at[pl.ds(pl.multiple_of(e * main, 8), main)]

    def deal(d, to, frm):
        return [
            pltpu.make_async_remote_copy(
                src_ref=src,
                dst_ref=dst,
                send_sem=esend.at[k, d],
                recv_sem=erecv.at[k, d],
                device_id=expert_place(to),
                device_id_type=MESH,
            )
            for k, (src, dst) in enumerate(
                (
                    (main_ref.at[to, :, pl.ds(0, half)], main_rows(frm).at[:, pl.ds(0, half)]),
                    (last_ref.at[to], last_in.at[frm]),
                    (main_ref.at[to, :, pl.ds(half, half)], main_rows(frm).at[:, pl.ds(half, half)]),
                )
            )
        ]

    for k in (1, 0, 2):

        @pl.loop(1, experts)
        def _(d):
            deal(d, lax.rem(mine_e + d, experts), mine_e)[k].start()

    own_main = pltpu.make_async_copy(main_ref.at[mine_e], main_rows(mine_e), lsem.at[6])
    own_last = pltpu.make_async_copy(last_ref.at[mine_e], last_in.at[mine_e], lsem.at[7])
    own_main.start()
    own_last.start()
    acc_g[...] = jnp.zeros_like(acc_g)
    acc_u[...] = jnp.zeros_like(acc_u)
    own_main.wait()
    own_last.wait()

    def dealt(k):
        @pl.loop(1, experts)
        def _(d):
            to, frm = lax.rem(mine_e + d, experts), lax.rem(mine_e - d + experts, experts)
            deal(d, to, frm)[k].wait()

    dealt(1)
    last_out[...] = last_in[...].reshape(last_out.shape).astype(jnp.bfloat16)
    put_last = pltpu.make_async_copy(
        last_out, rows_ref.at[pl.ds(experts * main, experts)], lsem.at[6]
    )
    put_last.start()
    put_last.wait()
    dealt(0)

    def row(h, fi, si):
        return buf[h].at[fi, pl.ds(pl.multiple_of(si * count, 8), count)]

    def cut(ref, k):
        return ref.at[:, pl.ds((k - 2) * quarter, quarter)] if k >= 2 else ref

    def send(h, stage, kind, axis, src, dst):
        to = step(axis, 1 if kind % 2 == 0 else -1)
        c = pltpu.make_async_remote_copy(
            src_ref=cut(src, kind),
            dst_ref=cut(dst, kind),
            send_sem=ssem.at[h, stage, kind],
            recv_sem=rsem.at[h, stage, kind],
            device_id={axis: to},
            device_id_type=MESH,
        )
        c.start()
        sent.append(c)

    def arrived(h, stage, kind, axis, dst):
        pltpu.make_async_remote_copy(
            src_ref=cut(dst, kind),
            dst_ref=cut(dst, kind),
            send_sem=ssem.at[h, stage, kind],
            recv_sem=rsem.at[h, stage, kind],
            device_id={axis: step(axis, 1)},
            device_id_type=MESH,
        ).wait_recv()

    sent = []
    shift = (0, -1, 1, 2)
    own = [rows_ref.at[:, pl.ds(h * half, half)] for h in range(2)]
    keep = []
    for h in range(2):
        first, second = AXES[h]
        mine = row(h, place[first], place[second])
        if h == 1:
            dealt(2)
        for kind in range(2):
            send(h, n, kind, first, own[h], mine)
        for kind in range(2):
            send(h, 0, kind, second, own[h], mine)
        keep.append(pltpu.make_async_copy(own[h], mine, lsem.at[2 + h]))
        keep[h].start()

    def spread(h, j):
        first, second = AXES[h]
        here = row(h, step(first, shift[j]), place[second])
        for kind in range(2):
            send(h, j, kind, second, here, here)

    def pass_on(h, stage, kind):
        first, second = AXES[h]
        by = -1 if kind == 0 else 1
        if stage == n:
            here = row(h, step(first, by), place[second])
            axis = first
        else:
            here = row(h, step(first, shift[stage]), step(second, by))
            axis = second
        arrived(h, stage, kind, axis, here)
        send(h, stage, kind + 2, axis, here, here)

    def far(h, stage):
        first, second = AXES[h]
        if stage == n:
            here, axis = row(h, step(first, 2), place[second]), first
        else:
            here, axis = row(h, step(first, shift[stage]), step(second, 2)), second
        for kind in (2, 3):
            arrived(h, stage, kind, axis, here)

    def load(h, j):
        return pltpu.make_async_copy(
            buf[h].at[step(AXES[h][0], shift[j])], xin.at[h], lsem.at[4 + h]
        )

    def multiply(h, j):
        load(h, j).wait()
        fi = step(AXES[h][0], shift[j])
        for w, acc in ((wg, acc_g), (wu, acc_u)):
            got = lax.dot_general(
                xin[h],
                w[:, pl.ds(h * half, half)],
                (((1,), (1,)), ((), ())),
                preferred_element_type=jnp.float32,
            ).reshape(n, count, hidden)
            if h == 0:
                acc[fi] += got
            else:
                acc[:, fi] += got

    def activate(p, q):
        g = acc_g[p, q]
        out = (g / (1.0 + jnp.exp(-g)) * acc_u[p, q]).astype(jnp.bfloat16)
        hid_ref[p, q] = out.astype(jnp.float32)

    for kind in range(2):
        for h in range(2):
            pass_on(h, n, kind)
            spread(h, 1 + kind)
    for kind in range(2):
        for h in range(2):
            pass_on(h, 0, kind)
    for h in range(2):
        far(h, n)
        spread(h, 3)
    load_g.wait()
    load_u.wait()
    for j in range(n):
        if j + 1 < n:
            for kind in range(2):
                for h in range(2):
                    pass_on(h, j + 1, kind)
        for h in range(2):
            if j == 0:
                keep[h].wait()
            far(h, j)
            load(h, j).start()
            if j == n - 1:
                multiply(h, j)
        if j < n - 1:
            for h in range(2):
                multiply(h, j)
        if j == 2:

            @pl.loop(0, 9)
            def _(k):
                a, b = k // 3, lax.rem(k, 3)
                activate(step("x", a + a // 2), step("y", b + b // 2))

    @pl.loop(0, n)
    def _(k):
        activate(step("x", 2), step("y", k))

    @pl.loop(0, n - 1)
    def _(k):
        activate(step("x", k + k // 2), step("y", 2))

    for c in sent:
        c.wait_send()


def reduce_kernel(
    hid_ref,
    wd_hbm,
    back_main,
    back_last,
    wd,
    rows,
    t_a,
    t_b,
    r_opp,
    r_full,
    part,
    r_opp2,
    r_full2,
    out_main,
    out_last,
    ssem,
    rsem,
    lsem,
    esend,
    erecv,
):
    n = 4
    experts, main, width = out_main.shape
    count = experts * (main + 1)
    mine_e = lax.axis_index("z") * 2 + lax.axis_index("c")
    half = width // 2
    quarter = half // 2
    block = min(512, quarter)
    t = (t_a, t_b)
    place = {a: lax.axis_index(a) for a in ("x", "y")}

    def step(axis, by):
        return lax.rem(place[axis] + (by + n), n)

    load = pltpu.make_async_copy(wd_hbm, wd, lsem.at[0])
    load.start()
    others = [{a: step(a, d)} for a in ("x", "y") for d in (1, -1)]
    others += [expert_place(lax.rem(mine_e + d, experts)) for d in range(1, experts)]
    barrier = signal_others(others)
    load.wait()
    shift = (2, 1, -1, 0)
    sent = []

    def copy(h, stage, kind, axis, src, dst):
        return pltpu.make_async_remote_copy(
            src_ref=src,
            dst_ref=dst,
            send_sem=ssem.at[h, stage, kind],
            recv_sem=rsem.at[h, stage, kind],
            device_id={axis: step(axis, 1 if kind % 2 == 0 else -1)},
            device_id_type=MESH,
        )

    def send(*a):
        c = copy(*a)
        c.start()
        sent.append(c)

    def arrived(h, stage, kind, axis, dst):
        copy(h, stage, kind, axis, dst, dst).wait_recv()

    def multiply(h, j):
        lead = step(AXES[h][0], shift[j])
        taken = hid_ref[lead] if h == 0 else hid_ref[:, pl.ds(lead, 1)]
        rows[...] = taken.reshape(rows.shape).astype(jnp.bfloat16)

        @pl.loop(0, half // block)
        def _(b):
            at = pl.multiple_of(b * block, 128)
            got = jnp.dot(
                rows[...],
                wd[:, pl.ds(pl.multiple_of(h * half + at, 128), block)],
                preferred_element_type=jnp.float32,
            )
            t[h][j, :, :, pl.ds(at, block)] = got.reshape(n, count, block).astype(jnp.bfloat16)

    def far_out(h, j):
        ring = AXES[h][1]
        for k in range(2):
            send(
                h,
                j,
                k,
                ring,
                t[h].at[j, step(ring, 2), :, pl.ds(k * quarter, quarter)],
                r_opp.at[h, j, k],
            )

    def add_to(ref, k, other):
        @pl.loop(0, quarter // block)
        def _(b):
            at = pl.multiple_of(b * block, 128)
            cols = pl.ds(pl.multiple_of(k * quarter + at, 128), block)
            ref[:, cols] = (
                ref[:, cols].astype(jnp.float32) + other[:, pl.ds(at, block)].astype(jnp.float32)
            ).astype(jnp.bfloat16)

    def add_up(refs, at):
        s = refs[0][:, pl.ds(at, block)].astype(jnp.float32)
        for r in refs[1:]:
            s = s + r[:, pl.ds(at, block)].astype(jnp.float32)
        return s

    def total(dst, refs):
        @pl.loop(0, half // block)
        def _(b):
            at = pl.multiple_of(b * block, 128)
            dst[:, pl.ds(at, block)] = add_up(refs, at).astype(jnp.bfloat16)

    def settle(h, refs):
        @pl.loop(0, half // block)
        def _(b):
            at = pl.multiple_of(b * block, 128)
            cols = pl.ds(pl.multiple_of(h * half + at, 128), block)
            s = add_up(refs, at)
            out_main[:, :, cols] = (
                s[: experts * main].reshape(experts, main, block).astype(jnp.bfloat16)
            )
            out_last[:, :, cols] = s[experts * main :].reshape(experts, 1, block)

    def give(k, d, to, frm):
        if k == 2:
            src, dst = out_last.at[to], back_last.at[frm]
        else:
            cols = pl.ds(k * half, half)
            src, dst = out_main.at[to, :, cols], back_main.at[frm, :, cols]
        return pltpu.make_async_remote_copy(
            src_ref=src,
            dst_ref=dst,
            send_sem=esend.at[k, d],
            recv_sem=erecv.at[k, d],
            device_id=expert_place(to),
            device_id_type=MESH,
        )

    def near(h, j):
        ring = AXES[h][1]
        for k in range(2):
            arrived(h, j, k, ring, r_opp.at[h, j, k])
            mine = t[h].at[j, step(ring, 1 if k == 0 else -1)]
            add_to(mine, k, r_opp.at[h, j, k])
            send(h, j, 2 + k, ring, mine, r_full.at[h, j, k])

    def both(h, j):
        for k in range(2):
            arrived(h, j, 2 + k, AXES[h][1], r_full.at[h, j, k])

    def finish(h, j):
        both(h, j)
        total(
            part.at[h, j],
            [t[h].at[j, place[AXES[h][1]]], r_full.at[h, j, 0], r_full.at[h, j, 1]],
        )

    for j in range(2):
        for h in range(2):
            multiply(h, j)
            if j == 0 and h == 0:
                pl.semaphore_wait(barrier, len(others))
            far_out(h, j)
    for j in range(n):
        for h in range(2):
            near(h, j)
        if j + 2 < n:
            for h in range(2):
                multiply(h, j + 2)
                far_out(h, j + 2)
        if j == 1:
            for h in range(2):
                finish(h, 0)
                for k in range(2):
                    send(
                        h,
                        n,
                        k,
                        AXES[h][0],
                        part.at[h, 0, :, pl.ds(k * quarter, quarter)],
                        r_opp2.at[h, k],
                    )
    for j in (1, 2):
        for h in range(2):
            finish(h, j)
            k = j - 1
            arrived(h, n, k, AXES[h][0], r_opp2.at[h, k])
            add_to(part.at[h, j], k, r_opp2.at[h, k])
            send(h, n, 2 + k, AXES[h][0], part.at[h, j], r_full2.at[h, k])
    for h in range(2):
        both(h, 3)
        for k in range(2):
            arrived(h, n, 2 + k, AXES[h][0], r_full2.at[h, k])
        settle(
            h,
            [
                t[h].at[3, place[AXES[h][1]]],
                r_full.at[h, 3, 0],
                r_full.at[h, 3, 1],
                r_full2.at[h, 0],
                r_full2.at[h, 1],
            ],
        )

        @pl.loop(1, experts)
        def _(d):
            for k in (h,) if h == 0 else (1, 2):
                give(k, d, lax.rem(mine_e + d, experts), mine_e).start()

    back_main[mine_e] = out_main[mine_e]
    back_last[mine_e] = out_last[mine_e]

    @pl.loop(1, experts)
    def _(d):
        for k in range(3):
            give(
                k, d, lax.rem(mine_e + d, experts), lax.rem(mine_e - d + experts, experts)
            ).wait()

    for c in sent:
        c.wait_send()


def expert_terms(main_rows, last_rows, w_gate, w_up):
    n = 4
    experts, main, width = main_rows.shape
    count = experts * (main + 1)
    hidden = w_gate.shape[0]
    half = width // 2
    any_spec = pl.BlockSpec(memory_space=pl.ANY)
    vmem = pl.BlockSpec(memory_space=pltpu.VMEM)
    bf16 = jnp.bfloat16
    return pl.pallas_call(
        gather_kernel,
        out_shape=[
            jax.ShapeDtypeStruct((n, n, count, hidden), jnp.float32),
            jax.ShapeDtypeStruct((n, n * count, half), bf16),
            jax.ShapeDtypeStruct((n, n * count, half), bf16),
            jax.ShapeDtypeStruct((count, width), bf16),
        ],
        in_specs=[any_spec] * 4,
        out_specs=[vmem, any_spec, any_spec, any_spec],
        scratch_shapes=[
            pltpu.VMEM((hidden, width), bf16),
            pltpu.VMEM((hidden, width), bf16),
            pltpu.VMEM((2, n * count, half), bf16),
            pltpu.VMEM((n, n, count, hidden), jnp.float32),
            pltpu.VMEM((n, n, count, hidden), jnp.float32),
            pltpu.VMEM((experts, 1, width), jnp.float32),
            pltpu.VMEM((experts, width), bf16),
            pltpu.SemaphoreType.DMA((2, n + 1, 4)),
            pltpu.SemaphoreType.DMA((2, n + 1, 4)),
            pltpu.SemaphoreType.DMA((8,)),
            pltpu.SemaphoreType.DMA((3, experts)),
            pltpu.SemaphoreType.DMA((3, experts)),
        ],
        compiler_params=pltpu.CompilerParams(
            collective_id=1, has_side_effects=True, vmem_limit_bytes=60 << 20
        ),
        name="gather_experts",
    )(main_rows, last_rows, w_gate, w_up)[0]


def expert_sum(hid, w_down, experts):
    n = 4
    hidden, width = w_down.shape
    count = hid.shape[2]
    main = count // experts - 1
    half = width // 2
    any_spec = pl.BlockSpec(memory_space=pl.ANY)
    vmem = pl.BlockSpec(memory_space=pltpu.VMEM)
    bf16 = jnp.bfloat16
    return pl.pallas_call(
        reduce_kernel,
        out_shape=[
            jax.ShapeDtypeStruct((experts, main, width), bf16),
            jax.ShapeDtypeStruct((experts, 1, width), jnp.float32),
        ],
        in_specs=[vmem, any_spec],
        out_specs=[vmem, vmem],
        scratch_shapes=[
            pltpu.VMEM((hidden, width), bf16),
            pltpu.VMEM((n * count, hidden), bf16),
            pltpu.VMEM((n, n, count, half), bf16),
            pltpu.VMEM((n, n, count, half), bf16),
            pltpu.VMEM((2, n, 2, count, half // 2), bf16),
            pltpu.VMEM((2, n, 2, count, half), bf16),
            pltpu.VMEM((2, 3, count, half), bf16),
            pltpu.VMEM((2, 2, count, half // 2), bf16),
            pltpu.VMEM((2, 2, count, half), bf16),
            pltpu.VMEM((experts, main, width), bf16),
            pltpu.VMEM((experts, 1, width), jnp.float32),
            pltpu.SemaphoreType.DMA((2, n + 1, 4)),
            pltpu.SemaphoreType.DMA((2, n + 1, 4)),
            pltpu.SemaphoreType.DMA((1,)),
            pltpu.SemaphoreType.DMA((3, experts)),
            pltpu.SemaphoreType.DMA((3, experts)),
        ],
        compiler_params=pltpu.CompilerParams(
            collective_id=2, has_side_effects=True, vmem_limit_bytes=60 << 20
        ),
        name="sum_experts",
    )(hid, w_down)


def front_kernel(
    chunks,
    fades,
    q_ref,
    k_ref,
    v_ref,
    gate_ref,
    gain_ref,
    cum_ref,
    cum_t_ref,
    stream_ref,
    norm_gain_ref,
    slots_ref,
    weight,
    residual_ref,
    main_ref,
    last_ref,
    out_ref,
    got,
    got_fade,
    held,
    incoming,
    decay,
    inner,
    scale,
    spread_tok,
    own_tok,
    tok,
    w,
    prod,
    other,
    ring_opp,
    ring_full,
    done,
    asend,
    arecv,
    wsend,
    wrecv,
    ssem,
    rsem,
    lsem,
):
    n = 4
    blocks, per, head_dim, _ = chunks.shape
    seqs, length, feats = q_ref.shape
    heads = fades.shape[0]
    cores, zs, count, width = prod.shape[1:]
    sub = length // (cores * zs)
    half_f = feats // 2
    half = width // 2
    block = width // n
    x = lax.axis_index("x")
    y = lax.axis_index("y")
    z = lax.axis_index("z")
    c = lax.axis_index("c")
    me = y * n + x

    def xs(by):
        return lax.rem(x + (by + n), n)

    def yy(by):
        return lax.rem(y + (by + n), n)

    def zz(by):
        return lax.rem(z + (by + n), n)

    def where(t):
        return {"y": t // n, "x": lax.rem(t, n)}

    load = pltpu.make_async_copy(weight, w.at[y], lsem.at[0])
    load.start()
    barrier = pltpu.get_barrier_semaphore()

    @pl.loop(1, blocks)
    def _(d):
        pl.semaphore_signal(
            barrier, inc=1, device_id=where(lax.rem(me + d, blocks)), device_id_type=MESH
        )

    for there in ({"z": zz(1)}, {"z": zz(-1)}, {"c": 1 - c}):
        pl.semaphore_signal(barrier, inc=1, device_id=there, device_id_type=MESH)
    pl.semaphore_wait(barrier, blocks + 2)

    def state_copy(kind, d, src, dst, t):
        return pltpu.make_async_remote_copy(
            src_ref=src,
            dst_ref=dst,
            send_sem=asend.at[kind, d],
            recv_sem=arecv.at[kind, d],
            device_id=where(t),
            device_id_type=MESH,
        )

    def fade_of(t):
        return fades.at[pl.ds(lax.rem(t * per, heads), per)]

    @pl.loop(1, blocks)
    def _(d):
        t = lax.rem(me + d, blocks)
        state_copy(0, d, chunks.at[t], got.at[me], t).start()
        state_copy(1, d, fade_of(t), got_fade.at[me], t).start()

    got[me] = chunks[me]
    got_fade[me] = fade_of(me)[...]

    row = lax.broadcasted_iota(jnp.int32, (length, length), 0)
    col = lax.broadcasted_iota(jnp.int32, (length, length), 1)
    for h in range(heads):
        gap = cum_ref[:, h : h + 1] - cum_t_ref[h : h + 1, :]
        decay[h] = jnp.exp(jnp.where(row >= col, gap, -1e30))

    @pl.loop(0, seqs)
    def _(s):
        g = gate_ref[s].astype(jnp.float32)
        scale[s] = gain_ref[...] / (1.0 + jnp.exp(-g))
        for h in range(heads):
            cols = pl.ds(h * head_dim, head_dim)
            scores = lax.dot_general(
                q_ref[s, :, cols],
                k_ref[s, :, cols],
                (((1,), (1,)), ((), ())),
                preferred_element_type=jnp.float32,
            )
            mix = (scores * decay[h]).astype(jnp.bfloat16)
            inner[s, :, cols] = jnp.dot(
                mix, v_ref[s, :, cols], preferred_element_type=jnp.float32
            )

    @pl.loop(1, blocks)
    def _(d):
        t = lax.rem(me + d, blocks)
        frm = lax.rem(me - d + blocks, blocks)
        state_copy(0, d, chunks.at[t], got.at[frm], t).wait()
        state_copy(1, d, fade_of(t), got_fade.at[frm], t).wait()

    def advance(b, state):
        held[b] = state.astype(jnp.bfloat16)
        d = lax.rem(b - me + blocks, blocks)

        @pl.when(d != 0)
        def _():
            state_copy(2, d, held.at[b], incoming.at[me], b).start()

        return got_fade[b][:, :1, :] * state + got[b].astype(jnp.float32)

    lax.fori_loop(0, blocks, advance, jnp.zeros(got.shape[1:], jnp.float32))
    incoming[me] = held[me]
    load.wait()
    rows_of = [pl.ds(k * half_f, half_f) for k in range(2)]

    def weight_copy(k, src, dst, by):
        return pltpu.make_async_remote_copy(
            src_ref=src,
            dst_ref=dst,
            send_sem=wsend.at[k],
            recv_sem=wrecv.at[k],
            device_id={"y": yy(by)},
            device_id_type=MESH,
        )

    sent = []
    for k, by in ((0, 1), (1, -1)):
        sent.append(weight_copy(k, weight, w.at[y], by))
        sent[-1].start()

    @pl.loop(1, blocks)
    def _(d):
        t = lax.rem(me + d, blocks)
        frm = lax.rem(me - d + blocks, blocks)
        state_copy(2, d, held.at[t], incoming.at[frm], t).wait()

    @pl.loop(0, seqs)
    def _(s):
        for h in range(heads):
            cols = pl.ds(h * head_dim, head_dim)
            pair = s * heads + h
            state = incoming[pair // per, lax.rem(pair, per)]
            carried = jnp.dot(q_ref[s, :, cols], state, preferred_element_type=jnp.float32)
            attended = inner[s, :, cols] + jnp.exp(cum_ref[:, h : h + 1]) * carried
            square = jnp.mean(attended * attended, axis=-1, keepdims=True)
            mixed = attended * lax.rsqrt(square + 1e-06) * scale[s, :, cols]
            parted = mixed.reshape(zs, cores, sub, head_dim)
            for k in range(cores):
                spread_tok[k, :, pl.ds(s, 1), :, cols] = parted[:, k : k + 1]

    own_tok[...] = spread_tok[...].reshape(own_tok.shape).astype(jnp.bfloat16)

    def copy(j, kind, src, dst, axis, to):
        return pltpu.make_async_remote_copy(
            src_ref=src,
            dst_ref=dst,
            send_sem=ssem.at[j, kind],
            recv_sem=rsem.at[j, kind],
            device_id={axis: to},
            device_id_type=MESH,
        )

    def send(*a):
        cp = copy(*a)
        cp.start()
        sent.append(cp)

    def arrived(j, kind, dst, axis):
        to = xs(1) if axis == "x" else zz(1) if axis == "z" else 1 - c
        copy(j, kind, dst, dst, axis, to).wait_recv()

    shift = (0, -1, 1, 2)
    send(0, 0, own_tok, tok.at[0], "x", xs(1))
    send(0, 1, own_tok, tok.at[1], "x", xs(-1))

    def dot_part(j, g):
        src = own_tok if j == 0 else tok.at[j - 1]
        cols = pl.ds(pl.multiple_of(g * block, 128), block)
        part = jnp.dot(src[...], w[g], preferred_element_type=jnp.float32)
        prod[j, :, :, :, cols] = part.reshape(cores, zs, count, block).astype(jnp.bfloat16)

    def near_groups(j):
        @pl.loop(0, n - 1)
        def _(i):
            dot_part(j, yy(i + i // 2))

    def exchange(j):
        send(j, 2, prod.at[j, 1 - c], other.at[j], "c", 1 - c)

    def core_add(j):
        arrived(j, 2, other.at[j], "c")
        mine = prod.at[j, c]

        @pl.loop(0, n)
        def _(b):
            cols = pl.ds(pl.multiple_of(b * block, 128), block)
            mine[:, :, cols] = (
                mine[:, :, cols].astype(jnp.float32) + other[j, :, :, cols].astype(jnp.float32)
            ).astype(jnp.bfloat16)

        for k in range(2):
            send(
                j,
                3 + k,
                mine.at[zz(2), :, pl.ds(k * half, half)],
                ring_opp.at[j, k],
                "z",
                zz(1 if k == 0 else -1),
            )

    def near(j):
        for k in range(2):
            arrived(j, 3 + k, ring_opp.at[j, k], "z")
            to = zz(1 if k == 0 else -1)
            mine = prod.at[j, c, to]
            cols = pl.ds(k * half, half)
            mine[:, cols] = (
                mine[:, cols].astype(jnp.float32) + ring_opp[j, k].astype(jnp.float32)
            ).astype(jnp.bfloat16)
            send(j, 5 + k, mine, ring_full.at[j, k], "z", to)

    def finish(j):
        for k in range(2):
            arrived(j, 5 + k, ring_full.at[j, k], "z")
        s = (
            prod[j, c, z].astype(jnp.float32)
            + ring_full[j, 0].astype(jnp.float32)
            + ring_full[j, 1].astype(jnp.float32)
        ).astype(jnp.bfloat16)
        if j == 0:
            out_ref[x] = s
        else:
            done[j] = s
            send(j, 7, done.at[j], out_ref.at[x], "x", xs(shift[j]))

    for k, by in ((0, 1), (1, -1)):
        weight_copy(k, weight, w.at[yy(-by)], by).wait_recv()
        part_w = w.at[yy(-by), rows_of[k]]
        sent.append(weight_copy(2 + k, part_w, part_w, by))
        sent[-1].start()
    near_groups(0)
    for k in range(2):
        arrived(0, k, tok.at[k], "x")
        cols = pl.ds(k * half_f, half_f)
        send(1, k, tok.at[k, :, cols], tok.at[2, :, cols], "x", xs(1 if k == 0 else -1))
    near_groups(1)
    for k, by in ((0, 1), (1, -1)):
        far_w = w.at[yy(2), rows_of[k]]
        weight_copy(2 + k, far_w, far_w, by).wait_recv()
    for j in range(2):
        dot_part(j, yy(2))
        exchange(j)
    near_groups(2)
    dot_part(2, yy(2))
    exchange(2)
    core_add(0)
    core_add(1)
    near(0)
    for k in range(2):
        arrived(1, k, tok.at[2, :, pl.ds(k * half_f, half_f)], "x")
    near_groups(3)
    dot_part(3, yy(2))
    exchange(3)
    core_add(2)
    near(1)
    core_add(3)
    finish(0)
    near(2)
    finish(1)
    near(3)
    finish(2)
    finish(3)
    for j in (1, 2, 3):
        arrived(j, 7, out_ref.at[xs(-shift[j])], "x")

    tokens, model = residual_ref.shape
    experts, main, _ = main_ref.shape
    total = jnp.zeros((tokens, 1), jnp.float32)
    for i in range(n):
        for k in range(n):
            cols = pl.ds((i * n + k) * block, block)
            r = stream_ref[:, :, cols].astype(jnp.float32).reshape(tokens, block)
            r = r + out_ref[k, :, pl.ds(i * block, block)].astype(jnp.float32)
            residual_ref[:, cols] = r
            total = total + jnp.sum(r * r, axis=-1, keepdims=True)
    inverse = lax.rsqrt(total / model + 1e-06)

    @pl.loop(0, n * n)
    def _(i):
        cols = pl.ds(pl.multiple_of(i * block, 128), block)
        normed = (residual_ref[:, cols] * inverse * norm_gain_ref[:, cols]).astype(jnp.bfloat16)
        placed = jnp.dot(slots_ref[...], normed, preferred_element_type=jnp.float32)
        main_ref[:, :, cols] = (
            placed[: experts * main].reshape(experts, main, block).astype(jnp.bfloat16)
        )
        last_ref[:, :, cols] = placed[experts * main :].reshape(experts, 1, block)

    for cp in sent:
        cp.wait_send()


def front(
    local_state,
    cumulative,
    queries,
    keys,
    values,
    out_gate,
    head_gain,
    out_weight,
    stream,
    norm_gain,
    slots,
    experts,
):
    n = 4
    seqs, heads, width, _ = local_state.shape
    blocks = n * n
    per = seqs * heads // blocks
    length, feats = queries.shape[1:]
    cores, zs = lax.axis_size("c"), lax.axis_size("z")
    count = seqs * length // (cores * zs)
    rows = seqs * length
    columns = out_weight.shape[1] * n
    model = stream.shape[2]
    bf16, f32 = jnp.bfloat16, jnp.float32
    chunks = local_state.reshape(blocks, per, width, width).astype(bf16)
    fades = jnp.broadcast_to(jnp.exp(cumulative[-1])[:, None, None], (heads, 8, width))
    vmem = pl.BlockSpec(memory_space=pltpu.VMEM)
    return pl.pallas_call(
        front_kernel,
        out_shape=[
            jax.ShapeDtypeStruct((count, model), f32),
            jax.ShapeDtypeStruct((experts, slots.shape[0] // experts - 1, model), bf16),
            jax.ShapeDtypeStruct((experts, 1, model), f32),
        ],
        in_specs=[vmem] * 12 + [pl.BlockSpec(memory_space=pl.ANY)],
        out_specs=[vmem] * 3,
        scratch_shapes=[
            pltpu.VMEM((n, count, columns), bf16),
            pltpu.VMEM(chunks.shape, bf16),
            pltpu.VMEM((blocks, per, 8, width), f32),
            pltpu.VMEM(chunks.shape, bf16),
            pltpu.VMEM(chunks.shape, bf16),
            pltpu.VMEM((heads, length, length), f32),
            pltpu.VMEM(queries.shape, f32),
            pltpu.VMEM(queries.shape, f32),
            pltpu.VMEM((cores, zs, seqs, length // (cores * zs), feats), f32),
            pltpu.VMEM((rows, feats), bf16),
            pltpu.VMEM((3, rows, feats), bf16),
            pltpu.VMEM((n, feats, columns // n), bf16),
            pltpu.VMEM((n, cores, zs, count, columns), bf16),
            pltpu.VMEM((n, zs, count, columns), bf16),
            pltpu.VMEM((n, 2, count, columns // 2), bf16),
            pltpu.VMEM((n, 2, count, columns), bf16),
            pltpu.VMEM((n, count, columns), bf16),
            pltpu.SemaphoreType.DMA((3, blocks)),
            pltpu.SemaphoreType.DMA((3, blocks)),
            pltpu.SemaphoreType.DMA((4,)),
            pltpu.SemaphoreType.DMA((4,)),
            pltpu.SemaphoreType.DMA((n, 8)),
            pltpu.SemaphoreType.DMA((n, 8)),
            pltpu.SemaphoreType.DMA((1,)),
        ],
        compiler_params=pltpu.CompilerParams(
            collective_id=3, has_side_effects=True, vmem_limit_bytes=56 << 20
        ),
        name="front",
    )(
        chunks,
        fades,
        queries,
        keys,
        values,
        out_gate,
        head_gain.reshape(1, feats),
        cumulative,
        cumulative.T,
        stream,
        norm_gain.reshape(1, model),
        slots,
        out_weight,
    )


def body(
    queries,
    keys,
    values,
    decay_log,
    out_gate,
    head_gain,
    out_weight,
    stream,
    norm_gain,
    expert_ids,
    expert_share,
    w_gate,
    w_up,
    w_down,
):
    seq_count, block_len, head_width = queries.shape
    head_count = decay_log.shape[1]
    head_dim = head_width // head_count
    split_shape = (seq_count, block_len, head_count, head_dim)
    key_heads = keys.reshape(split_shape)
    value_heads = values.reshape(split_shape)
    position = jnp.arange(block_len)
    causal = position[:, None] >= position[None, :]
    cumulative = jnp.sum(jnp.where(causal[:, :, None], decay_log[None], 0.0), axis=1)
    block_end = cumulative[-1]
    keys_faded = jnp.exp(block_end[None, :] - cumulative)[None, :, :, None] * key_heads.astype(
        jnp.float32
    )
    local_state = jnp.einsum(
        "sjhd,sjhe->shde",
        keys_faded.astype(jnp.bfloat16),
        value_heads,
        preferred_element_type=jnp.float32,
    )
    sub_len = stream.shape[1]
    model_width = stream.shape[2]
    exp_count = lax.axis_size(EXP)
    tok_count = seq_count * sub_len
    expert_count = exp_count
    capacity = max(2, (2 * tok_count + expert_count - 1) // expert_count + 1)
    slot_total = expert_count * capacity
    picks = expert_ids.reshape(2 * tok_count)
    copy_no = jnp.arange(2 * tok_count)
    earlier = (copy_no[None, :] < copy_no[:, None]) & (picks[None, :] == picks[:, None])
    ranking = jnp.sum(earlier.astype(jnp.int32), axis=1)
    main = capacity - 1
    slot_of = jnp.where(ranking < main, picks * main + ranking, expert_count * main + picks)
    placing = slot_of[:, None] == jnp.arange(slot_total, dtype=jnp.int32)[None, :]
    token_placing = jnp.any(placing.reshape(tok_count, 2, slot_total), axis=1)
    main_total = expert_count * main
    residual_sum, main_rows, last_rows = front(
        local_state,
        cumulative,
        queries,
        keys,
        values,
        out_gate,
        head_gain,
        out_weight,
        stream,
        norm_gain,
        token_placing.T.astype(jnp.bfloat16),
        expert_count,
    )
    hid = expert_terms(main_rows, last_rows, w_gate[0].T, w_up[0].T)
    back_main, back_last = expert_sum(hid, w_down[0], expert_count)
    returned = jnp.concatenate(
        [
            back_main.reshape(main_total, model_width).astype(jnp.float32),
            back_last.reshape(expert_count, model_width),
        ],
        axis=0,
    )
    weighting = jnp.where(placing, expert_share.reshape(2 * tok_count, 1), 0.0)
    weighting = jnp.sum(weighting.reshape(tok_count, 2, slot_total), axis=1)
    expert_mix = jnp.dot(weighting, returned, precision=lax.Precision.HIGHEST)
    result = (residual_sum + expert_mix).astype(jnp.bfloat16)
    return result.reshape(seq_count, sub_len, model_width)


def solution(mesh):
    n_exp = mesh.shape["exp"]
    side = round(mesh.shape["ctx"] ** 0.5)
    fine = Mesh(mesh.devices.reshape(side, side, n_exp // 2, 2), ("y", "x", "z", "c"))
    return jax.shard_map(
        body,
        mesh=fine,
        in_specs=(
            P(None, CTX, EXP),
            P(None, CTX, EXP),
            P(None, CTX, EXP),
            P(CTX, EXP),
            P(None, CTX, EXP),
            P(EXP),
            P(EXP, CTX),
            P(None, CTX + EXP, None),
            P(),
            P(CTX + EXP, None, None),
            P(CTX + EXP, None, None),
            P(EXP, None, CTX),
            P(EXP, None, CTX),
            P(EXP, CTX, None),
        ),
        out_specs=P(None, CTX + EXP, None),
        check_vma=False,
    )
```

```python
import jax
import jax.numpy as jnp
from jax import lax
from jax.experimental import pallas as pl
from jax.experimental.pallas import tpu as pltpu
from jax.sharding import Mesh, PartitionSpec as P

CTX = ("y", "x")
EXP = ("z", "c")


MESH = pl.DeviceIdType.MESH
AXES = (("x", "y"), ("y", "x"))


def greet(others):
    barrier = pltpu.get_barrier_semaphore()
    for where in others:
        pl.semaphore_signal(barrier, inc=1, device_id=where, device_id_type=MESH)
    pl.semaphore_wait(barrier, len(others))


def signal_others(others):
    barrier = pltpu.get_barrier_semaphore()
    for where in others:
        pl.semaphore_signal(barrier, inc=1, device_id=where, device_id_type=MESH)
    return barrier


def expert_place(t):
    return {"z": t // 2, "c": lax.rem(t, 2)}


def gather_kernel(
    main_ref,
    last_ref,
    wg_hbm,
    wu_hbm,
    hid_ref,
    buf_a,
    buf_b,
    rows_ref,
    wg,
    wu,
    xin,
    acc_g,
    acc_u,
    last_in,
    last_out,
    ssem,
    rsem,
    lsem,
    esend,
    erecv,
):
    n = 4
    experts, main, _ = main_ref.shape
    mine_e = lax.axis_index("z") * 2 + lax.axis_index("c")
    count, width = rows_ref.shape
    half = width // 2
    quarter = half // 2
    hidden = wg.shape[0]
    buf = (buf_a, buf_b)
    place = {a: lax.axis_index(a) for a in ("x", "y")}

    def step(axis, by):
        return lax.rem(place[axis] + (by + n), n)

    load_g = pltpu.make_async_copy(wg_hbm, wg, lsem.at[0])
    load_u = pltpu.make_async_copy(wu_hbm, wu, lsem.at[1])
    load_g.start()
    load_u.start()
    greet(
        [{a: step(a, d)} for a in ("x", "y") for d in (1, -1)]
        + [expert_place(lax.rem(mine_e + d, experts)) for d in range(1, experts)]
    )

    def main_rows(e):
        return rows_ref.at[pl.ds(pl.multiple_of(e * main, 8), main)]

    def deal(d, to, frm):
        return [
            pltpu.make_async_remote_copy(
                src_ref=src,
                dst_ref=dst,
                send_sem=esend.at[k, d],
                recv_sem=erecv.at[k, d],
                device_id=expert_place(to),
                device_id_type=MESH,
            )
            for k, (src, dst) in enumerate(
                (
                    (main_ref.at[to, :, pl.ds(0, half)], main_rows(frm).at[:, pl.ds(0, half)]),
                    (last_ref.at[to], last_in.at[frm]),
                    (main_ref.at[to, :, pl.ds(half, half)], main_rows(frm).at[:, pl.ds(half, half)]),
                )
            )
        ]

    for k in (1, 0, 2):

        @pl.loop(1, experts)
        def _(d):
            deal(d, lax.rem(mine_e + d, experts), mine_e)[k].start()

    own_main = pltpu.make_async_copy(main_ref.at[mine_e], main_rows(mine_e), lsem.at[6])
    own_last = pltpu.make_async_copy(last_ref.at[mine_e], last_in.at[mine_e], lsem.at[7])
    own_main.start()
    own_last.start()
    acc_g[...] = jnp.zeros_like(acc_g)
    acc_u[...] = jnp.zeros_like(acc_u)
    own_main.wait()
    own_last.wait()

    def dealt(k):
        @pl.loop(1, experts)
        def _(d):
            to, frm = lax.rem(mine_e + d, experts), lax.rem(mine_e - d + experts, experts)
            deal(d, to, frm)[k].wait()

    dealt(1)
    last_out[...] = last_in[...].reshape(last_out.shape).astype(jnp.bfloat16)
    put_last = pltpu.make_async_copy(
        last_out, rows_ref.at[pl.ds(experts * main, experts)], lsem.at[6]
    )
    put_last.start()
    put_last.wait()
    dealt(0)

    def row(h, fi, si):
        return buf[h].at[fi, pl.ds(pl.multiple_of(si * count, 8), count)]

    def cut(ref, k):
        return ref.at[:, pl.ds((k - 2) * quarter, quarter)] if k >= 2 else ref

    def send(h, stage, kind, axis, src, dst):
        to = step(axis, 1 if kind % 2 == 0 else -1)
        c = pltpu.make_async_remote_copy(
            src_ref=cut(src, kind),
            dst_ref=cut(dst, kind),
            send_sem=ssem.at[h, stage, kind],
            recv_sem=rsem.at[h, stage, kind],
            device_id={axis: to},
            device_id_type=MESH,
        )
        c.start()
        sent.append(c)

    def arrived(h, stage, kind, axis, dst):
        pltpu.make_async_remote_copy(
            src_ref=cut(dst, kind),
            dst_ref=cut(dst, kind),
            send_sem=ssem.at[h, stage, kind],
            recv_sem=rsem.at[h, stage, kind],
            device_id={axis: step(axis, 1)},
            device_id_type=MESH,
        ).wait_recv()

    sent = []
    shift = (0, -1, 1, 2)
    own = [rows_ref.at[:, pl.ds(h * half, half)] for h in range(2)]
    keep = []
    for h in range(2):
        first, second = AXES[h]
        mine = row(h, place[first], place[second])
        if h == 1:
            dealt(2)
        for kind in range(2):
            send(h, n, kind, first, own[h], mine)
        for kind in range(2):
            send(h, 0, kind, second, own[h], mine)
        keep.append(pltpu.make_async_copy(own[h], mine, lsem.at[2 + h]))
        keep[h].start()

    def spread(h, j):
        first, second = AXES[h]
        here = row(h, step(first, shift[j]), place[second])
        for kind in range(2):
            send(h, j, kind, second, here, here)

    def pass_on(h, stage, kind):
        first, second = AXES[h]
        by = -1 if kind == 0 else 1
        if stage == n:
            here = row(h, step(first, by), place[second])
            axis = first
        else:
            here = row(h, step(first, shift[stage]), step(second, by))
            axis = second
        arrived(h, stage, kind, axis, here)
        send(h, stage, kind + 2, axis, here, here)

    def far(h, stage):
        first, second = AXES[h]
        if stage == n:
            here, axis = row(h, step(first, 2), place[second]), first
        else:
            here, axis = row(h, step(first, shift[stage]), step(second, 2)), second
        for kind in (2, 3):
            arrived(h, stage, kind, axis, here)

    def load(h, j):
        return pltpu.make_async_copy(
            buf[h].at[step(AXES[h][0], shift[j])], xin.at[h], lsem.at[4 + h]
        )

    def multiply(h, j):
        load(h, j).wait()
        fi = step(AXES[h][0], shift[j])
        for w, acc in ((wg, acc_g), (wu, acc_u)):
            got = lax.dot_general(
                xin[h],
                w[:, pl.ds(h * half, half)],
                (((1,), (1,)), ((), ())),
                preferred_element_type=jnp.float32,
            ).reshape(n, count, hidden)
            if h == 0:
                acc[fi] += got
            else:
                acc[:, fi] += got

    def activate(p, q):
        g = acc_g[p, q]
        out = (g / (1.0 + jnp.exp(-g)) * acc_u[p, q]).astype(jnp.bfloat16)
        hid_ref[p, q] = out.astype(jnp.float32)

    for kind in range(2):
        for h in range(2):
            pass_on(h, n, kind)
            spread(h, 1 + kind)
    for kind in range(2):
        for h in range(2):
            pass_on(h, 0, kind)
    for h in range(2):
        far(h, n)
        spread(h, 3)
    load_g.wait()
    load_u.wait()
    for j in range(n):
        if j + 1 < n:
            for kind in range(2):
                for h in range(2):
                    pass_on(h, j + 1, kind)
        for h in range(2):
            if j == 0:
                keep[h].wait()
            far(h, j)
            load(h, j).start()
            if j == n - 1:
                multiply(h, j)
        if j < n - 1:
            for h in range(2):
                multiply(h, j)
        if j == 2:

            @pl.loop(0, 9)
            def _(k):
                a, b = k // 3, lax.rem(k, 3)
                activate(step("x", a + a // 2), step("y", b + b // 2))

    @pl.loop(0, n)
    def _(k):
        activate(step("x", 2), step("y", k))

    @pl.loop(0, n - 1)
    def _(k):
        activate(step("x", k + k // 2), step("y", 2))

    for c in sent:
        c.wait_send()


def reduce_kernel(
    hid_ref,
    wd_hbm,
    back_main,
    back_last,
    wd,
    rows,
    t_a,
    t_b,
    r_opp,
    r_full,
    part,
    r_opp2,
    r_full2,
    out_main,
    out_last,
    ssem,
    rsem,
    lsem,
    esend,
    erecv,
):
    n = 4
    experts, main, width = out_main.shape
    count = experts * (main + 1)
    mine_e = lax.axis_index("z") * 2 + lax.axis_index("c")
    half = width // 2
    quarter = half // 2
    block = min(512, quarter)
    t = (t_a, t_b)
    place = {a: lax.axis_index(a) for a in ("x", "y")}

    def step(axis, by):
        return lax.rem(place[axis] + (by + n), n)

    load = pltpu.make_async_copy(wd_hbm, wd, lsem.at[0])
    load.start()
    others = [{a: step(a, d)} for a in ("x", "y") for d in (1, -1)]
    others += [expert_place(lax.rem(mine_e + d, experts)) for d in range(1, experts)]
    barrier = signal_others(others)
    load.wait()
    shift = (2, 1, -1, 0)
    sent = []

    def copy(h, stage, kind, axis, src, dst):
        return pltpu.make_async_remote_copy(
            src_ref=src,
            dst_ref=dst,
            send_sem=ssem.at[h, stage, kind],
            recv_sem=rsem.at[h, stage, kind],
            device_id={axis: step(axis, 1 if kind % 2 == 0 else -1)},
            device_id_type=MESH,
        )

    def send(*a):
        c = copy(*a)
        c.start()
        sent.append(c)

    def arrived(h, stage, kind, axis, dst):
        copy(h, stage, kind, axis, dst, dst).wait_recv()

    def multiply(h, j, k):
        lead = step(AXES[h][0], shift[j])
        taken = hid_ref[lead] if h == 0 else hid_ref[:, pl.ds(lead, 1)]
        rows[...] = taken.reshape(rows.shape).astype(jnp.bfloat16)

        @pl.loop(0, quarter // block)
        def _(b):
            at = pl.multiple_of(k * quarter + b * block, 128)
            got = jnp.dot(
                rows[...],
                wd[:, pl.ds(pl.multiple_of(h * half + at, 128), block)],
                preferred_element_type=jnp.float32,
            )
            t[h][j, :, :, pl.ds(at, block)] = got.reshape(n, count, block).astype(jnp.bfloat16)

    def far_out(h, j, k):
        ring = AXES[h][1]
        src = t[h].at[j, step(ring, 2), :, pl.ds(k * quarter, quarter)]
        send(h, j, k, ring, src, r_opp.at[h, j, k])

    def add_to(ref, k, other):
        @pl.loop(0, quarter // block)
        def _(b):
            at = pl.multiple_of(b * block, 128)
            cols = pl.ds(pl.multiple_of(k * quarter + at, 128), block)
            ref[:, cols] = (
                ref[:, cols].astype(jnp.float32) + other[:, pl.ds(at, block)].astype(jnp.float32)
            ).astype(jnp.bfloat16)

    def add_up(refs, at):
        s = refs[0][:, pl.ds(at, block)].astype(jnp.float32)
        for r in refs[1:]:
            s = s + r[:, pl.ds(at, block)].astype(jnp.float32)
        return s

    def total(dst, refs):
        @pl.loop(0, half // block)
        def _(b):
            at = pl.multiple_of(b * block, 128)
            dst[:, pl.ds(at, block)] = add_up(refs, at).astype(jnp.bfloat16)

    def settle(h, refs):
        @pl.loop(0, half // block)
        def _(b):
            at = pl.multiple_of(b * block, 128)
            cols = pl.ds(pl.multiple_of(h * half + at, 128), block)
            s = add_up(refs, at)
            out_main[:, :, cols] = (
                s[: experts * main].reshape(experts, main, block).astype(jnp.bfloat16)
            )
            out_last[:, :, cols] = s[experts * main :].reshape(experts, 1, block)

    def give(k, d, to, frm):
        if k == 2:
            src, dst = out_last.at[to], back_last.at[frm]
        else:
            cols = pl.ds(k * half, half)
            src, dst = out_main.at[to, :, cols], back_main.at[frm, :, cols]
        return pltpu.make_async_remote_copy(
            src_ref=src,
            dst_ref=dst,
            send_sem=esend.at[k, d],
            recv_sem=erecv.at[k, d],
            device_id=expert_place(to),
            device_id_type=MESH,
        )

    def near(h, j):
        ring = AXES[h][1]
        for k in range(2):
            arrived(h, j, k, ring, r_opp.at[h, j, k])
            mine = t[h].at[j, step(ring, 1 if k == 0 else -1)]
            add_to(mine, k, r_opp.at[h, j, k])
            send(h, j, 2 + k, ring, mine, r_full.at[h, j, k])

    def both(h, j):
        for k in range(2):
            arrived(h, j, 2 + k, AXES[h][1], r_full.at[h, j, k])

    def finish(h, j):
        both(h, j)
        total(
            part.at[h, j],
            [t[h].at[j, place[AXES[h][1]]], r_full.at[h, j, 0], r_full.at[h, j, 1]],
        )

    for j in range(2):
        for k in range(2):
            for h in range(2):
                multiply(h, j, k)
                if j == 0 and h == 0 and k == 0:
                    pl.semaphore_wait(barrier, len(others))
                far_out(h, j, k)
    for j in range(n):
        for h in range(2):
            near(h, j)
        if j + 2 < n:
            for k in range(2):
                for h in range(2):
                    multiply(h, j + 2, k)
                    far_out(h, j + 2, k)
        if j == 1:
            for h in range(2):
                finish(h, 0)
                for k in range(2):
                    send(
                        h,
                        n,
                        k,
                        AXES[h][0],
                        part.at[h, 0, :, pl.ds(k * quarter, quarter)],
                        r_opp2.at[h, k],
                    )
    for j in (1, 2):
        for h in range(2):
            finish(h, j)
            k = j - 1
            arrived(h, n, k, AXES[h][0], r_opp2.at[h, k])
            add_to(part.at[h, j], k, r_opp2.at[h, k])
            send(h, n, 2 + k, AXES[h][0], part.at[h, j], r_full2.at[h, k])
    for h in range(2):
        both(h, 3)
        for k in range(2):
            arrived(h, n, 2 + k, AXES[h][0], r_full2.at[h, k])
        settle(
            h,
            [
                t[h].at[3, place[AXES[h][1]]],
                r_full.at[h, 3, 0],
                r_full.at[h, 3, 1],
                r_full2.at[h, 0],
                r_full2.at[h, 1],
            ],
        )

        @pl.loop(1, experts)
        def _(d):
            for k in (h,) if h == 0 else (1, 2):
                give(k, d, lax.rem(mine_e + d, experts), mine_e).start()

    back_main[mine_e] = out_main[mine_e]
    back_last[mine_e] = out_last[mine_e]

    @pl.loop(1, experts)
    def _(d):
        for k in range(3):
            give(
                k, d, lax.rem(mine_e + d, experts), lax.rem(mine_e - d + experts, experts)
            ).wait()

    for c in sent:
        c.wait_send()


def expert_terms(main_rows, last_rows, w_gate, w_up):
    n = 4
    experts, main, width = main_rows.shape
    count = experts * (main + 1)
    hidden = w_gate.shape[0]
    half = width // 2
    any_spec = pl.BlockSpec(memory_space=pl.ANY)
    vmem = pl.BlockSpec(memory_space=pltpu.VMEM)
    bf16 = jnp.bfloat16
    return pl.pallas_call(
        gather_kernel,
        out_shape=[
            jax.ShapeDtypeStruct((n, n, count, hidden), jnp.float32),
            jax.ShapeDtypeStruct((n, n * count, half), bf16),
            jax.ShapeDtypeStruct((n, n * count, half), bf16),
            jax.ShapeDtypeStruct((count, width), bf16),
        ],
        in_specs=[any_spec] * 4,
        out_specs=[vmem, any_spec, any_spec, any_spec],
        scratch_shapes=[
            pltpu.VMEM((hidden, width), bf16),
            pltpu.VMEM((hidden, width), bf16),
            pltpu.VMEM((2, n * count, half), bf16),
            pltpu.VMEM((n, n, count, hidden), jnp.float32),
            pltpu.VMEM((n, n, count, hidden), jnp.float32),
            pltpu.VMEM((experts, 1, width), jnp.float32),
            pltpu.VMEM((experts, width), bf16),
            pltpu.SemaphoreType.DMA((2, n + 1, 4)),
            pltpu.SemaphoreType.DMA((2, n + 1, 4)),
            pltpu.SemaphoreType.DMA((8,)),
            pltpu.SemaphoreType.DMA((3, experts)),
            pltpu.SemaphoreType.DMA((3, experts)),
        ],
        compiler_params=pltpu.CompilerParams(
            collective_id=1, has_side_effects=True, vmem_limit_bytes=60 << 20
        ),
        name="gather_experts",
    )(main_rows, last_rows, w_gate, w_up)[0]


def expert_sum(hid, w_down, experts):
    n = 4
    hidden, width = w_down.shape
    count = hid.shape[2]
    main = count // experts - 1
    half = width // 2
    any_spec = pl.BlockSpec(memory_space=pl.ANY)
    vmem = pl.BlockSpec(memory_space=pltpu.VMEM)
    bf16 = jnp.bfloat16
    return pl.pallas_call(
        reduce_kernel,
        out_shape=[
            jax.ShapeDtypeStruct((experts, main, width), bf16),
            jax.ShapeDtypeStruct((experts, 1, width), jnp.float32),
        ],
        in_specs=[vmem, any_spec],
        out_specs=[vmem, vmem],
        scratch_shapes=[
            pltpu.VMEM((hidden, width), bf16),
            pltpu.VMEM((n * count, hidden), bf16),
            pltpu.VMEM((n, n, count, half), bf16),
            pltpu.VMEM((n, n, count, half), bf16),
            pltpu.VMEM((2, n, 2, count, half // 2), bf16),
            pltpu.VMEM((2, n, 2, count, half), bf16),
            pltpu.VMEM((2, 3, count, half), bf16),
            pltpu.VMEM((2, 2, count, half // 2), bf16),
            pltpu.VMEM((2, 2, count, half), bf16),
            pltpu.VMEM((experts, main, width), bf16),
            pltpu.VMEM((experts, 1, width), jnp.float32),
            pltpu.SemaphoreType.DMA((2, n + 1, 4)),
            pltpu.SemaphoreType.DMA((2, n + 1, 4)),
            pltpu.SemaphoreType.DMA((1,)),
            pltpu.SemaphoreType.DMA((3, experts)),
            pltpu.SemaphoreType.DMA((3, experts)),
        ],
        compiler_params=pltpu.CompilerParams(
            collective_id=2, has_side_effects=True, vmem_limit_bytes=60 << 20
        ),
        name="sum_experts",
    )(hid, w_down)


def front_kernel(
    chunks,
    fades,
    q_ref,
    k_ref,
    v_ref,
    gate_ref,
    gain_ref,
    cum_ref,
    cum_t_ref,
    stream_ref,
    norm_gain_ref,
    slots_ref,
    weight,
    residual_ref,
    main_ref,
    last_ref,
    out_ref,
    got,
    got_fade,
    held,
    incoming,
    decay,
    inner,
    scale,
    spread_tok,
    own_tok,
    tok,
    w,
    prod,
    other,
    ring_opp,
    ring_full,
    done,
    asend,
    arecv,
    wsend,
    wrecv,
    ssem,
    rsem,
    lsem,
):
    n = 4
    blocks, per, head_dim, _ = chunks.shape
    seqs, length, feats = q_ref.shape
    heads = fades.shape[0]
    cores, zs, count, width = prod.shape[1:]
    sub = length // (cores * zs)
    half_f = feats // 2
    half = width // 2
    block = width // n
    x = lax.axis_index("x")
    y = lax.axis_index("y")
    z = lax.axis_index("z")
    c = lax.axis_index("c")
    me = y * n + x

    def xs(by):
        return lax.rem(x + (by + n), n)

    def yy(by):
        return lax.rem(y + (by + n), n)

    def zz(by):
        return lax.rem(z + (by + n), n)

    def where(t):
        return {"y": t // n, "x": lax.rem(t, n)}

    load = pltpu.make_async_copy(weight, w.at[y], lsem.at[0])
    load.start()
    barrier = pltpu.get_barrier_semaphore()

    @pl.loop(1, blocks)
    def _(d):
        pl.semaphore_signal(
            barrier, inc=1, device_id=where(lax.rem(me + d, blocks)), device_id_type=MESH
        )

    for there in ({"z": zz(1)}, {"z": zz(-1)}, {"c": 1 - c}):
        pl.semaphore_signal(barrier, inc=1, device_id=there, device_id_type=MESH)
    pl.semaphore_wait(barrier, blocks + 2)

    def state_copy(kind, d, src, dst, t):
        return pltpu.make_async_remote_copy(
            src_ref=src,
            dst_ref=dst,
            send_sem=asend.at[kind, d],
            recv_sem=arecv.at[kind, d],
            device_id=where(t),
            device_id_type=MESH,
        )

    def fade_of(t):
        return fades.at[pl.ds(lax.rem(t * per, heads), per)]

    @pl.loop(1, blocks)
    def _(d):
        t = lax.rem(me + d, blocks)
        state_copy(0, d, chunks.at[t], got.at[me], t).start()
        state_copy(1, d, fade_of(t), got_fade.at[me], t).start()

    got[me] = chunks[me]
    got_fade[me] = fade_of(me)[...]

    row = lax.broadcasted_iota(jnp.int32, (length, length), 0)
    col = lax.broadcasted_iota(jnp.int32, (length, length), 1)
    for h in range(heads):
        gap = cum_ref[:, h : h + 1] - cum_t_ref[h : h + 1, :]
        decay[h] = jnp.exp(jnp.where(row >= col, gap, -1e30))

    @pl.loop(0, seqs)
    def _(s):
        g = gate_ref[s].astype(jnp.float32)
        scale[s] = gain_ref[...] / (1.0 + jnp.exp(-g))
        for h in range(heads):
            cols = pl.ds(h * head_dim, head_dim)
            scores = lax.dot_general(
                q_ref[s, :, cols],
                k_ref[s, :, cols],
                (((1,), (1,)), ((), ())),
                preferred_element_type=jnp.float32,
            )
            mix = (scores * decay[h]).astype(jnp.bfloat16)
            inner[s, :, cols] = jnp.dot(
                mix, v_ref[s, :, cols], preferred_element_type=jnp.float32
            )

    @pl.loop(1, blocks)
    def _(d):
        t = lax.rem(me + d, blocks)
        frm = lax.rem(me - d + blocks, blocks)
        state_copy(0, d, chunks.at[t], got.at[frm], t).wait()
        state_copy(1, d, fade_of(t), got_fade.at[frm], t).wait()

    def advance(b, state):
        held[b] = state.astype(jnp.bfloat16)
        d = lax.rem(b - me + blocks, blocks)

        @pl.when(d != 0)
        def _():
            state_copy(2, d, held.at[b], incoming.at[me], b).start()

        return got_fade[b][:, :1, :] * state + got[b].astype(jnp.float32)

    lax.fori_loop(0, blocks, advance, jnp.zeros(got.shape[1:], jnp.float32))
    incoming[me] = held[me]
    load.wait()
    rows_of = [pl.ds(k * half_f, half_f) for k in range(2)]

    def weight_copy(k, src, dst, by):
        return pltpu.make_async_remote_copy(
            src_ref=src,
            dst_ref=dst,
            send_sem=wsend.at[k],
            recv_sem=wrecv.at[k],
            device_id={"y": yy(by)},
            device_id_type=MESH,
        )

    sent = []
    for k, by in ((0, 1), (1, -1)):
        sent.append(weight_copy(k, weight, w.at[y], by))
        sent[-1].start()

    @pl.loop(1, blocks)
    def _(d):
        t = lax.rem(me + d, blocks)
        frm = lax.rem(me - d + blocks, blocks)
        state_copy(2, d, held.at[t], incoming.at[frm], t).wait()

    @pl.loop(0, seqs)
    def _(s):
        for h in range(heads):
            cols = pl.ds(h * head_dim, head_dim)
            pair = s * heads + h
            state = incoming[pair // per, lax.rem(pair, per)]
            carried = jnp.dot(q_ref[s, :, cols], state, preferred_element_type=jnp.float32)
            attended = inner[s, :, cols] + jnp.exp(cum_ref[:, h : h + 1]) * carried
            square = jnp.mean(attended * attended, axis=-1, keepdims=True)
            mixed = attended * lax.rsqrt(square + 1e-06) * scale[s, :, cols]
            parted = mixed.reshape(zs, cores, sub, head_dim)
            for k in range(cores):
                spread_tok[k, :, pl.ds(s, 1), :, cols] = parted[:, k : k + 1]

    own_tok[...] = spread_tok[...].reshape(own_tok.shape).astype(jnp.bfloat16)

    def copy(j, kind, src, dst, axis, to):
        return pltpu.make_async_remote_copy(
            src_ref=src,
            dst_ref=dst,
            send_sem=ssem.at[j, kind],
            recv_sem=rsem.at[j, kind],
            device_id={axis: to},
            device_id_type=MESH,
        )

    def send(*a):
        cp = copy(*a)
        cp.start()
        sent.append(cp)

    def arrived(j, kind, dst, axis):
        to = xs(1) if axis == "x" else zz(1) if axis == "z" else 1 - c
        copy(j, kind, dst, dst, axis, to).wait_recv()

    shift = (0, -1, 1, 2)
    send(0, 0, own_tok, tok.at[0], "x", xs(1))
    send(0, 1, own_tok, tok.at[1], "x", xs(-1))

    def dot_part(j, g):
        src = own_tok if j == 0 else tok.at[j - 1]
        cols = pl.ds(pl.multiple_of(g * block, 128), block)
        part = jnp.dot(src[...], w[g], preferred_element_type=jnp.float32)
        prod[j, :, :, :, cols] = part.reshape(cores, zs, count, block).astype(jnp.bfloat16)

    def near_groups(j):
        @pl.loop(0, n - 1)
        def _(i):
            dot_part(j, yy(i + i // 2))

    def exchange(j):
        send(j, 2, prod.at[j, 1 - c], other.at[j], "c", 1 - c)

    def core_add(j):
        arrived(j, 2, other.at[j], "c")
        mine = prod.at[j, c]

        @pl.loop(0, n)
        def _(b):
            cols = pl.ds(pl.multiple_of(b * block, 128), block)
            mine[:, :, cols] = (
                mine[:, :, cols].astype(jnp.float32) + other[j, :, :, cols].astype(jnp.float32)
            ).astype(jnp.bfloat16)

        for k in range(2):
            send(
                j,
                3 + k,
                mine.at[zz(2), :, pl.ds(k * half, half)],
                ring_opp.at[j, k],
                "z",
                zz(1 if k == 0 else -1),
            )

    def near(j):
        for k in range(2):
            arrived(j, 3 + k, ring_opp.at[j, k], "z")
            to = zz(1 if k == 0 else -1)
            mine = prod.at[j, c, to]
            cols = pl.ds(k * half, half)
            mine[:, cols] = (
                mine[:, cols].astype(jnp.float32) + ring_opp[j, k].astype(jnp.float32)
            ).astype(jnp.bfloat16)
            send(j, 5 + k, mine, ring_full.at[j, k], "z", to)

    def finish(j):
        for k in range(2):
            arrived(j, 5 + k, ring_full.at[j, k], "z")
        s = (
            prod[j, c, z].astype(jnp.float32)
            + ring_full[j, 0].astype(jnp.float32)
            + ring_full[j, 1].astype(jnp.float32)
        ).astype(jnp.bfloat16)
        if j == 0:
            out_ref[x] = s
        else:
            done[j] = s
            send(j, 7, done.at[j], out_ref.at[x], "x", xs(shift[j]))

    for k, by in ((0, 1), (1, -1)):
        weight_copy(k, weight, w.at[yy(-by)], by).wait_recv()
        part_w = w.at[yy(-by), rows_of[k]]
        sent.append(weight_copy(2 + k, part_w, part_w, by))
        sent[-1].start()
    near_groups(0)
    for k in range(2):
        arrived(0, k, tok.at[k], "x")
        cols = pl.ds(k * half_f, half_f)
        send(1, k, tok.at[k, :, cols], tok.at[2, :, cols], "x", xs(1 if k == 0 else -1))
    near_groups(1)
    for k, by in ((0, 1), (1, -1)):
        far_w = w.at[yy(2), rows_of[k]]
        weight_copy(2 + k, far_w, far_w, by).wait_recv()
    for j in range(2):
        dot_part(j, yy(2))
        exchange(j)
    near_groups(2)
    dot_part(2, yy(2))
    exchange(2)
    core_add(0)
    core_add(1)
    near(0)
    for k in range(2):
        arrived(1, k, tok.at[2, :, pl.ds(k * half_f, half_f)], "x")
    near_groups(3)
    dot_part(3, yy(2))
    exchange(3)
    core_add(2)
    near(1)
    core_add(3)
    finish(0)
    near(2)
    finish(1)
    near(3)
    finish(2)
    finish(3)
    for j in (1, 2, 3):
        arrived(j, 7, out_ref.at[xs(-shift[j])], "x")

    tokens, model = residual_ref.shape
    experts, main, _ = main_ref.shape
    total = jnp.zeros((tokens, 1), jnp.float32)
    for i in range(n):
        for k in range(n):
            cols = pl.ds((i * n + k) * block, block)
            r = stream_ref[:, :, cols].astype(jnp.float32).reshape(tokens, block)
            r = r + out_ref[k, :, pl.ds(i * block, block)].astype(jnp.float32)
            residual_ref[:, cols] = r
            total = total + jnp.sum(r * r, axis=-1, keepdims=True)
    inverse = lax.rsqrt(total / model + 1e-06)

    @pl.loop(0, n * n)
    def _(i):
        cols = pl.ds(pl.multiple_of(i * block, 128), block)
        normed = (residual_ref[:, cols] * inverse * norm_gain_ref[:, cols]).astype(jnp.bfloat16)
        placed = jnp.dot(slots_ref[...], normed, preferred_element_type=jnp.float32)
        main_ref[:, :, cols] = (
            placed[: experts * main].reshape(experts, main, block).astype(jnp.bfloat16)
        )
        last_ref[:, :, cols] = placed[experts * main :].reshape(experts, 1, block)

    for cp in sent:
        cp.wait_send()


def front(
    local_state,
    cumulative,
    queries,
    keys,
    values,
    out_gate,
    head_gain,
    out_weight,
    stream,
    norm_gain,
    slots,
    experts,
):
    n = 4
    seqs, heads, width, _ = local_state.shape
    blocks = n * n
    per = seqs * heads // blocks
    length, feats = queries.shape[1:]
    cores, zs = lax.axis_size("c"), lax.axis_size("z")
    count = seqs * length // (cores * zs)
    rows = seqs * length
    columns = out_weight.shape[1] * n
    model = stream.shape[2]
    bf16, f32 = jnp.bfloat16, jnp.float32
    chunks = local_state.reshape(blocks, per, width, width).astype(bf16)
    fades = jnp.broadcast_to(jnp.exp(cumulative[-1])[:, None, None], (heads, 8, width))
    vmem = pl.BlockSpec(memory_space=pltpu.VMEM)
    return pl.pallas_call(
        front_kernel,
        out_shape=[
            jax.ShapeDtypeStruct((count, model), f32),
            jax.ShapeDtypeStruct((experts, slots.shape[0] // experts - 1, model), bf16),
            jax.ShapeDtypeStruct((experts, 1, model), f32),
        ],
        in_specs=[vmem] * 12 + [pl.BlockSpec(memory_space=pl.ANY)],
        out_specs=[vmem] * 3,
        scratch_shapes=[
            pltpu.VMEM((n, count, columns), bf16),
            pltpu.VMEM(chunks.shape, bf16),
            pltpu.VMEM((blocks, per, 8, width), f32),
            pltpu.VMEM(chunks.shape, bf16),
            pltpu.VMEM(chunks.shape, bf16),
            pltpu.VMEM((heads, length, length), f32),
            pltpu.VMEM(queries.shape, f32),
            pltpu.VMEM(queries.shape, f32),
            pltpu.VMEM((cores, zs, seqs, length // (cores * zs), feats), f32),
            pltpu.VMEM((rows, feats), bf16),
            pltpu.VMEM((3, rows, feats), bf16),
            pltpu.VMEM((n, feats, columns // n), bf16),
            pltpu.VMEM((n, cores, zs, count, columns), bf16),
            pltpu.VMEM((n, zs, count, columns), bf16),
            pltpu.VMEM((n, 2, count, columns // 2), bf16),
            pltpu.VMEM((n, 2, count, columns), bf16),
            pltpu.VMEM((n, count, columns), bf16),
            pltpu.SemaphoreType.DMA((3, blocks)),
            pltpu.SemaphoreType.DMA((3, blocks)),
            pltpu.SemaphoreType.DMA((4,)),
            pltpu.SemaphoreType.DMA((4,)),
            pltpu.SemaphoreType.DMA((n, 8)),
            pltpu.SemaphoreType.DMA((n, 8)),
            pltpu.SemaphoreType.DMA((1,)),
        ],
        compiler_params=pltpu.CompilerParams(
            collective_id=3, has_side_effects=True, vmem_limit_bytes=56 << 20
        ),
        name="front",
    )(
        chunks,
        fades,
        queries,
        keys,
        values,
        out_gate,
        head_gain.reshape(1, feats),
        cumulative,
        cumulative.T,
        stream,
        norm_gain.reshape(1, model),
        slots,
        out_weight,
    )


def body(
    queries,
    keys,
    values,
    decay_log,
    out_gate,
    head_gain,
    out_weight,
    stream,
    norm_gain,
    expert_ids,
    expert_share,
    w_gate,
    w_up,
    w_down,
):
    seq_count, block_len, head_width = queries.shape
    head_count = decay_log.shape[1]
    head_dim = head_width // head_count
    split_shape = (seq_count, block_len, head_count, head_dim)
    key_heads = keys.reshape(split_shape)
    value_heads = values.reshape(split_shape)
    position = jnp.arange(block_len)
    causal = position[:, None] >= position[None, :]
    cumulative = jnp.sum(jnp.where(causal[:, :, None], decay_log[None], 0.0), axis=1)
    block_end = cumulative[-1]
    keys_faded = jnp.exp(block_end[None, :] - cumulative)[None, :, :, None] * key_heads.astype(
        jnp.float32
    )
    local_state = jnp.einsum(
        "sjhd,sjhe->shde",
        keys_faded.astype(jnp.bfloat16),
        value_heads,
        preferred_element_type=jnp.float32,
    )
    sub_len = stream.shape[1]
    model_width = stream.shape[2]
    exp_count = lax.axis_size(EXP)
    tok_count = seq_count * sub_len
    expert_count = exp_count
    capacity = max(2, (2 * tok_count + expert_count - 1) // expert_count + 1)
    slot_total = expert_count * capacity
    picks = expert_ids.reshape(2 * tok_count)
    copy_no = jnp.arange(2 * tok_count)
    earlier = (copy_no[None, :] < copy_no[:, None]) & (picks[None, :] == picks[:, None])
    ranking = jnp.sum(earlier.astype(jnp.int32), axis=1)
    main = capacity - 1
    slot_of = jnp.where(ranking < main, picks * main + ranking, expert_count * main + picks)
    placing = slot_of[:, None] == jnp.arange(slot_total, dtype=jnp.int32)[None, :]
    token_placing = jnp.any(placing.reshape(tok_count, 2, slot_total), axis=1)
    main_total = expert_count * main
    residual_sum, main_rows, last_rows = front(
        local_state,
        cumulative,
        queries,
        keys,
        values,
        out_gate,
        head_gain,
        out_weight,
        stream,
        norm_gain,
        token_placing.T.astype(jnp.bfloat16),
        expert_count,
    )
    hid = expert_terms(main_rows, last_rows, w_gate[0].T, w_up[0].T)
    back_main, back_last = expert_sum(hid, w_down[0], expert_count)
    returned = jnp.concatenate(
        [
            back_main.reshape(main_total, model_width).astype(jnp.float32),
            back_last.reshape(expert_count, model_width),
        ],
        axis=0,
    )
    weighting = jnp.where(placing, expert_share.reshape(2 * tok_count, 1), 0.0)
    weighting = jnp.sum(weighting.reshape(tok_count, 2, slot_total), axis=1)
    expert_mix = jnp.dot(weighting, returned, precision=lax.Precision.HIGHEST)
    result = (residual_sum + expert_mix).astype(jnp.bfloat16)
    return result.reshape(seq_count, sub_len, model_width)


def solution(mesh):
    n_exp = mesh.shape["exp"]
    side = round(mesh.shape["ctx"] ** 0.5)
    fine = Mesh(mesh.devices.reshape(side, side, n_exp // 2, 2), ("y", "x", "z", "c"))
    return jax.shard_map(
        body,
        mesh=fine,
        in_specs=(
            P(None, CTX, EXP),
            P(None, CTX, EXP),
            P(None, CTX, EXP),
            P(CTX, EXP),
            P(None, CTX, EXP),
            P(EXP),
            P(EXP, CTX),
            P(None, CTX + EXP, None),
            P(),
            P(CTX + EXP, None, None),
            P(CTX + EXP, None, None),
            P(EXP, None, CTX),
            P(EXP, None, CTX),
            P(EXP, CTX, None),
        ),
        out_specs=P(None, CTX + EXP, None),
        check_vma=False,
    )
```
